256 devices in a mesh: tile: 32 (over x, z_hi, y), mode: 8 (over z_lo, core).
Axes of the slice: x: 4, y: 4, z: 8 (z_hi: 2, z_lo: 4; z = z_hi * 4 + z_lo), core: 2. Of those that a mesh axis runs over, the one named last changes fastest.
Arguments:
- object_field: float32 [2, 8192, 512], P(None, 'tile'), may hold values from -4.2 to 4.2
- probe: float32 [8, 2, 256, 256], P('mode'), may hold values from -2.1 to 2.1
- positions: int32 [2, 64, 2], P(None, 'tile'), may hold values from 0 to 7936, as said below
- measured: float32 [2, 64, 256, 256], P(None, 'tile'), may hold values from 0.1 to 30
Outputs:
- refined_object: float32 [2, 8192, 512], P(None, 'tile')
- refined_probe: float32 [8, 2, 256, 256], P('mode')
The draws below stay inside these ranges and needn't reach their ends.
Inputs may be any that keep to these rules, and one draw needn't show every extreme that they name: positions[b, j] = (row, column). Position j belongs to tile t = j // 2; its row lies from t * 256 - 256 / 2 to t * 256 - 256 / 2 + 256, both ends reached in some tile, and every pattern lies inside the object of 8192 x 512.
All inputs are finite; a program needn't handle non-finite values.
Results may differ from the reference program's by a relative error of at most 0.0001.
Values sent between devices are 32-bit elements; how exact they have to be, the bound alone decides.
A program may use at most 64 MiB of HBM per device.

```python
import math
import jax
import jax.numpy as jnp
from jax import lax

PAT = 256
MODES = 8
P_DEV = 2
POS = 64
STRIP = 256
OBJ_W = 512
OBJ_H = 8192
BATCHES = 2


def draw_positions(key, part):
    row_key, col_key = jax.random.split(jax.random.fold_in(key, 11))
    shift_rows = jax.random.randint(row_key, (BATCHES, POS), 0, STRIP + 1)
    tile_of = jnp.arange(POS, dtype=jnp.int32) // P_DEV
    row_values = tile_of[None, :] * STRIP - PAT // 2 + shift_rows
    row_values = jnp.clip(row_values, 0, OBJ_H - PAT)
    col_values = jax.random.randint(col_key, (BATCHES, POS), 0, OBJ_W - PAT + 1)
    row_values = row_values.at[0, 0].set(0)
    col_values = col_values.at[0, 0].set(0)
    row_values = row_values.at[0, POS - 1].set(OBJ_H - PAT)
    col_values = col_values.at[0, POS - 1].set(OBJ_W - PAT)
    row_values = row_values.at[0, P_DEV].set(STRIP - PAT // 2)
    row_values = row_values.at[1, P_DEV].set(2 * STRIP - PAT // 2)
    return jnp.stack([row_values, col_values], axis=2).astype(jnp.int32)


def steps_of(stream_key, extent, pieces, least, top_value):
    def one(dim, blocks):
        heights = jax.random.uniform(jax.random.fold_in(jax.random.fold_in(stream_key, 6), dim), (blocks,), jnp.float32, least / len(pieces), top_value / len(pieces))
        return jnp.repeat(jnp.exp(heights), extent[dim] // blocks).reshape((-1,) + (1,) * (len(extent) - dim - 1))

    loudness = one(*pieces[0])
    for cut in pieces[1:]:
        loudness = loudness * one(*cut)
    return loudness


def noise(key, dims, deviation, bound, cuts=(), held_as=jnp.bfloat16):
    factor_of = steps_of(key, dims, cuts, -0.22, 0.18) if cuts else 1.0
    entries = jax.random.normal(key, dims, jnp.float32) * deviation * factor_of
    return jnp.minimum(jnp.maximum(entries, -bound), bound).astype(held_as)


def setup_inputs(seed: int = 0) -> dict:
    key_of = jax.random.split(jax.random.key(seed), 5)
    return {
        "object_field": noise(key_of[0], (2, OBJ_H, OBJ_W), 0.7, 4.2, ((1, 32),), jnp.float32),
        "probe": noise(key_of[1], (MODES, 2, PAT, PAT), 0.35, 2.1, ((0, 8),), jnp.float32),
        "positions": draw_positions(jax.random.fold_in(key_of[4], 71), 0),
        "measured": jnp.clip(jnp.exp(math.log(30.0) - 5.7037825 * jax.random.uniform(key_of[3], (BATCHES, POS, PAT, PAT), jnp.float32) ** steps_of(key_of[3], (BATCHES, POS, PAT, PAT), ((1, 32),), -0.2, 0.2)), 0.1, 30.0),
    }


def tables(length):
    index_values = jnp.arange(length, dtype=jnp.int32)
    product = index_values[:, None] * index_values[None, :] % length
    angles = product.astype(jnp.float32) * (2.0 * math.pi / length)
    scaling = 1.0 / math.sqrt(length)
    return (jnp.cos(angles) * scaling, jnp.sin(angles) * scaling)

def apply_left(matrix, target):
    return jnp.einsum('ab,pbc->pac', matrix, target, precision=lax.Precision.HIGHEST)

def apply_right(target, matrix):
    return jnp.einsum('pab,bc->pac', target, matrix, precision=lax.Precision.HIGHEST)

def transform(real_part, imag_part, cosine, sine_table, direction):
    left_real = apply_left(cosine, real_part) + direction * apply_left(sine_table, imag_part)
    left_imag = apply_left(cosine, imag_part) - direction * apply_left(sine_table, real_part)
    out_real = apply_right(left_real, cosine) + direction * apply_right(left_imag, sine_table)
    out_imag = apply_right(left_imag, cosine) - direction * apply_right(left_real, sine_table)
    return (out_real, out_imag)

def place_add(target, placed, row_start, col_start):
    zero_index = jnp.int32(0)
    current = lax.dynamic_slice(target, (zero_index, row_start, col_start), placed.shape)
    return lax.dynamic_update_slice(target, current + placed, (zero_index, row_start, col_start))

def reference(object_field, probe, positions, measured):
    cosine, sine_table = tables(PAT)
    tiles = POS // P_DEV
    for minibatch in range(BATCHES):
        current_object = object_field
        current_probe = probe

        def tile_block(carry, block):
            accumulated, probe_total, coverage_total = carry
            offsets, observed = block

            def cut_one(row_start, col_start):
                return lax.dynamic_slice(current_object, (jnp.int32(0), row_start, col_start), (2, PAT, PAT))
            patches = jax.vmap(cut_one)(offsets[:, 0], offsets[:, 1])
            obj_real = patches[:, 0]
            obj_imag = patches[:, 1]
            far_fields = []
            total_power = jnp.zeros(obj_real.shape, jnp.float32)
            for mode_index in range(MODES):
                probe_real = current_probe[mode_index, 0]
                probe_imag = current_probe[mode_index, 1]
                exit_real = probe_real * obj_real - probe_imag * obj_imag
                exit_imag = probe_real * obj_imag + probe_imag * obj_real
                far_real, far_imag = transform(exit_real, exit_imag, cosine, sine_table, 1.0)
                far_fields.append((far_real, far_imag))
                total_power = total_power + far_real * far_real + far_imag * far_imag
            modulus = jnp.sqrt((observed + 1.0) / (total_power + 1.0)) - 1.0
            grad_real = jnp.zeros(obj_real.shape, jnp.float32)
            grad_imag = jnp.zeros(obj_real.shape, jnp.float32)
            probe_power = jnp.zeros((PAT, PAT), jnp.float32)
            probe_steps = []
            for mode_index in range(MODES):
                probe_real = current_probe[mode_index, 0]
                probe_imag = current_probe[mode_index, 1]
                far_real, far_imag = far_fields[mode_index]
                chi_real, chi_imag = transform(modulus * far_real, modulus * far_imag, cosine, sine_table, -1.0)
                grad_real = grad_real + probe_real * chi_real + probe_imag * chi_imag
                grad_imag = grad_imag + probe_real * chi_imag - probe_imag * chi_real
                probe_power = probe_power + probe_real * probe_real + probe_imag * probe_imag
                step_real = lax.optimization_barrier(jnp.sum(obj_real * chi_real + obj_imag * chi_imag, axis=0))
                step_imag = lax.optimization_barrier(jnp.sum(obj_real * chi_imag - obj_imag * chi_real, axis=0))
                probe_steps.append(jnp.stack([step_real, step_imag]))
            coverage = lax.optimization_barrier(jnp.sum(obj_real * obj_real + obj_imag * obj_imag, axis=0))
            for position in range(P_DEV):
                placed = jnp.stack([grad_real[position], grad_imag[position], probe_power])
                accumulated = place_add(accumulated, placed, offsets[position, 0], offsets[position, 1])
            return ((accumulated, probe_total + jnp.stack(probe_steps), coverage_total + coverage), None)
        start = (jnp.zeros((3, OBJ_H, OBJ_W), jnp.float32), jnp.zeros((MODES, 2, PAT, PAT), jnp.float32), jnp.zeros((PAT, PAT), jnp.float32))
        blocks = (positions[minibatch].reshape(tiles, P_DEV, 2), measured[minibatch].reshape(tiles, P_DEV, PAT, PAT))
        (accumulated, probe_total, coverage_total), unused = lax.scan(tile_block, start, blocks)
        divisor = accumulated[2] + 1.0
        object_field = jnp.stack([current_object[0] + accumulated[0] / divisor, current_object[1] + accumulated[1] / divisor])
        probe = current_probe + probe_total / (coverage_total + 1.0)
    return (object_field, probe)
```

```python
import math

import jax
import jax.numpy as jnp
import ml_dtypes
import numpy as np
from jax import lax
from jax.experimental import pallas as pl
from jax.experimental.pallas import tpu as pltpu
from jax.sharding import PartitionSpec as P

N = 256
HALF = 128
WIDTH = 512
OWN = 32
BATCHES = 2
F32 = jnp.float32
BF16 = jnp.bfloat16
MESH = pl.DeviceIdType.MESH


def split_tables():
    index = np.arange(N)
    angle = (np.outer(index, index) % N) * (2.0 * math.pi / N)
    cosine = np.cos(angle) / math.sqrt(N)
    sine = np.sin(angle) / math.sqrt(N)
    bf16 = ml_dtypes.bfloat16

    def parts(table):
        high = table.astype(np.float32).astype(bf16)
        low = (table - high.astype(np.float64)).astype(np.float32).astype(bf16)
        return high, low

    ch, cl = parts(cosine)
    sh, sl = parts(sine)
    high = np.concatenate([ch, sh], axis=1)
    low = np.concatenate([cl, sl], axis=1)
    right = np.concatenate([high, low, high], axis=0)
    left = np.concatenate(
        [np.concatenate([ch, ch, cl], axis=1), np.concatenate([sh, sh, sl], axis=1)], axis=0
    )
    left = left.reshape(2, 4, 64, 3 * N).transpose(1, 0, 2, 3).reshape(4, 128, 3 * N)
    return right, left


def halves(value):
    high = value.astype(BF16)
    low = (value - high.astype(F32)).astype(BF16)
    return high, low


def dot(a, b):
    return jnp.dot(a, b, preferred_element_type=F32)


def iota(shape, dim):
    return lax.broadcasted_iota(jnp.int32, shape, dim)


def scratch_plan():
    plan = {}
    for b in range(BATCHES):
        plan[f"halo{b}"] = pltpu.VMEM((2, OWN, WIDTH), F32)
        plan[f"patch{b}"] = pltpu.VMEM((2, N, N), F32)
        plan[f"pout{b}"] = pltpu.VMEM((2, 2, OWN, N), F32)
        plan[f"probes{b}"] = pltpu.VMEM((2, 3, N, N), F32)
        plan[f"power{b}"] = pltpu.VMEM((8, 8, N), F32)
        plan[f"inten{b}"] = pltpu.VMEM((N, N), F32)
        plan[f"irecv{b}"] = pltpu.VMEM((3, 64, N), F32)
        plan[f"factor{b}"] = pltpu.VMEM((N, N), F32)
        plan[f"grad{b}"] = pltpu.VMEM((2, N, N), F32)
        plan[f"grecv{b}"] = pltpu.VMEM((7, 2, OWN, N), F32)
        plan[f"gown{b}"] = pltpu.VMEM((2, 2, OWN, N), F32)
        plan[f"gnear{b}"] = pltpu.VMEM((2, 2, OWN, N), F32)
        plan[f"objnew{b}"] = pltpu.VMEM((2, OWN, WIDTH), F32)
        plan[f"dstep{b}"] = pltpu.VMEM((2, 2, N, N), F32)
        plan[f"dsib{b}"] = pltpu.VMEM((2, N, N), F32)
        plan[f"cov{b}"] = pltpu.VMEM((1, N, N), F32)
        plan[f"csib{b}"] = pltpu.VMEM((1, N, N), F32)
        for name, parts in (("p", 2), ("c", 1)):
            plan[f"{name}full{b}"] = pltpu.VMEM((parts, N, N), F32)
            plan[f"{name}y{b}"] = pltpu.VMEM((3, parts, 64, N), F32)
            plan[f"{name}ya{b}"] = pltpu.VMEM((parts, 64, N), F32)
            plan[f"{name}x{b}"] = pltpu.VMEM((3, parts, 16, N), F32)
            plan[f"{name}xa{b}"] = pltpu.VMEM((parts, 16, N), F32)
            plan[f"{name}z{b}"] = pltpu.VMEM((parts, 8, N), F32)
    plan["where_own"] = pltpu.VMEM((8, N), jnp.int32)
    plan["where_near"] = pltpu.VMEM((8, N), jnp.int32)
    plan["ofield"] = pltpu.VMEM((2, N, N), F32)
    plan["far"] = pltpu.VMEM((2, 2, N, N), F32)
    plan["stage"] = pltpu.VMEM((2, 3 * N, 2 * N), BF16)
    plan["illum"] = pltpu.VMEM((OWN, WIDTH), F32)
    return plan


COPIES = 136


def kernel(names, pos, obj, probe, measured, rw, lw, out_obj, out_probe, *scratch):
    buf = dict(zip(names, scratch))
    ssem, rsem = scratch[len(names)], scratch[len(names) + 1]
    t = lax.axis_index("tile")
    m = lax.axis_index("mode")
    x, zh, y = t // 8, (t // 4) % 2, t % 4
    z, c = m // 2, m % 2
    sibling = m + 1 - 2 * c
    side = 1 - 2 * (m // 4)
    t_plus = lax.rem(t + side + 32, 32)
    t_minus = lax.rem(t - side + 32, 32)
    t_pair = t + 4 - 8 * zh
    own_row = pl.multiple_of(OWN * m, OWN)
    y_row = pl.multiple_of(64 * y, 64)
    x_sub = pl.multiple_of(16 * x, 16)
    x_row = pl.multiple_of(64 * y + 16 * x, 16)
    z_sub = pl.multiple_of(8 * zh, 8)
    z_other = pl.multiple_of(8 - 8 * zh, 8)
    z_row = pl.multiple_of(64 * y + 16 * x + 8 * zh, 8)
    i_row = pl.multiple_of(64 * z, 64)
    sent = []

    def send(src, dst, tile, mode):
        index = len(sent)
        copy = pltpu.make_async_remote_copy(
            src_ref=src,
            dst_ref=dst,
            send_sem=ssem.at[index],
            recv_sem=rsem.at[index],
            device_id=(tile, mode),
            device_id_type=MESH,
        )
        copy.start()
        sent.append(copy)
        return copy

    def arrived(copies):
        for copy in copies:
            copy.wait_recv()

    def y_tile(k):
        other = lax.rem(y + k, 4)
        return other, t - y + other

    def x_tile(k):
        other = lax.rem(x + k, 4)
        return other, t - 8 * x + 8 * other

    barrier = pltpu.get_barrier_semaphore()
    partners = [(t, lax.rem(m + k, 8)) for k in range(1, 8)]
    partners += [(y_tile(k)[1], m) for k in range(1, 4)]
    partners += [(x_tile(k)[1], m) for k in range(1, 4)]
    partners += [(t_pair, m), (t_plus, m), (t_minus, m)]
    for partner in partners:
        pl.semaphore_signal(barrier, inc=1, device_id=partner, device_id_type=MESH)

    for b in range(BATCHES):
        for j in range(2):
            core = c if j == 0 else 1 - c
            row = pos[b, core, 0] - N * t
            column = pos[b, core, 1]
            buf["where_own"][4 * b + 2 * j : 4 * b + 2 * j + 1, :] = jnp.full((1, N), row, jnp.int32)
            buf["where_own"][4 * b + 2 * j + 1 : 4 * b + 2 * j + 2, :] = jnp.full(
                (1, N), column, jnp.int32
            )
    for part in range(2):
        buf["probes0"][0, part] = probe[0, part]
    pl.semaphore_wait(barrier, len(partners))

    def place(ref, b, j):
        return ref[4 * b + 2 * j : 4 * b + 2 * j + 1, :], ref[4 * b + 2 * j + 1 : 4 * b + 2 * j + 2, :]

    class Reduce:
        def __init__(self, name, b):
            self.full, self.y, self.ya, self.x, self.xa, self.z = (
                buf[f"{name}{part}{b}"] for part in ("full", "y", "ya", "x", "xa", "z")
            )

        def start_y(self):
            self.copies = []
            for k in range(1, 4):
                other, tile = y_tile(k)
                rows = pl.ds(pl.multiple_of(64 * other, 64), 64)
                self.copies.append(send(self.full.at[:, rows], self.y.at[k - 1], tile, m))

        def start_x(self):
            arrived(self.copies)
            self.ya[...] = self.full[:, pl.ds(y_row, 64)] + self.y[0] + self.y[1] + self.y[2]
            self.copies = []
            for k in range(1, 4):
                other, tile = x_tile(k)
                rows = pl.ds(pl.multiple_of(16 * other, 16), 16)
                self.copies.append(send(self.ya.at[:, rows], self.x.at[k - 1], tile, m))

        def start_z(self):
            arrived(self.copies)
            self.xa[...] = self.ya[:, pl.ds(x_sub, 16)] + self.x[0] + self.x[1] + self.x[2]
            self.copies = [send(self.xa.at[:, pl.ds(z_other, 8)], self.z, t_pair, m)]

        def finish(self):
            arrived(self.copies)
            return self.xa[:, pl.ds(z_sub, 8)] + self.z[...]

    class Gather:
        def __init__(self, view):
            self.view = view

        def start_z(self):
            part = self.view(pl.ds(z_row, 8))
            self.copies = [send(part, part, t_pair, m)]

        def start_x(self):
            arrived(self.copies)
            part = self.view(pl.ds(x_row, 16))
            self.copies = [send(part, part, x_tile(k)[1], m) for k in range(1, 4)]

        def start_y(self):
            arrived(self.copies)
            part = self.view(pl.ds(y_row, 64))
            self.copies = [send(part, part, y_tile(k)[1], m) for k in range(1, 4)]

        def finish(self):
            arrived(self.copies)

    def send_power(b, real, imag):
        power = buf[f"power{b}"]
        power[0] = real * real + imag * imag
        return [
            send(power.at[0], power.at[k], t, lax.rem(m + k, 8)) for k in range(1, 8)
        ]

    def sum_power(b, copies):
        arrived(copies)
        power = buf[f"power{b}"]
        total = power[0]
        for k in range(1, 8):
            total = total + power[k]
        return total

    def send_patches(b, field, field_rows):
        halo, out, patch = buf[f"halo{b}"], buf[f"pout{b}"], buf[f"patch{b}"]
        rows = own_row + iota((OWN, N), 0)
        columns = iota((OWN, N), 1)
        for j in range(2):
            row, column = place(buf["where_own"], b, j)
            ahead = rows - row
            inside = (ahead >= 0) & (ahead < N)
            first = columns >= column
            for part in range(2):
                low = jnp.where(inside, field[part, field_rows, :N], halo[part, :, :N])
                high = jnp.where(inside, field[part, field_rows, N:], halo[part, :, N:])
                out[j, part] = jnp.where(first, low, high)
        copies = []
        for k in range(1, 8):
            copies.append(
                send(out.at[k % 2], patch.at[:, pl.ds(own_row, OWN)], t, lax.rem(m + k, 8))
            )
        patch[:, pl.ds(own_row, OWN)] = out[0]
        return copies

    def shifted(real, imag, row, column):
        i0, i1 = iota((N, N), 0), iota((N, N), 1)
        pick = (((i0 + row) & (N - 1)) == i1).astype(F32).astype(BF16)
        high, low = halves(jnp.concatenate([real, imag], axis=1))
        moved = dot(jnp.concatenate([pick, pick], axis=1), jnp.concatenate([high, low], axis=0))
        pick = (((i1 + column) & (N - 1)) == i0).astype(F32).astype(BF16)
        high, low = halves(jnp.concatenate([moved[:, :N], moved[:, N:]], axis=0))
        moved = dot(jnp.concatenate([high, low], axis=1), jnp.concatenate([pick, pick], axis=0))
        return moved[:N], moved[N:]

    def chunk_rows(q):
        return pl.ds(pl.multiple_of(q * 64, 64), 64)

    stage = buf["stage"]

    def right_stage(mode, q, real, imag, sign):
        high, low = halves(jnp.concatenate([real, imag], axis=0))
        product = dot(jnp.concatenate([high, high, low], axis=1), rw[...])
        out_real = product[:64, :N] + sign * product[64:, N:]
        out_imag = product[64:, :N] - sign * product[:64, N:]
        high, low = halves(jnp.concatenate([out_real, out_imag], axis=1))
        stage[mode, pl.ds(pl.multiple_of(q * 64, 64), 64), :] = high
        stage[mode, pl.ds(pl.multiple_of(N + q * 64, 64), 64), :] = low
        stage[mode, pl.ds(pl.multiple_of(2 * N + q * 64, 64), 64), :] = high

    def left_stage(mode, q, sign):
        product = dot(lw[q], stage[mode])
        return (
            product[:64, :N] + sign * product[64:, N:],
            product[:64, N:] - sign * product[64:, :N],
        )

    far, ofield = buf["far"], buf["ofield"]

    def forward(b):
        probes, inten = buf[f"probes{b}"], buf[f"inten{b}"]

        def first(q, carry):
            rows = chunk_rows(q)
            o_real, o_imag = ofield[0, rows, :], ofield[1, rows, :]
            for mode in range(2):
                p_real, p_imag = probes[mode, 0, rows, :], probes[mode, 1, rows, :]
                right_stage(
                    mode,
                    q,
                    p_real * o_real - p_imag * o_imag,
                    p_real * o_imag + p_imag * o_real,
                    1.0,
                )
            return carry

        lax.fori_loop(0, 4, first, 0)

        def second(q, carry):
            rows = chunk_rows(q)
            total = None
            for mode in range(2):
                f_real, f_imag = left_stage(mode, q, 1.0)
                far[mode, 0, rows, :] = f_real
                far[mode, 1, rows, :] = f_imag
                power = f_real * f_real + f_imag * f_imag
                total = power if total is None else total + power
            inten[rows, :] = total
            return carry

        lax.fori_loop(0, 4, second, 0)

    def inverse(b):
        probes, factor = buf[f"probes{b}"], buf[f"factor{b}"]
        grad, dstep = buf[f"grad{b}"], buf[f"dstep{b}"]

        def first(q, carry):
            rows = chunk_rows(q)
            scale = factor[rows, :]
            for mode in range(2):
                right_stage(mode, q, scale * far[mode, 0, rows, :], scale * far[mode, 1, rows, :], -1.0)
            return carry

        lax.fori_loop(0, 4, first, 0)

        def second(q, carry):
            rows = chunk_rows(q)
            o_real, o_imag = ofield[0, rows, :], ofield[1, rows, :]
            g_real = jnp.zeros((64, N), F32)
            g_imag = jnp.zeros((64, N), F32)
            for mode in range(2):
                c_real, c_imag = left_stage(mode, q, -1.0)
                p_real, p_imag = probes[mode, 0, rows, :], probes[mode, 1, rows, :]
                g_real = g_real + p_real * c_real + p_imag * c_imag
                g_imag = g_imag + p_real * c_imag - p_imag * c_real
                dstep[mode, 0, rows, :] = o_real * c_real + o_imag * c_imag
                dstep[mode, 1, rows, :] = o_real * c_imag - o_imag * c_real
            grad[0, rows, :] = g_real
            grad[1, rows, :] = g_imag
            return carry

        lax.fori_loop(0, 4, second, 0)
        row, column = place(buf["where_own"], b, 0)
        grad[0], grad[1] = shifted(grad[0], grad[1], -row, -column)

    def masks(b):
        rows = own_row + iota((OWN, N), 0)
        columns = iota((OWN, N), 1)
        found = []
        for ref, near in ((buf["where_own"], False), (buf["where_near"], True)):
            for j in range(2):
                row, column = place(ref, b, j)
                ahead = rows - row
                inside = (ahead >= 0) & (ahead < N)
                if near:
                    inside = jnp.logical_not(inside)
                first = columns >= column
                found.append((inside & first, inside & jnp.logical_not(first)))
        return found

    def illumination(b):
        high, low = halves(buf[f"probes{b}"][0, 2])
        power = jnp.concatenate([high, low], axis=0)
        rows = own_row + iota((OWN, N), 0)
        lanes = iota((OWN, N), 1)
        places = [
            place(ref, b, j) for ref in (buf["where_own"], buf["where_near"]) for j in range(2)
        ]
        picks = []
        for row, _ in places:
            pick = (((rows - row) & (N - 1)) == lanes).astype(F32).astype(BF16)
            picks.append(jnp.concatenate([pick, pick], axis=1))
        taken = dot(jnp.concatenate(picks, axis=0), power)
        i0, i1 = iota((N, N), 0), iota((N, N), 1)
        left = jnp.zeros((OWN, N), F32)
        right = jnp.zeros((OWN, N), F32)
        for index, ((_, column), (in_left, in_right)) in enumerate(zip(places, masks(b))):
            pick = (((i1 - column) & (N - 1)) == i0).astype(F32).astype(BF16)
            high, low = halves(taken[OWN * index : OWN * (index + 1)])
            moved = dot(
                jnp.concatenate([high, low], axis=1), jnp.concatenate([pick, pick], axis=0)
            )
            left = left + jnp.where(in_left, moved, 0.0)
            right = right + jnp.where(in_right, moved, 0.0)
        buf["illum"][:, :N] = left
        buf["illum"][:, N:] = right

    def update_object(b, field, field_rows):
        own, near, new = buf[f"gown{b}"], buf[f"gnear{b}"], buf[f"objnew{b}"]
        found = masks(b)
        for part in range(2):
            steps = [own[0, part], own[1, part], near[0, part], near[1, part]]
            for side_index, columns in ((0, slice(0, N)), (1, slice(N, WIDTH))):
                total = jnp.zeros((OWN, N), F32)
                for step, mask in zip(steps, found):
                    total = total + jnp.where(mask[side_index], step, 0.0)
                new[part, :, columns] = field[part, field_rows, columns] + total / (
                    buf["illum"][:, columns] + 1.0
                )

    halo_copy = send(obj.at[:, pl.ds(own_row, OWN)], buf["halo0"], t_minus, m)
    probe_copy = send(buf["probes0"].at[0, pl.ds(0, 2)], buf["probes0"].at[1, pl.ds(0, 2)], t, sibling)
    where_copy = send(buf["where_own"], buf["where_near"], t_plus, m)
    power_copies = send_power(0, probe[0, 0, pl.ds(z_row, 8)], probe[0, 1, pl.ds(z_row, 8)])
    arrived([halo_copy])
    patch_copies = send_patches(0, obj, pl.ds(own_row, OWN))
    buf["probes0"][0, 2, pl.ds(z_row, 8)] = sum_power(0, power_copies)
    power_gather = Gather(lambda rows: buf["probes0"].at[0, 2, rows])
    power_gather.start_z()
    arrived([where_copy])
    probe_gather = None

    for b in range(BATCHES):
        last = b == BATCHES - 1
        if b == 0:
            field, field_rows = obj, pl.ds(own_row, OWN)
        else:
            field, field_rows = buf[f"objnew{b - 1}"], slice(0, OWN)
        arrived(patch_copies)
        row, column = place(buf["where_own"], b, 0)
        patch = buf[f"patch{b}"]
        ofield[0], ofield[1] = shifted(patch[0], patch[1], row, column)
        cover = buf[f"cov{b}"]
        cover[0] = ofield[0] * ofield[0] + ofield[1] * ofield[1]
        cover_copy = send(cover, buf[f"csib{b}"], t, sibling)
        arrived([probe_copy])
        forward(b)
        inten, irecv, factor = buf[f"inten{b}"], buf[f"irecv{b}"], buf[f"factor{b}"]
        copies = []
        for k in range(1, 4):
            other = lax.rem(z + k, 4)
            rows = pl.ds(pl.multiple_of(64 * other, 64), 64)
            copies.append(send(inten.at[rows], irecv.at[k - 1], t, 2 * other + c))
        if b == 0:
            power_gather.start_x()
        arrived([cover_copy])
        buf[f"cfull{b}"][...] = cover[...] + buf[f"csib{b}"][...]
        cover_sum = Reduce("c", b)
        cover_sum.start_y()
        arrived(copies)
        own_rows = pl.ds(i_row, 64)
        total = inten[own_rows, :] + irecv[0] + irecv[1] + irecv[2]
        factor[own_rows, :] = jnp.sqrt((measured[b, c, own_rows, :] + 1.0) / (total + 1.0)) - 1.0
        copies = []
        for k in range(1, 4):
            other = lax.rem(z + k, 4)
            copies.append(send(factor.at[own_rows], factor.at[own_rows], t, 2 * other + c))
        if b == 0:
            power_gather.start_y()
        cover_sum.start_x()
        arrived(copies)
        inverse(b)
        grad, grecv, dstep = buf[f"grad{b}"], buf[f"grecv{b}"], buf[f"dstep{b}"]
        copies = []
        for k in range(1, 8):
            other = lax.rem(m + k, 8)
            rows = pl.ds(pl.multiple_of(OWN * other, OWN), OWN)
            copies.append(send(grad.at[:, rows], grecv.at[k - 1], t, other))
        step_copy = send(dstep.at[1], buf[f"dsib{b}"], t, sibling)
        cover_sum.start_z()
        if b == 0:
            power_gather.finish()
        arrived([step_copy])
        buf[f"pfull{b}"][...] = dstep[0] + buf[f"dsib{b}"][...]
        probe_sum = Reduce("p", b)
        probe_sum.start_y()
        illumination(b)
        arrived(copies)
        gown = buf[f"gown{b}"]
        gown[0] = grad[:, pl.ds(own_row, OWN)] + grecv[1] + grecv[3] + grecv[5]
        gown[1] = grecv[0] + grecv[2] + grecv[4] + grecv[6]
        near_copy = send(gown, buf[f"gnear{b}"], t_plus, m)
        probe_sum.start_x()
        arrived([near_copy])
        update_object(b, field, field_rows)
        new = buf[f"objnew{b}"]
        if last:
            rows = pl.ds(own_row, OWN)
            final_copies = [
                send(new, out_obj.at[:, rows], t, lax.rem(m + k, 8)) for k in range(1, 8)
            ]
            out_obj[:, rows] = new[...]
        else:
            halo_copy = send(new, buf[f"halo{b + 1}"], t_minus, m)
        probe_sum.start_z()
        coverage = cover_sum.finish()[0]
        step = probe_sum.finish()
        probes = buf[f"probes{b}"]
        rows = pl.ds(z_row, 8)
        updated = [probes[0, part, rows, :] + step[part] / (coverage + 1.0) for part in range(2)]
        if last:
            for part in range(2):
                out_probe[0, part, rows, :] = updated[part]
            gather = Gather(lambda rows: out_probe.at[0, :, rows])
            gather.start_z()
            gather.start_x()
            gather.start_y()
            arrived(final_copies)
            gather.finish()
        else:
            following = buf[f"probes{b + 1}"]
            for part in range(2):
                following[0, part, rows, :] = updated[part]
            power_copies = send_power(b + 1, updated[0], updated[1])
            arrived([halo_copy])
            patch_copies = send_patches(b + 1, new, slice(0, OWN))
            following[0, 2, rows, :] = sum_power(b + 1, power_copies)
            gather = Gather(lambda rows: following.at[0, :, rows])
            gather.start_z()
            gather.start_x()
            gather.start_y()
            gather.finish()
            probe_copy = send(following.at[0, pl.ds(0, 2)], following.at[1, pl.ds(0, 2)], t, sibling)

    for copy in sent:
        copy.wait_send()


def shards(object_field, probe, positions, measured):
    right, left = split_tables()
    plan = scratch_plan()
    names = list(plan)

    def body(*refs):
        kernel(names, *refs)

    vmem = pl.BlockSpec(memory_space=pltpu.VMEM)
    return pl.pallas_call(
        body,
        name="refine",
        out_shape=(
            jax.ShapeDtypeStruct(object_field.shape, F32),
            jax.ShapeDtypeStruct(probe.shape, F32),
        ),
        in_specs=[pl.BlockSpec(memory_space=pltpu.SMEM)] + [vmem] * 5,
        out_specs=(vmem, vmem),
        scratch_shapes=list(plan.values())
        + [pltpu.SemaphoreType.DMA((COPIES,)), pltpu.SemaphoreType.DMA((COPIES,))],
        compiler_params=pltpu.CompilerParams(
            collective_id=0, has_side_effects=True, vmem_limit_bytes=56 * 1024 * 1024
        ),
    )(positions, object_field, probe, measured, jnp.asarray(right), jnp.asarray(left))


def solution(mesh):
    in_specs = (
        P(None, "tile", None),
        P("mode", None, None, None),
        P(None, "tile", None),
        P(None, "tile", None, None),
    )
    out_specs = (P(None, "tile", None), P("mode", None, None, None))
    return jax.shard_map(shards, mesh=mesh, in_specs=in_specs, out_specs=out_specs, check_vma=False)
```

```python
import math

import jax
import jax.numpy as jnp
import ml_dtypes
import numpy as np
from jax import lax
from jax.experimental import pallas as pl
from jax.experimental.pallas import tpu as pltpu
from jax.sharding import PartitionSpec as P

N = 256
HALF = 128
WIDTH = 512
OWN = 32
BATCHES = 2
F32 = jnp.float32
BF16 = jnp.bfloat16
MESH = pl.DeviceIdType.MESH


def split_tables():
    index = np.arange(N)
    angle = (np.outer(index, index) % N) * (2.0 * math.pi / N)
    cosine = np.cos(angle) / math.sqrt(N)
    sine = np.sin(angle) / math.sqrt(N)
    bf16 = ml_dtypes.bfloat16

    def parts(table):
        high = table.astype(np.float32).astype(bf16)
        low = (table - high.astype(np.float64)).astype(np.float32).astype(bf16)
        return high, low

    ch, cl = parts(cosine)
    sh, sl = parts(sine)
    high = np.concatenate([ch, sh], axis=1)
    low = np.concatenate([cl, sl], axis=1)
    right = np.concatenate([high, low, high], axis=0)
    left = np.concatenate(
        [np.concatenate([ch, ch, cl], axis=1), np.concatenate([sh, sh, sl], axis=1)], axis=0
    )
    left = left.reshape(2, 4, 64, 3 * N).transpose(1, 0, 2, 3).reshape(4, 128, 3 * N)
    return right, left


def halves(value):
    high = value.astype(BF16)
    low = (value - high.astype(F32)).astype(BF16)
    return high, low


def dot(a, b):
    return jnp.dot(a, b, preferred_element_type=F32)


def iota(shape, dim):
    return lax.broadcasted_iota(jnp.int32, shape, dim)


def reduce_plan(parts):
    return dict(
        full=pltpu.VMEM((parts, N, N), F32),
        one=pltpu.VMEM((2, 3, parts, 32, N), F32),
        onesum=pltpu.VMEM((2, parts, 32, N), F32),
        two=pltpu.VMEM((2, 3, parts, 8, N), F32),
        twosum=pltpu.VMEM((2, parts, 8, N), F32),
        pair=pltpu.VMEM((2, parts, 8, N), F32),
    )


def batch_plan():
    return dict(
        halo=pltpu.VMEM((2, OWN, WIDTH), F32),
        patch=pltpu.VMEM((2, N, N), F32),
        pout=pltpu.VMEM((2, 2, OWN, N), F32),
        probes=pltpu.VMEM((2, 3, N, N), F32),
        power=pltpu.VMEM((8, 2, 8, N), F32),
        inten=pltpu.VMEM((N, N), F32),
        irecv=pltpu.VMEM((3, 64, N), F32),
        factor=pltpu.VMEM((N, N), F32),
        grad=pltpu.VMEM((2, N, N), F32),
        grecv=pltpu.VMEM((7, 2, OWN, N), F32),
        gown=pltpu.VMEM((2, 2, OWN, N), F32),
        gminus=pltpu.VMEM((2, 2, OWN, N), F32),
        gplus=pltpu.VMEM((2, 2, OWN, N), F32),
        objnew=pltpu.VMEM((2, OWN, WIDTH), F32),
        dstep=pltpu.VMEM((2, 2, N, N), F32),
        dsib=pltpu.VMEM((2, N, N), F32),
        cov=pltpu.VMEM((1, N, N), F32),
        csib=pltpu.VMEM((1, N, N), F32),
        probe_sum=reduce_plan(2),
        cover_sum=reduce_plan(1),
    )


def scratch_plan():
    common = dict(
        edge_plus=pltpu.VMEM((2, 16, WIDTH), F32),
        edge_minus=pltpu.VMEM((2, 16, WIDTH), F32),
        edge_out=pltpu.VMEM((2, 2, 16, N), F32),
        edge_rows=pltpu.VMEM((2, HALF, N), F32),
        observed=pltpu.VMEM((2, N, N), F32),
        rtable=pltpu.VMEM((3 * N, 2 * N), BF16),
        ltable=pltpu.VMEM((4, 128, 3 * N), BF16),
        where_own=pltpu.VMEM((8, N), jnp.int32),
        where_minus=pltpu.VMEM((8, N), jnp.int32),
        where_plus=pltpu.VMEM((8, N), jnp.int32),
        rolled=pltpu.VMEM((2, 2, N, N), F32),
        far=pltpu.VMEM((2, 2, N, N), F32),
        stage=pltpu.VMEM((2, 3 * N, 2 * N), BF16),
        illum=pltpu.VMEM((2, OWN, WIDTH), F32),
    )
    return [common] + [batch_plan() for _ in range(BATCHES)]


class Box:
    def __init__(self, entries):
        for name, entry in entries.items():
            setattr(self, name, Box(entry) if isinstance(entry, dict) else entry)


COPIES = 200


def kernel(tree, pos, obj, probe, measured, rtable, ltable, out_obj, out_probe, *scratch):
    ssem, rsem, lsem = scratch[-3:]
    com, *mem = [Box(entries) for entries in jax.tree.unflatten(tree, scratch[:-3])]
    t = lax.axis_index("tile")
    m = lax.axis_index("mode")
    x, zh, y = t // 8, (t // 4) % 2, t % 4
    z, c = m // 2, m % 2
    sibling = m + 1 - 2 * c
    side = 1 - 2 * (m // 4)
    t_plus = lax.rem(t + side + 32, 32)
    t_minus = lax.rem(t - side + 32, 32)
    t_pair = t + 4 - 8 * zh
    own_row = pl.multiple_of(OWN * m, OWN)
    i_row = pl.multiple_of(64 * z, 64)
    sent = []

    def send(src, dst, tile, mode):
        index = len(sent)
        copy = pltpu.make_async_remote_copy(
            src_ref=src,
            dst_ref=dst,
            send_sem=ssem.at[index],
            recv_sem=rsem.at[index],
            device_id=(tile, mode),
            device_id_type=MESH,
        )
        copy.start()
        sent.append(copy)
        return copy

    def arrived(copies):
        for copy in copies:
            copy.wait_recv()

    def y_tile(k):
        other = lax.rem(y + k, 4)
        return other, t - y + other

    def x_tile(k):
        other = lax.rem(x + k, 4)
        return other, t - 8 * x + 8 * other

    barrier = pltpu.get_barrier_semaphore()
    rw, lw, observed = com.rtable, com.ltable, com.observed
    loads = [
        pltpu.make_async_copy(rtable, rw, lsem.at[0]),
        pltpu.make_async_copy(ltable, lw, lsem.at[1]),
        pltpu.make_async_copy(measured.at[0, c], observed.at[0], lsem.at[2]),
        pltpu.make_async_copy(measured.at[1, c], observed.at[1], lsem.at[3]),
    ]
    partners = [(t, lax.rem(m + k, 8)) for k in range(1, 8)]
    partners += [(y_tile(k)[1], m) for k in range(1, 4)]
    partners += [(x_tile(k)[1], m) for k in range(1, 4)]
    partners += [(t_pair, m), (t_plus, m), (t_minus, m)]
    for partner in partners:
        pl.semaphore_signal(barrier, inc=1, device_id=partner, device_id_type=MESH)
    for load in loads:
        load.start()

    for b in range(BATCHES):
        for j in range(2):
            core = c if j == 0 else 1 - c
            row = pos[b, core, 0] - N * t
            column = pos[b, core, 1]
            com.where_own[4 * b + 2 * j : 4 * b + 2 * j + 1, :] = jnp.full((1, N), row, jnp.int32)
            com.where_own[4 * b + 2 * j + 1 : 4 * b + 2 * j + 2, :] = jnp.full(
                (1, N), column, jnp.int32
            )
    for part in range(2):
        mem[0].probes[0, part] = probe[0, part]
    pl.semaphore_wait(barrier, len(partners))

    def place(ref, b, j):
        return ref[4 * b + 2 * j : 4 * b + 2 * j + 1, :], ref[4 * b + 2 * j + 1 : 4 * b + 2 * j + 2, :]

    def whole(part, other):
        return pl.ds(pl.multiple_of(HALF * part + 32 * other, 32), 32)

    def piece(other):
        return pl.ds(pl.multiple_of(8 * other, 8), 8)

    lines = ((y_tile, x_tile), (x_tile, y_tile))
    spots = ((y, x), (x, y))
    held = [
        pl.ds(pl.multiple_of(HALF * part + 32 * spots[part][0] + 8 * spots[part][1], 8), 8)
        for part in range(2)
    ]

    class Reduce:
        def __init__(self, box):
            self.full, self.one, self.onesum = box.full, box.one, box.onesum
            self.two, self.twosum, self.pair = box.two, box.twosum, box.pair

        def start_one(self):
            self.copies = [[], []]
            for k in range(1, 4):
                for part in range(2):
                    other, tile = lines[part][0](k)
                    self.copies[part].append(
                        send(self.full.at[:, whole(part, other)], self.one.at[part, k - 1], tile, m)
                    )

        def start_two(self):
            after = [[], []]
            for part in range(2):
                arrived(self.copies[part])
                self.onesum[part] = (
                    self.full[:, whole(part, spots[part][0])]
                    + self.one[part, 0]
                    + self.one[part, 1]
                    + self.one[part, 2]
                )
                for k in range(1, 4):
                    other, tile = lines[part][1](k)
                    after[part].append(
                        send(
                            self.onesum.at[part, :, piece(other)], self.two.at[part, k - 1], tile, m
                        )
                    )
            self.copies = after

        def start_pair(self):
            for part in range(2):
                arrived(self.copies[part])
                self.twosum[part] = (
                    self.onesum[part, :, piece(spots[part][1])]
                    + self.two[part, 0]
                    + self.two[part, 1]
                    + self.two[part, 2]
                )
            self.copies = [send(self.twosum, self.pair, t_pair, m)]

        def finish(self):
            arrived(self.copies)
            return [self.twosum[part] + self.pair[part] for part in range(2)]

    class Gather:
        def __init__(self, view):
            self.view = view

        def start_one(self):
            self.copies = [[], []]
            for k in range(1, 4):
                for part in range(2):
                    rows = self.view(held[part])
                    self.copies[part].append(send(rows, rows, lines[part][1](k)[1], m))

        def start_two(self):
            after = [[], []]
            for part in range(2):
                arrived(self.copies[part])
                rows = self.view(whole(part, spots[part][0]))
                for k in range(1, 4):
                    after[part].append(send(rows, rows, lines[part][0](k)[1], m))
            self.copies = after

        def finish(self):
            for part in range(2):
                arrived(self.copies[part])

    def send_power(b, values):
        power = mem[b].power
        for part, (real, imag) in enumerate(values):
            power[0, part] = real * real + imag * imag
        return [send(power.at[0], power.at[k], t, lax.rem(m + k, 8)) for k in range(1, 8)]

    def sum_power(b, copies):
        arrived(copies)
        power = mem[b].power
        total = power[0]
        for k in range(1, 8):
            total = total + power[k]
        for part in range(2):
            mem[b].probes[0, 2, held[part], :] = total[part]

    def send_edges():
        plus, minus, out, rows = com.edge_plus, com.edge_minus, com.edge_out, com.edge_rows
        columns = iota((16, N), 1)
        spot = pl.ds(pl.multiple_of(16 * m, 16), 16)
        for j in range(2):
            row, column = place(com.where_own, 0, j)
            ahead = jnp.broadcast_to(row, (16, N)) >= 0
            first = columns >= column
            for part in range(2):
                low = jnp.where(ahead, plus[part, :, :N], minus[part, :, :N])
                high = jnp.where(ahead, plus[part, :, N:], minus[part, :, N:])
                out[j, part] = jnp.where(first, low, high)
        copies = [
            send(out.at[k % 2], rows.at[:, spot], t, lax.rem(m + k, 8)) for k in range(1, 8)
        ]
        rows[:, spot] = out[0]
        return copies

    def join_edges():
        rows, patch = com.edge_rows, mem[0].patch
        row, column = place(com.where_own, 0, 0)
        columns = iota((HALF, N), 1)
        first = columns >= column
        for half in range(2):
            span = slice(HALF * half, HALF * (half + 1))
            ahead = HALF * half + iota((HALF, N), 0) - row
            inside = (ahead >= 0) & (ahead < N)
            for part in range(2):
                own = jnp.where(first, obj[part, span, :N], obj[part, span, N:])
                patch[part, span, :] = jnp.where(inside, own, rows[part])

    def send_patches(b, field, halo):
        out, patch = mem[b].pout, mem[b].patch
        rows = own_row + iota((OWN, N), 0)
        columns = iota((OWN, N), 1)
        for j in range(2):
            row, column = place(com.where_own, b, j)
            ahead = rows - row
            inside = (ahead >= 0) & (ahead < N)
            first = columns >= column
            for part in range(2):
                low = jnp.where(inside, field[part, :, :N], halo[part, :, :N])
                high = jnp.where(inside, field[part, :, N:], halo[part, :, N:])
                out[j, part] = jnp.where(first, low, high)
        copies = []
        for k in range(1, 8):
            copies.append(
                send(out.at[k % 2], patch.at[:, pl.ds(own_row, OWN)], t, lax.rem(m + k, 8))
            )
        patch[:, pl.ds(own_row, OWN)] = out[0]
        return copies

    def shifted(real, imag, row, column):
        i0, i1 = iota((N, N), 0), iota((N, N), 1)
        pick = (((i0 + row) & (N - 1)) == i1).astype(F32).astype(BF16)
        both = real if imag is None else jnp.concatenate([real, imag], axis=1)
        high, low = halves(both)
        moved = dot(jnp.concatenate([pick, pick], axis=1), jnp.concatenate([high, low], axis=0))
        pick = (((i1 + column) & (N - 1)) == i0).astype(F32).astype(BF16)
        if imag is not None:
            moved = jnp.concatenate([moved[:, :N], moved[:, N:]], axis=0)
        high, low = halves(moved)
        moved = dot(jnp.concatenate([high, low], axis=1), jnp.concatenate([pick, pick], axis=0))
        return moved[:N], moved[N:]

    def roll_probes(b):
        row, column = place(com.where_own, b, 0)
        probes = mem[b].probes
        for mode in range(2):
            rolled[mode, 0], rolled[mode, 1] = shifted(
                probes[mode, 0], probes[mode, 1], -row, -column
            )

    def unroll_step(b, mode):
        row, column = place(com.where_own, b, 0)
        dstep = mem[b].dstep
        dstep[mode, 0], dstep[mode, 1] = shifted(dstep[mode, 0], dstep[mode, 1], row, column)

    def unrolled_one(field, b):
        row, column = place(com.where_own, b, 0)
        return shifted(field, None, row, column)[0]

    def chunk_rows(q):
        return pl.ds(pl.multiple_of(q * 64, 64), 64)

    stage = com.stage

    def right_stage(mode, q, real, imag, sign):
        high, low = halves(jnp.concatenate([real, imag], axis=0))
        product = dot(jnp.concatenate([high, high, low], axis=1), rw[...])
        out_real = product[:64, :N] + sign * product[64:, N:]
        out_imag = product[64:, :N] - sign * product[:64, N:]
        high, low = halves(jnp.concatenate([out_real, out_imag], axis=1))
        stage[mode, pl.ds(pl.multiple_of(q * 64, 64), 64), :] = high
        stage[mode, pl.ds(pl.multiple_of(N + q * 64, 64), 64), :] = low
        stage[mode, pl.ds(pl.multiple_of(2 * N + q * 64, 64), 64), :] = high

    def left_stage(mode, q, sign):
        product = dot(lw[q], stage[mode])
        return (
            product[:64, :N] + sign * product[64:, N:],
            product[:64, N:] - sign * product[64:, :N],
        )

    far, rolled = com.far, com.rolled

    def forward(b):
        ofield, inten = mem[b].patch, mem[b].inten

        def first(q, carry):
            rows = chunk_rows(q)
            o_real, o_imag = ofield[0, rows, :], ofield[1, rows, :]
            for mode in range(2):
                p_real, p_imag = rolled[mode, 0, rows, :], rolled[mode, 1, rows, :]
                right_stage(
                    mode,
                    q,
                    p_real * o_real - p_imag * o_imag,
                    p_real * o_imag + p_imag * o_real,
                    1.0,
                )
            return carry

        lax.fori_loop(0, 4, first, 0)

        irecv, copies = mem[b].irecv, []
        for k in (1, 2, 3, 0):
            q = lax.rem(z + k, 4)
            rows = chunk_rows(q)
            total = None
            for mode in range(2):
                f_real, f_imag = left_stage(mode, q, 1.0)
                far[mode, 0, rows, :] = f_real
                far[mode, 1, rows, :] = f_imag
                power = f_real * f_real + f_imag * f_imag
                total = power if total is None else total + power
            inten[rows, :] = total
            if k:
                copies.append(send(inten.at[rows], irecv.at[k - 1], t, 2 * q + c))
        return copies

    def inverse(b, copies, between):
        ofield, factor = mem[b].patch, mem[b].factor
        grad, dstep, grecv = mem[b].grad, mem[b].dstep, mem[b].grecv

        for k in range(4):
            if k:
                arrived(copies[k - 1 : k])
            q = lax.rem(z - k + 4, 4)
            rows = chunk_rows(q)
            scale = factor[rows, :]
            for mode in range(2):
                right_stage(mode, q, scale * far[mode, 0, rows, :], scale * far[mode, 1, rows, :], -1.0)
        between()

        sends = [None] * 8
        for k in (2, 1, 3, 0):
            q = lax.rem(z + k, 4)
            rows = chunk_rows(q)
            o_real, o_imag = ofield[0, rows, :], ofield[1, rows, :]
            g_real = jnp.zeros((64, N), F32)
            g_imag = jnp.zeros((64, N), F32)
            for mode in range(2):
                c_real, c_imag = left_stage(mode, q, -1.0)
                p_real, p_imag = rolled[mode, 0, rows, :], rolled[mode, 1, rows, :]
                g_real = g_real + p_real * c_real + p_imag * c_imag
                g_imag = g_imag + p_real * c_imag - p_imag * c_real
                dstep[mode, 0, rows, :] = o_real * c_real + o_imag * c_imag
                dstep[mode, 1, rows, :] = o_real * c_imag - o_imag * c_real
            grad[0, rows, :] = g_real
            grad[1, rows, :] = g_imag
            for twin in range(2):
                if k == 0 and twin == 0:
                    continue
                core = c if twin == 0 else 1 - c
                part = pl.ds(pl.multiple_of(OWN * (2 * q + core), OWN), OWN)
                slot = 2 * k + twin
                sends[slot] = send(grad.at[:, part], grecv.at[slot - 1], t, 2 * q + core)
        return sends[1:]

    def masks(ref, b, j):
        rows = own_row + iota((OWN, N), 0)
        row, column = place(ref, b, j)
        ahead = rows - row
        inside = (ahead >= 0) & (ahead < N)
        first = iota((OWN, N), 1) >= column
        return inside, first

    def sides(ref, b, j, here):
        inside, first = masks(ref, b, j)
        if not here:
            inside = jnp.logical_not(inside)
        return inside & first, inside & jnp.logical_not(first)

    def illumination(b, with_halo):
        high, low = halves(mem[b].probes[0, 2])
        power = jnp.concatenate([high, low], axis=0)
        rows = own_row + iota((OWN, N), 0)
        lanes = iota((OWN, N), 1)
        refs = [com.where_own, com.where_minus] + ([com.where_plus] if with_halo else [])
        spots_of = [(ref, j) for ref in refs for j in range(2)]
        picks = []
        for ref, j in spots_of:
            row, _ = place(ref, b, j)
            pick = (((rows - row) & (N - 1)) == lanes).astype(F32).astype(BF16)
            picks.append(jnp.concatenate([pick, pick], axis=1))
        taken = dot(jnp.concatenate(picks, axis=0), power)
        i0, i1 = iota((N, N), 0), iota((N, N), 1)
        blocks = [[jnp.zeros((OWN, N), F32) for _ in range(2)] for _ in range(2)]
        for index, (ref, j) in enumerate(spots_of):
            _, column = place(ref, b, j)
            pick = (((i1 - column) & (N - 1)) == i0).astype(F32).astype(BF16)
            high, low = halves(taken[OWN * index : OWN * (index + 1)])
            moved = dot(
                jnp.concatenate([high, low], axis=1), jnp.concatenate([pick, pick], axis=0)
            )
            kind = index // 2
            for block, here in ((0, kind == 0), (1, kind == 2)):
                if (block, kind) in ((0, 2), (1, 1)):
                    continue
                for side_index, mask in enumerate(sides(ref, b, j, here)):
                    blocks[block][side_index] = blocks[block][side_index] + jnp.where(
                        mask, moved, 0.0
                    )
        for block in range(2 if with_halo else 1):
            com.illum[block, :, :N] = blocks[block][0]
            com.illum[block, :, N:] = blocks[block][1]

    def update_block(b, field, field_rows, new, block, steps):
        for part in range(2):
            for side_index, columns in ((0, slice(0, N)), (1, slice(N, WIDTH))):
                total = jnp.zeros((OWN, N), F32)
                for step, j, ref, here in steps:
                    total = total + jnp.where(sides(ref, b, j, here)[side_index], step[j, part], 0.0)
                new[part, :, columns] = field[part, field_rows, columns] + total / (
                    com.illum[block, :, columns] + 1.0
                )

    def refine():
        spot = pl.ds(pl.multiple_of(16 * m, 16), 16)
        far_spot = pl.ds(pl.multiple_of(HALF + 16 * m, 16), 16)
        edge_copies = [
            send(obj.at[:, spot], com.edge_plus, lax.rem(t + 31, 32), m),
            send(obj.at[:, far_spot], com.edge_minus, lax.rem(t + 1, 32), m),
        ]
        probe_copy = send(
            mem[0].probes.at[0, pl.ds(0, 2)], mem[0].probes.at[1, pl.ds(0, 2)], t, sibling
        )
        where_copies = [
            send(com.where_own, com.where_minus, t_plus, m),
            send(com.where_own, com.where_plus, t_minus, m),
        ]
        halo_copy = send(obj.at[:, pl.ds(own_row, OWN)], mem[0].halo, t_minus, m)
        arrived(edge_copies)
        patch_copies = send_edges()
        arrived([probe_copy])
        roll_probes(0)
        power_copies = send_power(
            0, [(probe[0, 0, held[part]], probe[0, 1, held[part]]) for part in range(2)]
        )
        arrived(where_copies)
        for load in loads:
            load.wait()
        for b in range(BATCHES):
            last = b == BATCHES - 1
            if b == 0:
                field, field_rows = obj, pl.ds(own_row, OWN)
            else:
                field, field_rows = mem[b - 1].objnew, slice(0, OWN)
            arrived(patch_copies)
            if b == 0:
                join_edges()
            if b:
                arrived([probe_copy])
                roll_probes(b)
            copies = forward(b)
            sum_power(b, power_copies)
            power_gather = Gather(lambda rows: mem[b].probes.at[0, 2, rows])
            power_gather.start_one()
            patch, cover = mem[b].patch, mem[b].cov
            cover[0] = unrolled_one(patch[0] * patch[0] + patch[1] * patch[1], b)
            cover_copy = send(cover, mem[b].csib, t, sibling)
            arrived([cover_copy])
            mem[b].cover_sum.full[...] = cover[...] + mem[b].csib[...]
            cover_sum = Reduce(mem[b].cover_sum)
            cover_sum.start_one()
            inten, irecv, factor = mem[b].inten, mem[b].irecv, mem[b].factor
            arrived(copies)
            own_rows = pl.ds(i_row, 64)
            total = inten[own_rows, :] + irecv[0] + irecv[1] + irecv[2]
            factor[own_rows, :] = (
                jnp.sqrt((observed[b, own_rows, :] + 1.0) / (total + 1.0)) - 1.0
            )
            copies = []
            for k in range(1, 4):
                other = lax.rem(z + k, 4)
                copies.append(send(factor.at[own_rows], factor.at[own_rows], t, 2 * other + c))
            power_gather.start_two()
            cover_sum.start_two()
            copies = inverse(b, copies, cover_sum.start_pair)
            grad, grecv, dstep = mem[b].grad, mem[b].grecv, mem[b].dstep
            unroll_step(b, 1)
            step_copy = send(dstep.at[1], mem[b].dsib, t, sibling)
            unroll_step(b, 0)
            power_gather.finish()
            arrived([step_copy])
            mem[b].probe_sum.full[...] = dstep[0] + mem[b].dsib[...]
            probe_sum = Reduce(mem[b].probe_sum)
            probe_sum.start_one()
            illumination(b, not last)
            probe_sum.start_two()
            arrived(copies)
            own, minus, plus = mem[b].gown, mem[b].gminus, mem[b].gplus
            own[0] = grad[:, pl.ds(own_row, OWN)] + grecv[1] + grecv[3] + grecv[5]
            own[1] = grecv[0] + grecv[2] + grecv[4] + grecv[6]
            copies = [send(own, minus, t_plus, m)]
            if not last:
                copies.append(send(own, plus, t_minus, m))
            probe_sum.start_pair()
            if b == 0:
                arrived([halo_copy])
            arrived(copies)
            own_steps = [(own, j, com.where_own, True) for j in range(2)]
            own_steps += [(minus, j, com.where_minus, False) for j in range(2)]
            new = mem[b].objnew
            update_block(b, field, field_rows, new, 0, own_steps)
            if last:
                rows = pl.ds(own_row, OWN)
                final_copies = []
                for k in range(1, 4):
                    other = 2 * lax.rem(z + k, 4) + c
                    final_copies.append(send(new, out_obj.at[:, rows], t, other))
                sibling_copies = [send(new, out_obj.at[:, rows], t, sibling)]
                out_obj[:, rows] = new[...]
            else:
                halo_steps = [(plus, j, com.where_plus, True) for j in range(2)]
                halo_steps += [(own, j, com.where_own, False) for j in range(2)]
                halo = mem[b + 1].halo
                update_block(b, mem[b].halo, slice(0, OWN), halo, 1, halo_steps)
                patch_copies = send_patches(b + 1, new, halo)
            coverage = cover_sum.finish()
            step = probe_sum.finish()
            probes = mem[b].probes
            following = out_probe if last else mem[b + 1].probes
            values = []
            for half in range(2):
                values.append(
                    [
                        probes[0, part, held[half], :]
                        + step[half][part] / (coverage[half][0] + 1.0)
                        for part in range(2)
                    ]
                )
                for part in range(2):
                    following[0, part, held[half], :] = values[half][part]
            gather = Gather(lambda rows: following.at[0, pl.ds(0, 2), rows])
            gather.start_one()
            gather.start_two()
            if last:
                for k in range(1, 4):
                    arrived(final_copies[k - 1 : k])
                    other = 2 * lax.rem(z - k + 4, 4) + c
                    rows = pl.ds(pl.multiple_of(OWN * other, OWN), OWN)
                    part = out_obj.at[:, rows]
                    sibling_copies.append(send(part, part, t, sibling))
                gather.finish()
                arrived(sibling_copies)
            else:
                power_copies = send_power(b + 1, values)
                gather.finish()
                probe_copy = send(
                    following.at[0, pl.ds(0, 2)], following.at[1, pl.ds(0, 2)], t, sibling
                )

    refine()
    for copy in sent:
        copy.wait_send()


def shards(object_field, probe, positions, measured):
    right, left = split_tables()
    plan = scratch_plan()
    leaves, tree = jax.tree.flatten(plan)

    def body(*refs):
        kernel(tree, *refs)

    vmem = pl.BlockSpec(memory_space=pltpu.VMEM)
    anywhere = pl.BlockSpec(memory_space=pl.ANY)
    return pl.pallas_call(
        body,
        name="refine",
        out_shape=(
            jax.ShapeDtypeStruct(object_field.shape, F32),
            jax.ShapeDtypeStruct(probe.shape, F32),
        ),
        in_specs=[pl.BlockSpec(memory_space=pltpu.SMEM)] + [vmem] * 2 + [anywhere] * 3,
        out_specs=(vmem, vmem),
        scratch_shapes=leaves
        + [pltpu.SemaphoreType.DMA((count,)) for count in (COPIES, COPIES, 4)],
        compiler_params=pltpu.CompilerParams(
            collective_id=0, has_side_effects=True, vmem_limit_bytes=30 * 1024 * 1024
        ),
    )(positions, object_field, probe, measured, jnp.asarray(right), jnp.asarray(left))


def solution(mesh):
    in_specs = (
        P(None, "tile", None),
        P("mode", None, None, None),
        P(None, "tile", None),
        P(None, "tile", None, None),
    )
    out_specs = (P(None, "tile", None), P("mode", None, None, None))
    return jax.shard_map(shards, mesh=mesh, in_specs=in_specs, out_specs=out_specs, check_vma=False)
```

```python
import math

import jax
import jax.numpy as jnp
import ml_dtypes
import numpy as np
from jax import lax
from jax.experimental import pallas as pl
from jax.experimental.pallas import tpu as pltpu
from jax.sharding import PartitionSpec as P

N = 256
HALF = 128
WIDTH = 512
OWN = 32
BATCHES = 2
F32 = jnp.float32
BF16 = jnp.bfloat16
MESH = pl.DeviceIdType.MESH


def split_tables():
    index = np.arange(N)
    angle = (np.outer(index, index) % N) * (2.0 * math.pi / N)
    cosine = np.cos(angle) / math.sqrt(N)
    sine = np.sin(angle) / math.sqrt(N)
    bf16 = ml_dtypes.bfloat16

    def parts(table):
        high = table.astype(np.float32).astype(bf16)
        low = (table - high.astype(np.float64)).astype(np.float32).astype(bf16)
        return high, low

    ch, cl = parts(cosine)
    sh, sl = parts(sine)
    high = np.concatenate([ch, sh], axis=1)
    low = np.concatenate([cl, sl], axis=1)
    right = np.concatenate([high, low, high], axis=0)
    left = np.concatenate(
        [np.concatenate([ch, ch, cl], axis=1), np.concatenate([sh, sh, sl], axis=1)], axis=0
    )
    left = left.reshape(2, 4, 64, 3 * N).transpose(1, 0, 2, 3).reshape(4, 128, 3 * N)
    return right, left


def halves(value):
    high = value.astype(BF16)
    low = (value - high.astype(F32)).astype(BF16)
    return high, low


def dot(a, b):
    return jnp.dot(a, b, preferred_element_type=F32)


def iota(shape, dim):
    return lax.broadcasted_iota(jnp.int32, shape, dim)


def reduce_plan(parts):
    return dict(
        full=pltpu.VMEM((parts, N, N), F32),
        one=pltpu.VMEM((2, 3, parts, 32, N), F32),
        onesum=pltpu.VMEM((2, parts, 32, N), F32),
        two=pltpu.VMEM((2, 3, parts, 8, N), F32),
        twosum=pltpu.VMEM((2, parts, 8, N), F32),
        pair=pltpu.VMEM((2, parts, 8, N), F32),
    )


def batch_plan():
    return dict(
        halo=pltpu.VMEM((2, OWN, WIDTH), F32),
        patch=pltpu.VMEM((2, N, N), F32),
        pout=pltpu.VMEM((2, 2, OWN, N), F32),
        probes=pltpu.VMEM((2, 3, N, N), F32),
        power=pltpu.VMEM((8, 2, 8, N), F32),
        inten=pltpu.VMEM((N, N), F32),
        irecv=pltpu.VMEM((3, 64, N), F32),
        factor=pltpu.VMEM((N, N), F32),
        grad=pltpu.VMEM((2, N, N), F32),
        grecv=pltpu.VMEM((7, 2, OWN, N), F32),
        gown=pltpu.VMEM((2, 2, OWN, N), F32),
        gminus=pltpu.VMEM((2, 2, OWN, N), F32),
        gplus=pltpu.VMEM((2, 2, OWN, N), F32),
        objnew=pltpu.VMEM((2, OWN, WIDTH), F32),
        dstep=pltpu.VMEM((2, 2, N, N), F32),
        dsib=pltpu.VMEM((2, N, N), F32),
        cov=pltpu.VMEM((1, N, N), F32),
        csib=pltpu.VMEM((1, N, N), F32),
        probe_sum=reduce_plan(2),
        cover_sum=reduce_plan(1),
    )


def scratch_plan():
    common = dict(
        edge_plus=pltpu.VMEM((2, 16, WIDTH), F32),
        edge_minus=pltpu.VMEM((2, 16, WIDTH), F32),
        edge_out=pltpu.VMEM((2, 2, 16, N), F32),
        edge_rows=pltpu.VMEM((2, HALF, N), F32),
        observed=pltpu.VMEM((2, N, N), F32),
        rtable=pltpu.VMEM((3 * N, 2 * N), BF16),
        ltable=pltpu.VMEM((4, 128, 3 * N), BF16),
        where_own=pltpu.VMEM((8, N), jnp.int32),
        where_minus=pltpu.VMEM((8, N), jnp.int32),
        where_plus=pltpu.VMEM((8, N), jnp.int32),
        rolled=pltpu.VMEM((2, 2, N, N), F32),
        far=pltpu.VMEM((2, 2, N, N), F32),
        stage=pltpu.VMEM((2, 3 * N, 2 * N), BF16),
        illum=pltpu.VMEM((2, OWN, WIDTH), F32),
    )
    return [common] + [batch_plan() for _ in range(BATCHES)]


class Box:
    def __init__(self, entries):
        for name, entry in entries.items():
            setattr(self, name, Box(entry) if isinstance(entry, dict) else entry)


COPIES = 248


def kernel(tree, pos, obj, probe, measured, rtable, ltable, out_obj, out_probe, *scratch):
    ssem, rsem, lsem = scratch[-3:]
    com, *mem = [Box(entries) for entries in jax.tree.unflatten(tree, scratch[:-3])]
    t = lax.axis_index("tile")
    m = lax.axis_index("mode")
    x, zh, y = t // 8, (t // 4) % 2, t % 4
    z, c = m // 2, m % 2
    sibling = m + 1 - 2 * c
    side = 1 - 2 * (m // 4)
    t_plus = lax.rem(t + side + 32, 32)
    t_minus = lax.rem(t - side + 32, 32)
    t_pair = t + 4 - 8 * zh
    own_row = pl.multiple_of(OWN * m, OWN)
    i_row = pl.multiple_of(64 * z, 64)
    sent = []

    def send(src, dst, tile, mode):
        index = len(sent)
        copy = pltpu.make_async_remote_copy(
            src_ref=src,
            dst_ref=dst,
            send_sem=ssem.at[index],
            recv_sem=rsem.at[index],
            device_id=(tile, mode),
            device_id_type=MESH,
        )
        copy.start()
        sent.append(copy)
        return copy

    def arrived(copies):
        for copy in copies:
            copy.wait_recv()

    def y_tile(k):
        other = lax.rem(y + k, 4)
        return other, t - y + other

    def x_tile(k):
        other = lax.rem(x + k, 4)
        return other, t - 8 * x + 8 * other

    barrier = pltpu.get_barrier_semaphore()
    rw, lw, observed = com.rtable, com.ltable, com.observed
    loads = [
        pltpu.make_async_copy(rtable, rw, lsem.at[0]),
        pltpu.make_async_copy(ltable, lw, lsem.at[1]),
        pltpu.make_async_copy(measured.at[0, c], observed.at[0], lsem.at[2]),
        pltpu.make_async_copy(measured.at[1, c], observed.at[1], lsem.at[3]),
    ]
    partners = [(t, lax.rem(m + k, 8)) for k in range(1, 8)]
    partners += [(y_tile(k)[1], m) for k in range(1, 4)]
    partners += [(x_tile(k)[1], m) for k in range(1, 4)]
    partners += [(t_pair, m), (t_plus, m), (t_minus, m)]
    for partner in partners:
        pl.semaphore_signal(barrier, inc=1, device_id=partner, device_id_type=MESH)
    for load in loads:
        load.start()

    for b in range(BATCHES):
        for j in range(2):
            core = c if j == 0 else 1 - c
            row = pos[b, core, 0] - N * t
            column = pos[b, core, 1]
            com.where_own[4 * b + 2 * j : 4 * b + 2 * j + 1, :] = jnp.full((1, N), row, jnp.int32)
            com.where_own[4 * b + 2 * j + 1 : 4 * b + 2 * j + 2, :] = jnp.full(
                (1, N), column, jnp.int32
            )
    for part in range(2):
        mem[0].probes[0, part] = probe[0, part]
    pl.semaphore_wait(barrier, len(partners))

    def place(ref, b, j):
        return ref[4 * b + 2 * j : 4 * b + 2 * j + 1, :], ref[4 * b + 2 * j + 1 : 4 * b + 2 * j + 2, :]

    def whole(part, other):
        return pl.ds(pl.multiple_of(HALF * part + 32 * other, 32), 32)

    def piece(other):
        return pl.ds(pl.multiple_of(8 * other, 8), 8)

    lines = ((y_tile, x_tile), (x_tile, y_tile))
    spots = ((y, x), (x, y))
    held = [
        pl.ds(pl.multiple_of(HALF * part + 32 * spots[part][0] + 8 * spots[part][1], 8), 8)
        for part in range(2)
    ]

    class Reduce:
        def __init__(self, box):
            self.full, self.one, self.onesum = box.full, box.one, box.onesum
            self.two, self.twosum, self.pair = box.two, box.twosum, box.pair

        def start_one(self):
            self.copies = [[], []]
            for k in range(1, 4):
                for part in range(2):
                    other, tile = lines[part][0](k)
                    self.copies[part].append(
                        send(self.full.at[:, whole(part, other)], self.one.at[part, k - 1], tile, m)
                    )

        def start_two(self):
            after = [[], []]
            for part in range(2):
                arrived(self.copies[part])
                self.onesum[part] = (
                    self.full[:, whole(part, spots[part][0])]
                    + self.one[part, 0]
                    + self.one[part, 1]
                    + self.one[part, 2]
                )
                for k in range(1, 4):
                    other, tile = lines[part][1](k)
                    after[part].append(
                        send(
                            self.onesum.at[part, :, piece(other)], self.two.at[part, k - 1], tile, m
                        )
                    )
            self.copies = after

        def start_pair(self):
            for part in range(2):
                arrived(self.copies[part])
                self.twosum[part] = (
                    self.onesum[part, :, piece(spots[part][1])]
                    + self.two[part, 0]
                    + self.two[part, 1]
                    + self.two[part, 2]
                )
            self.copies = [send(self.twosum, self.pair, t_pair, m)]

        def finish(self):
            arrived(self.copies)
            return [self.twosum[part] + self.pair[part] for part in range(2)]

    class Gather:
        def __init__(self, view):
            self.view = view

        def start_one(self):
            self.copies = [[], []]
            for k in range(1, 4):
                for part in range(2):
                    rows = self.view(held[part])
                    self.copies[part].append(send(rows, rows, lines[part][1](k)[1], m))

        def start_two(self):
            after = [[], []]
            for part in range(2):
                arrived(self.copies[part])
                rows = self.view(whole(part, spots[part][0]))
                for k in range(1, 4):
                    after[part].append(send(rows, rows, lines[part][0](k)[1], m))
            self.copies = after

        def finish(self):
            for part in range(2):
                arrived(self.copies[part])

    def send_power(b, values):
        power = mem[b].power
        for part, (real, imag) in enumerate(values):
            power[0, part] = real * real + imag * imag
        return [send(power.at[0], power.at[k], t, lax.rem(m + k, 8)) for k in range(1, 8)]

    def sum_power(b, copies):
        arrived(copies)
        power = mem[b].power
        total = power[0]
        for k in range(1, 8):
            total = total + power[k]
        for part in range(2):
            mem[b].probes[0, 2, held[part], :] = total[part]

    def send_edges():
        plus, minus, out, rows = com.edge_plus, com.edge_minus, com.edge_out, com.edge_rows
        columns = iota((16, N), 1)
        spot = pl.ds(pl.multiple_of(16 * m, 16), 16)
        for j in range(2):
            row, column = place(com.where_own, 0, j)
            ahead = jnp.broadcast_to(row, (16, N)) >= 0
            first = columns >= column
            for part in range(2):
                low = jnp.where(ahead, plus[part, :, :N], minus[part, :, :N])
                high = jnp.where(ahead, plus[part, :, N:], minus[part, :, N:])
                out[j, part] = jnp.where(first, low, high)
        copies = [
            send(out.at[k % 2], rows.at[:, spot], t, lax.rem(m + k, 8)) for k in range(1, 8)
        ]
        rows[:, spot] = out[0]
        return copies

    def join_edges():
        rows, patch = com.edge_rows, mem[0].patch
        row, column = place(com.where_own, 0, 0)
        columns = iota((HALF, N), 1)
        first = columns >= column
        for half in range(2):
            span = slice(HALF * half, HALF * (half + 1))
            ahead = HALF * half + iota((HALF, N), 0) - row
            inside = (ahead >= 0) & (ahead < N)
            for part in range(2):
                own = jnp.where(first, obj[part, span, :N], obj[part, span, N:])
                patch[part, span, :] = jnp.where(inside, own, rows[part])

    def send_patches(b, field, halo, part):
        out, patch = mem[b].pout, mem[b].patch
        rows = own_row + iota((OWN, N), 0)
        columns = iota((OWN, N), 1)
        for j in range(2):
            row, column = place(com.where_own, b, j)
            ahead = rows - row
            inside = (ahead >= 0) & (ahead < N)
            first = columns >= column
            low = jnp.where(inside, field[part, :, :N], halo[part, :, :N])
            high = jnp.where(inside, field[part, :, N:], halo[part, :, N:])
            out[j, part] = jnp.where(first, low, high)
        copies = []
        spot = patch.at[part, pl.ds(own_row, OWN)]
        for k in range(1, 8):
            copies.append(send(out.at[k % 2, part], spot, t, lax.rem(m + k, 8)))
        patch[part, pl.ds(own_row, OWN)] = out[0, part]
        return copies

    def shifted(real, imag, row, column):
        i0, i1 = iota((N, N), 0), iota((N, N), 1)
        pick = (((i0 + row) & (N - 1)) == i1).astype(F32).astype(BF16)
        both = real if imag is None else jnp.concatenate([real, imag], axis=1)
        high, low = halves(both)
        moved = dot(jnp.concatenate([pick, pick], axis=1), jnp.concatenate([high, low], axis=0))
        pick = (((i1 + column) & (N - 1)) == i0).astype(F32).astype(BF16)
        if imag is not None:
            moved = jnp.concatenate([moved[:, :N], moved[:, N:]], axis=0)
        high, low = halves(moved)
        moved = dot(jnp.concatenate([high, low], axis=1), jnp.concatenate([pick, pick], axis=0))
        return moved[:N], moved[N:]

    def roll_probes(b):
        row, column = place(com.where_own, b, 0)
        probes = mem[b].probes
        for mode in range(2):
            rolled[mode, 0], rolled[mode, 1] = shifted(
                probes[mode, 0], probes[mode, 1], -row, -column
            )

    def unroll_step(b, mode):
        row, column = place(com.where_own, b, 0)
        dstep = mem[b].dstep
        dstep[mode, 0], dstep[mode, 1] = shifted(dstep[mode, 0], dstep[mode, 1], row, column)

    def unrolled_one(field, b):
        row, column = place(com.where_own, b, 0)
        return shifted(field, None, row, column)[0]

    def chunk_rows(q):
        return pl.ds(pl.multiple_of(q * 64, 64), 64)

    stage = com.stage

    def right_stage(mode, q, real, imag, sign):
        high, low = halves(jnp.concatenate([real, imag], axis=0))
        product = dot(jnp.concatenate([high, high, low], axis=1), rw[...])
        out_real = product[:64, :N] + sign * product[64:, N:]
        out_imag = product[64:, :N] - sign * product[:64, N:]
        high, low = halves(jnp.concatenate([out_real, out_imag], axis=1))
        stage[mode, pl.ds(pl.multiple_of(q * 64, 64), 64), :] = high
        stage[mode, pl.ds(pl.multiple_of(N + q * 64, 64), 64), :] = low
        stage[mode, pl.ds(pl.multiple_of(2 * N + q * 64, 64), 64), :] = high

    def left_stage(mode, q, sign):
        product = dot(lw[q], stage[mode])
        return (
            product[:64, :N] + sign * product[64:, N:],
            product[:64, N:] - sign * product[64:, :N],
        )

    far, rolled = com.far, com.rolled

    def forward(b):
        ofield, inten = mem[b].patch, mem[b].inten

        def first(q, carry):
            rows = chunk_rows(q)
            o_real, o_imag = ofield[0, rows, :], ofield[1, rows, :]
            for mode in range(2):
                p_real, p_imag = rolled[mode, 0, rows, :], rolled[mode, 1, rows, :]
                right_stage(
                    mode,
                    q,
                    p_real * o_real - p_imag * o_imag,
                    p_real * o_imag + p_imag * o_real,
                    1.0,
                )
            return carry

        lax.fori_loop(0, 4, first, 0)

        irecv, copies = mem[b].irecv, []
        for k in (1, 2, 3, 0):
            q = lax.rem(z + k, 4)
            rows = chunk_rows(q)
            total = None
            for mode in range(2):
                f_real, f_imag = left_stage(mode, q, 1.0)
                far[mode, 0, rows, :] = f_real
                far[mode, 1, rows, :] = f_imag
                power = f_real * f_real + f_imag * f_imag
                total = power if total is None else total + power
            inten[rows, :] = total
            if k:
                copies.append(send(inten.at[rows], irecv.at[k - 1], t, 2 * q + c))
        return copies

    def inverse(b, copies, between):
        ofield, factor = mem[b].patch, mem[b].factor
        grad, dstep, grecv = mem[b].grad, mem[b].dstep, mem[b].grecv

        for k in range(4):
            if k:
                arrived(copies[k - 1 : k])
            q = lax.rem(z - k + 4, 4)
            rows = chunk_rows(q)
            scale = factor[rows, :]
            for mode in range(2):
                right_stage(mode, q, scale * far[mode, 0, rows, :], scale * far[mode, 1, rows, :], -1.0)
        between()

        sends, later = [], []
        for k in (2, 1, 3, 0):
            q = lax.rem(z + k, 4)
            rows = chunk_rows(q)
            o_real, o_imag = ofield[0, rows, :], ofield[1, rows, :]
            g_real = jnp.zeros((64, N), F32)
            g_imag = jnp.zeros((64, N), F32)
            for mode in range(2):
                c_real, c_imag = left_stage(mode, q, -1.0)
                p_real, p_imag = rolled[mode, 0, rows, :], rolled[mode, 1, rows, :]
                g_real = g_real + p_real * c_real + p_imag * c_imag
                g_imag = g_imag + p_real * c_imag - p_imag * c_real
                dstep[mode, 0, rows, :] = o_real * c_real + o_imag * c_imag
                dstep[mode, 1, rows, :] = o_real * c_imag - o_imag * c_real
            grad[0, rows, :] = g_real
            grad[1, rows, :] = g_imag
            for twin in range(2):
                if k == 0 and twin == 0:
                    continue
                core = c if twin == 0 else 1 - c
                part = pl.ds(pl.multiple_of(OWN * (2 * q + core), OWN), OWN)
                slot = 2 * k + twin - 1
                sends.append(send(grad.at[0, part], grecv.at[slot, 0], t, 2 * q + core))
                later.append((grad.at[1, part], grecv.at[slot, 1], t, 2 * q + core))
        return [sends, [send(*args) for args in later]]

    def masks(ref, b, j):
        rows = own_row + iota((OWN, N), 0)
        row, column = place(ref, b, j)
        ahead = rows - row
        inside = (ahead >= 0) & (ahead < N)
        first = iota((OWN, N), 1) >= column
        return inside, first

    def sides(ref, b, j, here):
        inside, first = masks(ref, b, j)
        if not here:
            inside = jnp.logical_not(inside)
        return inside & first, inside & jnp.logical_not(first)

    def illumination(b, with_halo):
        high, low = halves(mem[b].probes[0, 2])
        power = jnp.concatenate([high, low], axis=0)
        rows = own_row + iota((OWN, N), 0)
        lanes = iota((OWN, N), 1)
        refs = [com.where_own, com.where_minus] + ([com.where_plus] if with_halo else [])
        spots_of = [(ref, j) for ref in refs for j in range(2)]
        picks = []
        for ref, j in spots_of:
            row, _ = place(ref, b, j)
            pick = (((rows - row) & (N - 1)) == lanes).astype(F32).astype(BF16)
            picks.append(jnp.concatenate([pick, pick], axis=1))
        taken = dot(jnp.concatenate(picks, axis=0), power)
        i0, i1 = iota((N, N), 0), iota((N, N), 1)
        blocks = [[jnp.zeros((OWN, N), F32) for _ in range(2)] for _ in range(2)]
        for index, (ref, j) in enumerate(spots_of):
            _, column = place(ref, b, j)
            pick = (((i1 - column) & (N - 1)) == i0).astype(F32).astype(BF16)
            high, low = halves(taken[OWN * index : OWN * (index + 1)])
            moved = dot(
                jnp.concatenate([high, low], axis=1), jnp.concatenate([pick, pick], axis=0)
            )
            kind = index // 2
            for block, here in ((0, kind == 0), (1, kind == 2)):
                if (block, kind) in ((0, 2), (1, 1)):
                    continue
                for side_index, mask in enumerate(sides(ref, b, j, here)):
                    blocks[block][side_index] = blocks[block][side_index] + jnp.where(
                        mask, moved, 0.0
                    )
        for block in range(2 if with_halo else 1):
            com.illum[block, :, :N] = blocks[block][0]
            com.illum[block, :, N:] = blocks[block][1]

    def update_block(b, part, field, field_rows, new, block, steps):
        for side_index, columns in ((0, slice(0, N)), (1, slice(N, WIDTH))):
            total = jnp.zeros((OWN, N), F32)
            for step, j, ref, here in steps:
                total = total + jnp.where(sides(ref, b, j, here)[side_index], step[j, part], 0.0)
            new[part, :, columns] = field[part, field_rows, columns] + total / (
                com.illum[block, :, columns] + 1.0
            )

    def refine():
        spot = pl.ds(pl.multiple_of(16 * m, 16), 16)
        far_spot = pl.ds(pl.multiple_of(HALF + 16 * m, 16), 16)
        edge_copies = [
            send(obj.at[:, spot], com.edge_plus, lax.rem(t + 31, 32), m),
            send(obj.at[:, far_spot], com.edge_minus, lax.rem(t + 1, 32), m),
        ]
        probe_copy = send(
            mem[0].probes.at[0, pl.ds(0, 2)], mem[0].probes.at[1, pl.ds(0, 2)], t, sibling
        )
        where_copies = [
            send(com.where_own, com.where_minus, t_plus, m),
            send(com.where_own, com.where_plus, t_minus, m),
        ]
        halo_copy = send(obj.at[:, pl.ds(own_row, OWN)], mem[0].halo, t_minus, m)
        arrived(edge_copies)
        patch_copies = send_edges()
        arrived([probe_copy])
        roll_probes(0)
        power_copies = send_power(
            0, [(probe[0, 0, held[part]], probe[0, 1, held[part]]) for part in range(2)]
        )
        arrived(where_copies)
        for load in loads:
            load.wait()
        for b in range(BATCHES):
            last = b == BATCHES - 1
            if b == 0:
                field, field_rows = obj, pl.ds(own_row, OWN)
            else:
                field, field_rows = mem[b - 1].objnew, slice(0, OWN)
            arrived(patch_copies)
            if b == 0:
                join_edges()
            if b:
                arrived([probe_copy])
                roll_probes(b)
            copies = forward(b)
            sum_power(b, power_copies)
            power_gather = Gather(lambda rows: mem[b].probes.at[0, 2, rows])
            power_gather.start_one()
            patch, cover = mem[b].patch, mem[b].cov
            cover[0] = unrolled_one(patch[0] * patch[0] + patch[1] * patch[1], b)
            cover_copy = send(cover, mem[b].csib, t, sibling)
            arrived([cover_copy])
            mem[b].cover_sum.full[...] = cover[...] + mem[b].csib[...]
            cover_sum = Reduce(mem[b].cover_sum)
            cover_sum.start_one()
            inten, irecv, factor = mem[b].inten, mem[b].irecv, mem[b].factor
            arrived(copies)
            own_rows = pl.ds(i_row, 64)
            total = inten[own_rows, :] + irecv[0] + irecv[1] + irecv[2]
            factor[own_rows, :] = (
                jnp.sqrt((observed[b, own_rows, :] + 1.0) / (total + 1.0)) - 1.0
            )
            copies = []
            for k in range(1, 4):
                other = lax.rem(z + k, 4)
                copies.append(send(factor.at[own_rows], factor.at[own_rows], t, 2 * other + c))
            power_gather.start_two()
            cover_sum.start_two()
            copies = inverse(b, copies, cover_sum.start_pair)
            grad, grecv, dstep = mem[b].grad, mem[b].grecv, mem[b].dstep
            unroll_step(b, 1)
            step_copy = send(dstep.at[1], mem[b].dsib, t, sibling)
            unroll_step(b, 0)
            power_gather.finish()
            arrived([step_copy])
            mem[b].probe_sum.full[...] = dstep[0] + mem[b].dsib[...]
            probe_sum = Reduce(mem[b].probe_sum)
            probe_sum.start_one()
            illumination(b, not last)
            own, minus, plus = mem[b].gown, mem[b].gminus, mem[b].gplus
            near = []
            for part in range(2):
                arrived(copies[part])
                here = grad[part, pl.ds(own_row, OWN)]
                own[0, part] = here + grecv[1, part] + grecv[3, part] + grecv[5, part]
                own[1, part] = (
                    grecv[0, part] + grecv[2, part] + grecv[4, part] + grecv[6, part]
                )
                near.append([send(own.at[:, part], minus.at[:, part], t_plus, m)])
                if not last:
                    near[part].append(send(own.at[:, part], plus.at[:, part], t_minus, m))
                if part == 0:
                    probe_sum.start_two()
            probe_sum.start_pair()
            if b == 0:
                arrived([halo_copy])
            own_steps = [(own, j, com.where_own, True) for j in range(2)]
            own_steps += [(minus, j, com.where_minus, False) for j in range(2)]
            halo_steps = [(plus, j, com.where_plus, True) for j in range(2)]
            halo_steps += [(own, j, com.where_own, False) for j in range(2)]
            new = mem[b].objnew
            final_copies, sibling_copies, patch_copies = [], [], []
            for part in range(2):
                arrived(near[part])
                update_block(b, part, field, field_rows, new, 0, own_steps)
                if last:
                    rows = pl.ds(own_row, OWN)
                    spot = out_obj.at[part, rows]
                    final_copies.append(
                        [
                            send(new.at[part], spot, t, 2 * lax.rem(z + k, 4) + c)
                            for k in range(1, 4)
                        ]
                    )
                    sibling_copies.append(send(new.at[part], spot, t, sibling))
                    out_obj[part, rows] = new[part]
                else:
                    halo = mem[b + 1].halo
                    update_block(b, part, mem[b].halo, slice(0, OWN), halo, 1, halo_steps)
                    patch_copies += send_patches(b + 1, new, halo, part)
            coverage = cover_sum.finish()
            step = probe_sum.finish()
            probes = mem[b].probes
            following = out_probe if last else mem[b + 1].probes
            values = []
            for half in range(2):
                values.append(
                    [
                        probes[0, part, held[half], :]
                        + step[half][part] / (coverage[half][0] + 1.0)
                        for part in range(2)
                    ]
                )
                for part in range(2):
                    following[0, part, held[half], :] = values[half][part]
            gather = Gather(lambda rows: following.at[0, pl.ds(0, 2), rows])
            gather.start_one()
            gather.start_two()
            if last:
                for part in range(2):
                    for k in range(1, 4):
                        arrived(final_copies[part][k - 1 : k])
                        other = 2 * lax.rem(z - k + 4, 4) + c
                        rows = pl.ds(pl.multiple_of(OWN * other, OWN), OWN)
                        spot = out_obj.at[part, rows]
                        sibling_copies.append(send(spot, spot, t, sibling))
                gather.finish()
                arrived(sibling_copies)
            else:
                power_copies = send_power(b + 1, values)
                gather.finish()
                probe_copy = send(
                    following.at[0, pl.ds(0, 2)], following.at[1, pl.ds(0, 2)], t, sibling
                )

    refine()
    for copy in sent:
        copy.wait_send()


def shards(object_field, probe, positions, measured):
    right, left = split_tables()
    plan = scratch_plan()
    leaves, tree = jax.tree.flatten(plan)

    def body(*refs):
        kernel(tree, *refs)

    vmem = pl.BlockSpec(memory_space=pltpu.VMEM)
    anywhere = pl.BlockSpec(memory_space=pl.ANY)
    return pl.pallas_call(
        body,
        name="refine",
        out_shape=(
            jax.ShapeDtypeStruct(object_field.shape, F32),
            jax.ShapeDtypeStruct(probe.shape, F32),
        ),
        in_specs=[pl.BlockSpec(memory_space=pltpu.SMEM)] + [vmem] * 2 + [anywhere] * 3,
        out_specs=(vmem, vmem),
        scratch_shapes=leaves
        + [pltpu.SemaphoreType.DMA((count,)) for count in (COPIES, COPIES, 4)],
        compiler_params=pltpu.CompilerParams(
            collective_id=0, has_side_effects=True, vmem_limit_bytes=30 * 1024 * 1024
        ),
    )(positions, object_field, probe, measured, jnp.asarray(right), jnp.asarray(left))


def solution(mesh):
    in_specs = (
        P(None, "tile", None),
        P("mode", None, None, None),
        P(None, "tile", None),
        P(None, "tile", None, None),
    )
    out_specs = (P(None, "tile", None), P("mode", None, None, None))
    return jax.shard_map(shards, mesh=mesh, in_specs=in_specs, out_specs=out_specs, check_vma=False)
```

```python
import math

import jax
import jax.numpy as jnp
import ml_dtypes
import numpy as np
from jax import lax
from jax.experimental import pallas as pl
from jax.experimental.pallas import tpu as pltpu
from jax.sharding import PartitionSpec as P

N = 256
HALF = 128
WIDTH = 512
OWN = 32
BATCHES = 2
F32 = jnp.float32
BF16 = jnp.bfloat16
MESH = pl.DeviceIdType.MESH


def split_tables():
    index = np.arange(N)
    angle = (np.outer(index, index) % N) * (2.0 * math.pi / N)
    cosine = np.cos(angle) / math.sqrt(N)
    sine = np.sin(angle) / math.sqrt(N)
    bf16 = ml_dtypes.bfloat16

    def parts(table):
        high = table.astype(np.float32).astype(bf16)
        low = (table - high.astype(np.float64)).astype(np.float32).astype(bf16)
        return high, low

    ch, cl = parts(cosine)
    sh, sl = parts(sine)
    high = np.concatenate([ch, sh], axis=1)
    low = np.concatenate([cl, sl], axis=1)
    right = np.concatenate([high, low, high], axis=0)
    left = np.concatenate(
        [np.concatenate([ch, ch, cl], axis=1), np.concatenate([sh, sh, sl], axis=1)], axis=0
    )
    left = left.reshape(2, 4, 64, 3 * N).transpose(1, 0, 2, 3).reshape(4, 128, 3 * N)
    return right, left


def halves(value):
    high = value.astype(BF16)
    low = (value - high.astype(F32)).astype(BF16)
    return high, low


def dot(a, b):
    return jnp.dot(a, b, preferred_element_type=F32)


def iota(shape, dim):
    return lax.broadcasted_iota(jnp.int32, shape, dim)


def reduce_plan(parts):
    return dict(
        full=pltpu.VMEM((parts, N, N), F32),
        one=pltpu.VMEM((2, 3, parts, 32, N), F32),
        onesum=pltpu.VMEM((2, parts, 32, N), F32),
        two=pltpu.VMEM((2, 3, parts, 8, N), F32),
        twosum=pltpu.VMEM((2, parts, 8, N), F32),
        pair=pltpu.VMEM((2, parts, 8, N), F32),
    )


def batch_plan():
    return dict(
        halo=pltpu.VMEM((2, OWN, WIDTH), F32),
        patch=pltpu.VMEM((2, N, N), F32),
        pout=pltpu.VMEM((2, 2, OWN, N), F32),
        probes=pltpu.VMEM((2, 3, N, N), F32),
        power=pltpu.VMEM((8, 2, 8, N), F32),
        inten=pltpu.VMEM((N, N), F32),
        irecv=pltpu.VMEM((3, 64, N), F32),
        factor=pltpu.VMEM((N, N), F32),
        grad=pltpu.VMEM((2, N, N), F32),
        grecv=pltpu.VMEM((7, 2, OWN, N), F32),
        gown=pltpu.VMEM((2, 2, OWN, N), F32),
        gminus=pltpu.VMEM((2, 2, OWN, N), F32),
        gplus=pltpu.VMEM((2, 2, OWN, N), F32),
        objnew=pltpu.VMEM((2, OWN, WIDTH), F32),
        dstep=pltpu.VMEM((2, 2, N, N), F32),
        dsib=pltpu.VMEM((2, N, N), F32),
        cov=pltpu.VMEM((1, N, N), F32),
        csib=pltpu.VMEM((1, N, N), F32),
        probe_sum=reduce_plan(2),
        cover_sum=reduce_plan(1),
    )


def scratch_plan():
    common = dict(
        edge_plus=pltpu.VMEM((2, 16, WIDTH), F32),
        edge_minus=pltpu.VMEM((2, 16, WIDTH), F32),
        edge_out=pltpu.VMEM((2, 2, 16, N), F32),
        edge_rows=pltpu.VMEM((2, HALF, N), F32),
        observed=pltpu.VMEM((2, N, N), F32),
        rtable=pltpu.VMEM((3 * N, 2 * N), BF16),
        ltable=pltpu.VMEM((4, 128, 3 * N), BF16),
        where_own=pltpu.VMEM((8, N), jnp.int32),
        where_minus=pltpu.VMEM((8, N), jnp.int32),
        where_plus=pltpu.VMEM((8, N), jnp.int32),
        rolled=pltpu.VMEM((2, 2, N, N), F32),
        far=pltpu.VMEM((2, 2, N, N), F32),
        stage=pltpu.VMEM((2, 3 * N, 2 * N), BF16),
        illum=pltpu.VMEM((2, OWN, WIDTH), F32),
    )
    return [common] + [batch_plan() for _ in range(BATCHES)]


class Box:
    def __init__(self, entries):
        for name, entry in entries.items():
            setattr(self, name, Box(entry) if isinstance(entry, dict) else entry)


COPIES = 248
RELAYS = 12


def kernel(tree, pos, obj, probe, measured, rtable, ltable, out_obj, out_probe, *scratch):
    ssem, rsem, lsem, slots, relay_sem = scratch[-5:]
    com, *mem = [Box(entries) for entries in jax.tree.unflatten(tree, scratch[:-5])]
    t = lax.axis_index("tile")
    m = lax.axis_index("mode")
    x, zh, y = t // 8, (t // 4) % 2, t % 4
    z, c = m // 2, m % 2
    sibling = m + 1 - 2 * c
    side = 1 - 2 * (m // 4)
    t_plus = lax.rem(t + side + 32, 32)
    t_minus = lax.rem(t - side + 32, 32)
    t_pair = t + 4 - 8 * zh
    own_row = pl.multiple_of(OWN * m, OWN)
    i_row = pl.multiple_of(64 * z, 64)
    sent = []

    def send(src, dst, tile, mode, slot=None):
        index = len(sent)
        copy = pltpu.make_async_remote_copy(
            src_ref=src,
            dst_ref=dst,
            send_sem=ssem.at[index],
            recv_sem=rsem.at[index] if slot is None else slots.at[slot],
            device_id=(tile, mode),
            device_id_type=MESH,
        )
        copy.start()
        sent.append(copy)
        return copy

    def arrived(copies):
        for copy in copies:
            copy.wait_recv()

    mate = z + 1 - 2 * (z % 2)
    cross = 2 - z // 2
    cross_mate = cross + 1 - 2 * (cross % 2)
    inner = (z == 1) | (z == 2)
    outer_class = jnp.where(inner, 0, 1)
    relayed = []

    def relay(slot, part):
        copy = pltpu.make_async_remote_copy(
            src_ref=part,
            dst_ref=part,
            send_sem=relay_sem.at[slot],
            recv_sem=slots.at[slot],
            device_id=(t, 2 * mate + c),
            device_id_type=MESH,
        )
        copy.wait_recv()

        @pl.when(inner)
        def _():
            copy.start()

        relayed.append(copy)

    def y_tile(k):
        other = lax.rem(y + k, 4)
        return other, t - y + other

    def x_tile(k):
        other = lax.rem(x + k, 4)
        return other, t - 8 * x + 8 * other

    barrier = pltpu.get_barrier_semaphore()
    rw, lw, observed = com.rtable, com.ltable, com.observed
    loads = [
        pltpu.make_async_copy(rtable, rw, lsem.at[0]),
        pltpu.make_async_copy(ltable, lw, lsem.at[1]),
        pltpu.make_async_copy(measured.at[0, c], observed.at[0], lsem.at[2]),
        pltpu.make_async_copy(measured.at[1, c], observed.at[1], lsem.at[3]),
    ]
    partners = [(t, lax.rem(m + k, 8)) for k in range(1, 8)]
    partners += [(y_tile(k)[1], m) for k in range(1, 4)]
    partners += [(x_tile(k)[1], m) for k in range(1, 4)]
    partners += [(t_pair, m), (t_plus, m), (t_minus, m)]
    for partner in partners:
        pl.semaphore_signal(barrier, inc=1, device_id=partner, device_id_type=MESH)
    for load in loads:
        load.start()

    for b in range(BATCHES):
        for j in range(2):
            core = c if j == 0 else 1 - c
            row = pos[b, core, 0] - N * t
            column = pos[b, core, 1]
            com.where_own[4 * b + 2 * j : 4 * b + 2 * j + 1, :] = jnp.full((1, N), row, jnp.int32)
            com.where_own[4 * b + 2 * j + 1 : 4 * b + 2 * j + 2, :] = jnp.full(
                (1, N), column, jnp.int32
            )
    for part in range(2):
        mem[0].probes[0, part] = probe[0, part]
    pl.semaphore_wait(barrier, len(partners))

    def place(ref, b, j):
        return ref[4 * b + 2 * j : 4 * b + 2 * j + 1, :], ref[4 * b + 2 * j + 1 : 4 * b + 2 * j + 2, :]

    def whole(part, other):
        return pl.ds(pl.multiple_of(HALF * part + 32 * other, 32), 32)

    def piece(other):
        return pl.ds(pl.multiple_of(8 * other, 8), 8)

    lines = ((y_tile, x_tile), (x_tile, y_tile))
    spots = ((y, x), (x, y))
    held = [
        pl.ds(pl.multiple_of(HALF * part + 32 * spots[part][0] + 8 * spots[part][1], 8), 8)
        for part in range(2)
    ]

    class Reduce:
        def __init__(self, box):
            self.full, self.one, self.onesum = box.full, box.one, box.onesum
            self.two, self.twosum, self.pair = box.two, box.twosum, box.pair

        def start_one(self):
            self.copies = [[], []]
            for k in range(1, 4):
                for part in range(2):
                    other, tile = lines[part][0](k)
                    self.copies[part].append(
                        send(self.full.at[:, whole(part, other)], self.one.at[part, k - 1], tile, m)
                    )

        def start_two(self):
            after = [[], []]
            for part in range(2):
                arrived(self.copies[part])
                self.onesum[part] = (
                    self.full[:, whole(part, spots[part][0])]
                    + self.one[part, 0]
                    + self.one[part, 1]
                    + self.one[part, 2]
                )
                for k in range(1, 4):
                    other, tile = lines[part][1](k)
                    after[part].append(
                        send(
                            self.onesum.at[part, :, piece(other)], self.two.at[part, k - 1], tile, m
                        )
                    )
            self.copies = after

        def start_pair(self):
            for part in range(2):
                arrived(self.copies[part])
                self.twosum[part] = (
                    self.onesum[part, :, piece(spots[part][1])]
                    + self.two[part, 0]
                    + self.two[part, 1]
                    + self.two[part, 2]
                )
            self.copies = [send(self.twosum, self.pair, t_pair, m)]

        def finish(self):
            arrived(self.copies)
            return [self.twosum[part] + self.pair[part] for part in range(2)]

    class Gather:
        def __init__(self, view):
            self.view = view

        def start_one(self):
            self.copies = [[], []]
            for k in range(1, 4):
                for part in range(2):
                    rows = self.view(held[part])
                    self.copies[part].append(send(rows, rows, lines[part][1](k)[1], m))

        def start_two(self):
            after = [[], []]
            for part in range(2):
                arrived(self.copies[part])
                rows = self.view(whole(part, spots[part][0]))
                for k in range(1, 4):
                    after[part].append(send(rows, rows, lines[part][0](k)[1], m))
            self.copies = after

        def finish(self):
            for part in range(2):
                arrived(self.copies[part])

    def send_power(b, values):
        power = mem[b].power
        for part, (real, imag) in enumerate(values):
            power[0, part] = real * real + imag * imag
        return [send(power.at[0], power.at[k], t, lax.rem(m + k, 8)) for k in range(1, 8)]

    def sum_power(b, copies):
        arrived(copies)
        power = mem[b].power
        total = power[0]
        for k in range(1, 8):
            total = total + power[k]
        for part in range(2):
            mem[b].probes[0, 2, held[part], :] = total[part]

    def send_edges():
        plus, minus, out, rows = com.edge_plus, com.edge_minus, com.edge_out, com.edge_rows
        columns = iota((16, N), 1)
        spot = pl.ds(pl.multiple_of(16 * m, 16), 16)
        for j in range(2):
            row, column = place(com.where_own, 0, j)
            ahead = jnp.broadcast_to(row, (16, N)) >= 0
            first = columns >= column
            for part in range(2):
                low = jnp.where(ahead, plus[part, :, :N], minus[part, :, :N])
                high = jnp.where(ahead, plus[part, :, N:], minus[part, :, N:])
                out[j, part] = jnp.where(first, low, high)
        copies = [
            send(out.at[k % 2], rows.at[:, spot], t, lax.rem(m + k, 8)) for k in range(1, 8)
        ]
        rows[:, spot] = out[0]
        return copies

    def join_edges():
        rows, patch = com.edge_rows, mem[0].patch
        row, column = place(com.where_own, 0, 0)
        columns = iota((HALF, N), 1)
        first = columns >= column
        for half in range(2):
            span = slice(HALF * half, HALF * (half + 1))
            ahead = HALF * half + iota((HALF, N), 0) - row
            inside = (ahead >= 0) & (ahead < N)
            for part in range(2):
                own = jnp.where(first, obj[part, span, :N], obj[part, span, N:])
                patch[part, span, :] = jnp.where(inside, own, rows[part])

    def relay_patches(b, part):
        for place_class, chip in enumerate((cross, cross_mate)):
            for twin in range(2):
                core = c if twin == 0 else 1 - c
                rows = pl.ds(pl.multiple_of(OWN * (2 * chip + core), OWN), OWN)
                relay(4 * part + 2 * place_class + twin, mem[b].patch.at[part, rows])

    def relay_final(part, final_copies, sibling_copies):
        for index, chip in enumerate((mate, cross, cross_mate)):
            rows = pl.ds(pl.multiple_of(OWN * (2 * chip + c), OWN), OWN)
            spot = out_obj.at[part, rows]
            if index:
                relay(8 + 2 * part + index - 1, spot)
            else:
                arrived(final_copies[part : part + 1])
            sibling_copies.append(send(spot, spot, t, sibling))

    def send_patches(b, field, halo, part):
        out, patch = mem[b].pout, mem[b].patch
        rows = own_row + iota((OWN, N), 0)
        columns = iota((OWN, N), 1)
        for j in range(2):
            row, column = place(com.where_own, b, j)
            ahead = rows - row
            inside = (ahead >= 0) & (ahead < N)
            first = columns >= column
            low = jnp.where(inside, field[part, :, :N], halo[part, :, :N])
            high = jnp.where(inside, field[part, :, N:], halo[part, :, N:])
            out[j, part] = jnp.where(first, low, high)
        copies = []
        spot = patch.at[part, pl.ds(own_row, OWN)]
        for twin in range(2):
            core = c if twin == 0 else 1 - c
            slot = 4 * part + 2 * outer_class + twin
            send(out.at[twin, part], spot, t, 2 * cross + core, slot)
        for twin in range(2):
            core = c if twin == 0 else 1 - c
            copies.append(send(out.at[twin, part], spot, t, 2 * mate + core))
        copies.append(send(out.at[1, part], spot, t, sibling))
        patch[part, pl.ds(own_row, OWN)] = out[0, part]
        return copies

    def shifted(real, imag, row, column):
        i0, i1 = iota((N, N), 0), iota((N, N), 1)
        pick = (((i0 + row) & (N - 1)) == i1).astype(F32).astype(BF16)
        both = real if imag is None else jnp.concatenate([real, imag], axis=1)
        high, low = halves(both)
        moved = dot(jnp.concatenate([pick, pick], axis=1), jnp.concatenate([high, low], axis=0))
        pick = (((i1 + column) & (N - 1)) == i0).astype(F32).astype(BF16)
        if imag is not None:
            moved = jnp.concatenate([moved[:, :N], moved[:, N:]], axis=0)
        high, low = halves(moved)
        moved = dot(jnp.concatenate([high, low], axis=1), jnp.concatenate([pick, pick], axis=0))
        return moved[:N], moved[N:]

    def roll_probes(b):
        row, column = place(com.where_own, b, 0)
        probes = mem[b].probes
        for mode in range(2):
            rolled[mode, 0], rolled[mode, 1] = shifted(
                probes[mode, 0], probes[mode, 1], -row, -column
            )

    def unroll_step(b, mode):
        row, column = place(com.where_own, b, 0)
        dstep = mem[b].dstep
        dstep[mode, 0], dstep[mode, 1] = shifted(dstep[mode, 0], dstep[mode, 1], row, column)

    def unrolled_one(field, b):
        row, column = place(com.where_own, b, 0)
        return shifted(field, None, row, column)[0]

    def chunk_rows(q):
        return pl.ds(pl.multiple_of(q * 64, 64), 64)

    stage = com.stage

    def right_stage(mode, q, real, imag, sign):
        high, low = halves(jnp.concatenate([real, imag], axis=0))
        product = dot(jnp.concatenate([high, high, low], axis=1), rw[...])
        out_real = product[:64, :N] + sign * product[64:, N:]
        out_imag = product[64:, :N] - sign * product[:64, N:]
        high, low = halves(jnp.concatenate([out_real, out_imag], axis=1))
        stage[mode, pl.ds(pl.multiple_of(q * 64, 64), 64), :] = high
        stage[mode, pl.ds(pl.multiple_of(N + q * 64, 64), 64), :] = low
        stage[mode, pl.ds(pl.multiple_of(2 * N + q * 64, 64), 64), :] = high

    def left_stage(mode, q, sign):
        product = dot(lw[q], stage[mode])
        return (
            product[:64, :N] + sign * product[64:, N:],
            product[:64, N:] - sign * product[64:, :N],
        )

    far, rolled = com.far, com.rolled

    def forward(b):
        ofield, inten = mem[b].patch, mem[b].inten

        def first(q, carry):
            rows = chunk_rows(q)
            o_real, o_imag = ofield[0, rows, :], ofield[1, rows, :]
            for mode in range(2):
                p_real, p_imag = rolled[mode, 0, rows, :], rolled[mode, 1, rows, :]
                right_stage(
                    mode,
                    q,
                    p_real * o_real - p_imag * o_imag,
                    p_real * o_imag + p_imag * o_real,
                    1.0,
                )
            return carry

        lax.fori_loop(0, 4, first, 0)

        irecv, copies = mem[b].irecv, []
        for k in (1, 2, 3, 0):
            q = lax.rem(z + k, 4)
            rows = chunk_rows(q)
            total = None
            for mode in range(2):
                f_real, f_imag = left_stage(mode, q, 1.0)
                far[mode, 0, rows, :] = f_real
                far[mode, 1, rows, :] = f_imag
                power = f_real * f_real + f_imag * f_imag
                total = power if total is None else total + power
            inten[rows, :] = total
            if k:
                copies.append(send(inten.at[rows], irecv.at[k - 1], t, 2 * q + c))
        return copies

    def inverse(b, copies, between):
        ofield, factor = mem[b].patch, mem[b].factor
        grad, dstep, grecv = mem[b].grad, mem[b].dstep, mem[b].grecv

        for k in range(4):
            if k:
                arrived(copies[k - 1 : k])
            q = lax.rem(z - k + 4, 4)
            rows = chunk_rows(q)
            scale = factor[rows, :]
            for mode in range(2):
                right_stage(mode, q, scale * far[mode, 0, rows, :], scale * far[mode, 1, rows, :], -1.0)
        between()

        sends, later = [], []
        for k in (2, 1, 3, 0):
            q = lax.rem(z + k, 4)
            rows = chunk_rows(q)
            o_real, o_imag = ofield[0, rows, :], ofield[1, rows, :]
            g_real = jnp.zeros((64, N), F32)
            g_imag = jnp.zeros((64, N), F32)
            for mode in range(2):
                c_real, c_imag = left_stage(mode, q, -1.0)
                p_real, p_imag = rolled[mode, 0, rows, :], rolled[mode, 1, rows, :]
                g_real = g_real + p_real * c_real + p_imag * c_imag
                g_imag = g_imag + p_real * c_imag - p_imag * c_real
                dstep[mode, 0, rows, :] = o_real * c_real + o_imag * c_imag
                dstep[mode, 1, rows, :] = o_real * c_imag - o_imag * c_real
            grad[0, rows, :] = g_real
            grad[1, rows, :] = g_imag
            for twin in range(2):
                if k == 0 and twin == 0:
                    continue
                core = c if twin == 0 else 1 - c
                part = pl.ds(pl.multiple_of(OWN * (2 * q + core), OWN), OWN)
                slot = 2 * k + twin - 1
                sends.append(send(grad.at[0, part], grecv.at[slot, 0], t, 2 * q + core))
                later.append((grad.at[1, part], grecv.at[slot, 1], t, 2 * q + core))
        return [sends, [send(*args) for args in later]]

    def masks(ref, b, j):
        rows = own_row + iota((OWN, N), 0)
        row, column = place(ref, b, j)
        ahead = rows - row
        inside = (ahead >= 0) & (ahead < N)
        first = iota((OWN, N), 1) >= column
        return inside, first

    def sides(ref, b, j, here):
        inside, first = masks(ref, b, j)
        if not here:
            inside = jnp.logical_not(inside)
        return inside & first, inside & jnp.logical_not(first)

    def illumination(b, with_halo):
        high, low = halves(mem[b].probes[0, 2])
        power = jnp.concatenate([high, low], axis=0)
        rows = own_row + iota((OWN, N), 0)
        lanes = iota((OWN, N), 1)
        refs = [com.where_own, com.where_minus] + ([com.where_plus] if with_halo else [])
        spots_of = [(ref, j) for ref in refs for j in range(2)]
        picks = []
        for ref, j in spots_of:
            row, _ = place(ref, b, j)
            pick = (((rows - row) & (N - 1)) == lanes).astype(F32).astype(BF16)
            picks.append(jnp.concatenate([pick, pick], axis=1))
        taken = dot(jnp.concatenate(picks, axis=0), power)
        i0, i1 = iota((N, N), 0), iota((N, N), 1)
        blocks = [[jnp.zeros((OWN, N), F32) for _ in range(2)] for _ in range(2)]
        for index, (ref, j) in enumerate(spots_of):
            _, column = place(ref, b, j)
            pick = (((i1 - column) & (N - 1)) == i0).astype(F32).astype(BF16)
            high, low = halves(taken[OWN * index : OWN * (index + 1)])
            moved = dot(
                jnp.concatenate([high, low], axis=1), jnp.concatenate([pick, pick], axis=0)
            )
            kind = index // 2
            for block, here in ((0, kind == 0), (1, kind == 2)):
                if (block, kind) in ((0, 2), (1, 1)):
                    continue
                for side_index, mask in enumerate(sides(ref, b, j, here)):
                    blocks[block][side_index] = blocks[block][side_index] + jnp.where(
                        mask, moved, 0.0
                    )
        for block in range(2 if with_halo else 1):
            com.illum[block, :, :N] = blocks[block][0]
            com.illum[block, :, N:] = blocks[block][1]

    def update_block(b, part, field, field_rows, new, block, steps):
        for side_index, columns in ((0, slice(0, N)), (1, slice(N, WIDTH))):
            total = jnp.zeros((OWN, N), F32)
            for step, j, ref, here in steps:
                total = total + jnp.where(sides(ref, b, j, here)[side_index], step[j, part], 0.0)
            new[part, :, columns] = field[part, field_rows, columns] + total / (
                com.illum[block, :, columns] + 1.0
            )

    def refine():
        spot = pl.ds(pl.multiple_of(16 * m, 16), 16)
        far_spot = pl.ds(pl.multiple_of(HALF + 16 * m, 16), 16)
        edge_copies = [
            send(obj.at[:, spot], com.edge_plus, lax.rem(t + 31, 32), m),
            send(obj.at[:, far_spot], com.edge_minus, lax.rem(t + 1, 32), m),
        ]
        probe_copy = send(
            mem[0].probes.at[0, pl.ds(0, 2)], mem[0].probes.at[1, pl.ds(0, 2)], t, sibling
        )
        where_copies = [
            send(com.where_own, com.where_minus, t_plus, m),
            send(com.where_own, com.where_plus, t_minus, m),
        ]
        halo_copy = send(obj.at[:, pl.ds(own_row, OWN)], mem[0].halo, t_minus, m)
        arrived(edge_copies)
        patch_copies = send_edges()
        arrived([probe_copy])
        roll_probes(0)
        power_copies = send_power(
            0, [(probe[0, 0, held[part]], probe[0, 1, held[part]]) for part in range(2)]
        )
        arrived(where_copies)
        for load in loads:
            load.wait()
        for b in range(BATCHES):
            last = b == BATCHES - 1
            if b == 0:
                field, field_rows = obj, pl.ds(own_row, OWN)
            else:
                field, field_rows = mem[b - 1].objnew, slice(0, OWN)
            arrived(patch_copies)
            if b == 0:
                join_edges()
            if b:
                arrived([probe_copy])
                roll_probes(b)
            copies = forward(b)
            sum_power(b, power_copies)
            power_gather = Gather(lambda rows: mem[b].probes.at[0, 2, rows])
            power_gather.start_one()
            patch, cover = mem[b].patch, mem[b].cov
            cover[0] = unrolled_one(patch[0] * patch[0] + patch[1] * patch[1], b)
            cover_copy = send(cover, mem[b].csib, t, sibling)
            arrived([cover_copy])
            mem[b].cover_sum.full[...] = cover[...] + mem[b].csib[...]
            cover_sum = Reduce(mem[b].cover_sum)
            cover_sum.start_one()
            inten, irecv, factor = mem[b].inten, mem[b].irecv, mem[b].factor
            arrived(copies)
            own_rows = pl.ds(i_row, 64)
            total = inten[own_rows, :] + irecv[0] + irecv[1] + irecv[2]
            factor[own_rows, :] = (
                jnp.sqrt((observed[b, own_rows, :] + 1.0) / (total + 1.0)) - 1.0
            )
            copies = []
            for k in range(1, 4):
                other = lax.rem(z + k, 4)
                copies.append(send(factor.at[own_rows], factor.at[own_rows], t, 2 * other + c))
            power_gather.start_two()
            cover_sum.start_two()
            copies = inverse(b, copies, cover_sum.start_pair)
            grad, grecv, dstep = mem[b].grad, mem[b].grecv, mem[b].dstep
            unroll_step(b, 1)
            step_copy = send(dstep.at[1], mem[b].dsib, t, sibling)
            unroll_step(b, 0)
            power_gather.finish()
            arrived([step_copy])
            mem[b].probe_sum.full[...] = dstep[0] + mem[b].dsib[...]
            probe_sum = Reduce(mem[b].probe_sum)
            probe_sum.start_one()
            illumination(b, not last)
            own, minus, plus = mem[b].gown, mem[b].gminus, mem[b].gplus
            near = []
            for part in range(2):
                arrived(copies[part])
                here = grad[part, pl.ds(own_row, OWN)]
                own[0, part] = here + grecv[1, part] + grecv[3, part] + grecv[5, part]
                own[1, part] = (
                    grecv[0, part] + grecv[2, part] + grecv[4, part] + grecv[6, part]
                )
                near.append([send(own.at[:, part], minus.at[:, part], t_plus, m)])
                if not last:
                    near[part].append(send(own.at[:, part], plus.at[:, part], t_minus, m))
                if part == 0:
                    probe_sum.start_two()
            probe_sum.start_pair()
            if b == 0:
                arrived([halo_copy])
            own_steps = [(own, j, com.where_own, True) for j in range(2)]
            own_steps += [(minus, j, com.where_minus, False) for j in range(2)]
            halo_steps = [(plus, j, com.where_plus, True) for j in range(2)]
            halo_steps += [(own, j, com.where_own, False) for j in range(2)]
            new = mem[b].objnew
            final_copies, sibling_copies, patch_copies = [], [], []
            for part in range(2):
                arrived(near[part])
                update_block(b, part, field, field_rows, new, 0, own_steps)
                if last:
                    rows = pl.ds(own_row, OWN)
                    spot = out_obj.at[part, rows]
                    slot = 8 + 2 * part + outer_class
                    send(new.at[part], spot, t, 2 * cross + c, slot)
                    final_copies.append(send(new.at[part], spot, t, 2 * mate + c))
                    sibling_copies.append(send(new.at[part], spot, t, sibling))
                    out_obj[part, rows] = new[part]
                else:
                    halo = mem[b + 1].halo
                    update_block(b, part, mem[b].halo, slice(0, OWN), halo, 1, halo_steps)
                    patch_copies += send_patches(b + 1, new, halo, part)
            if last:
                relay_final(0, final_copies, sibling_copies)
            else:
                relay_patches(b + 1, 0)
            coverage = cover_sum.finish()
            step = probe_sum.finish()
            probes = mem[b].probes
            following = out_probe if last else mem[b + 1].probes
            values = []
            for half in range(2):
                values.append(
                    [
                        probes[0, part, held[half], :]
                        + step[half][part] / (coverage[half][0] + 1.0)
                        for part in range(2)
                    ]
                )
                for part in range(2):
                    following[0, part, held[half], :] = values[half][part]
            gather = Gather(lambda rows: following.at[0, pl.ds(0, 2), rows])
            gather.start_one()
            if last:
                relay_final(1, final_copies, sibling_copies)
            else:
                relay_patches(b + 1, 1)
            gather.start_two()
            if last:
                gather.finish()
                arrived(sibling_copies)
            else:
                power_copies = send_power(b + 1, values)
                gather.finish()
                probe_copy = send(
                    following.at[0, pl.ds(0, 2)], following.at[1, pl.ds(0, 2)], t, sibling
                )

    refine()
    for copy in relayed:
        pl.when(inner)(copy.wait_send)
    for copy in sent:
        copy.wait_send()


def shards(object_field, probe, positions, measured):
    right, left = split_tables()
    plan = scratch_plan()
    leaves, tree = jax.tree.flatten(plan)

    def body(*refs):
        kernel(tree, *refs)

    vmem = pl.BlockSpec(memory_space=pltpu.VMEM)
    anywhere = pl.BlockSpec(memory_space=pl.ANY)
    return pl.pallas_call(
        body,
        name="refine",
        out_shape=(
            jax.ShapeDtypeStruct(object_field.shape, F32),
            jax.ShapeDtypeStruct(probe.shape, F32),
        ),
        in_specs=[pl.BlockSpec(memory_space=pltpu.SMEM)] + [vmem] * 2 + [anywhere] * 3,
        out_specs=(vmem, vmem),
        scratch_shapes=leaves
        + [pltpu.SemaphoreType.DMA((count,)) for count in (COPIES, COPIES, 4, RELAYS, RELAYS)],
        compiler_params=pltpu.CompilerParams(
            collective_id=0, has_side_effects=True, vmem_limit_bytes=30 * 1024 * 1024
        ),
    )(positions, object_field, probe, measured, jnp.asarray(right), jnp.asarray(left))


def solution(mesh):
    in_specs = (
        P(None, "tile", None),
        P("mode", None, None, None),
        P(None, "tile", None),
        P(None, "tile", None, None),
    )
    out_specs = (P(None, "tile", None), P("mode", None, None, None))
    return jax.shard_map(shards, mesh=mesh, in_specs=in_specs, out_specs=out_specs, check_vma=False)
```

```python
import math

import jax
import jax.numpy as jnp
import ml_dtypes
import numpy as np
from jax import lax
from jax.experimental import pallas as pl
from jax.experimental.pallas import tpu as pltpu
from jax.sharding import PartitionSpec as P

N = 256
HALF = 128
WIDTH = 512
OWN = 32
BATCHES = 2
F32 = jnp.float32
BF16 = jnp.bfloat16
MESH = pl.DeviceIdType.MESH


def split_tables():
    index = np.arange(N)
    angle = (np.outer(index, index) % N) * (2.0 * math.pi / N)
    cosine = np.cos(angle) / math.sqrt(N)
    sine = np.sin(angle) / math.sqrt(N)
    bf16 = ml_dtypes.bfloat16

    def parts(table):
        high = table.astype(np.float32).astype(bf16)
        low = (table - high.astype(np.float64)).astype(np.float32).astype(bf16)
        return high, low

    ch, cl = parts(cosine)
    sh, sl = parts(sine)
    high = np.concatenate([ch, sh], axis=1)
    low = np.concatenate([cl, sl], axis=1)
    right = np.concatenate([high, low, high], axis=0)
    left = np.concatenate(
        [np.concatenate([ch, ch, cl], axis=1), np.concatenate([sh, sh, sl], axis=1)], axis=0
    )
    left = left.reshape(2, 4, 64, 3 * N).transpose(1, 0, 2, 3).reshape(4, 128, 3 * N)
    return right, left


def halves(value):
    high = value.astype(BF16)
    low = (value - high.astype(F32)).astype(BF16)
    return high, low


def dot(a, b):
    return jnp.dot(a, b, preferred_element_type=F32)


def iota(shape, dim):
    return lax.broadcasted_iota(jnp.int32, shape, dim)


def reduce_plan(parts):
    return dict(
        full=pltpu.VMEM((parts, N, N), F32),
        one=pltpu.VMEM((2, 3, parts, 32, N), F32),
        onesum=pltpu.VMEM((2, parts, 32, N), F32),
        two=pltpu.VMEM((2, 3, parts, 8, N), F32),
        twosum=pltpu.VMEM((2, parts, 8, N), F32),
        pair=pltpu.VMEM((2, parts, 8, N), F32),
    )


def batch_plan():
    return dict(
        halo=pltpu.VMEM((2, OWN, WIDTH), F32),
        patch=pltpu.VMEM((2, N, N), F32),
        pout=pltpu.VMEM((2, 2, OWN, N), F32),
        probes=pltpu.VMEM((2, 3, N, N), F32),
        power=pltpu.VMEM((8, 2, 8, N), F32),
        inten=pltpu.VMEM((N, N), F32),
        irecv=pltpu.VMEM((3, 64, N), F32),
        factor=pltpu.VMEM((N, N), F32),
        grad=pltpu.VMEM((2, N, N), F32),
        grecv=pltpu.VMEM((7, 2, OWN, N), F32),
        gown=pltpu.VMEM((2, 2, OWN, N), F32),
        gminus=pltpu.VMEM((2, 2, OWN, N), F32),
        gplus=pltpu.VMEM((2, 2, OWN, N), F32),
        objnew=pltpu.VMEM((2, OWN, WIDTH), F32),
        dstep=pltpu.VMEM((2, 2, N, N), F32),
        dsib=pltpu.VMEM((2, N, N), F32),
        cov=pltpu.VMEM((1, N, N), F32),
        csib=pltpu.VMEM((1, N, N), F32),
        probe_sum=reduce_plan(2),
        cover_sum=reduce_plan(1),
    )


def scratch_plan():
    common = dict(
        edge_plus=pltpu.VMEM((2, 16, WIDTH), F32),
        edge_minus=pltpu.VMEM((2, 16, WIDTH), F32),
        edge_out=pltpu.VMEM((2, 2, 16, N), F32),
        edge_rows=pltpu.VMEM((2, HALF, N), F32),
        observed=pltpu.VMEM((2, N, N), F32),
        rtable=pltpu.VMEM((3 * N, 2 * N), BF16),
        ltable=pltpu.VMEM((4, 128, 3 * N), BF16),
        where_own=pltpu.VMEM((8, N), jnp.int32),
        where_minus=pltpu.VMEM((8, N), jnp.int32),
        where_plus=pltpu.VMEM((8, N), jnp.int32),
        rolled=pltpu.VMEM((2, 2, N, N), F32),
        far=pltpu.VMEM((2, 2, N, N), F32),
        stage=pltpu.VMEM((2, 3 * N, 2 * N), BF16),
        illum=pltpu.VMEM((2, OWN, WIDTH), F32),
    )
    return [common] + [batch_plan() for _ in range(BATCHES)]


class Box:
    def __init__(self, entries):
        for name, entry in entries.items():
            setattr(self, name, Box(entry) if isinstance(entry, dict) else entry)


COPIES = 248


def kernel(tree, pos, obj, probe, measured, rtable, ltable, out_obj, out_probe, *scratch):
    ssem, rsem, lsem = scratch[-3:]
    com, *mem = [Box(entries) for entries in jax.tree.unflatten(tree, scratch[:-3])]
    t = lax.axis_index("tile")
    m = lax.axis_index("mode")
    x, zh, y = t // 8, (t // 4) % 2, t % 4
    z, c = m // 2, m % 2
    sibling = m + 1 - 2 * c

    def mirrored(chip):
        return chip + zh * (3 - 2 * chip)

    def facing(tile):
        flip = jnp.abs((tile // 4) % 2 - zh)
        return 2 * (z + flip * (3 - 2 * z)) + c

    block = 2 * mirrored(z) + c
    side = 1 - 2 * (block // 4)
    t_plus = lax.rem(t + side + 32, 32)
    t_minus = lax.rem(t - side + 32, 32)
    t_pair = t + 4 - 8 * zh
    own_row = pl.multiple_of(OWN * block, OWN)
    i_row = pl.multiple_of(64 * z, 64)
    sent = []

    def send(src, dst, tile, mode):
        index = len(sent)
        copy = pltpu.make_async_remote_copy(
            src_ref=src,
            dst_ref=dst,
            send_sem=ssem.at[index],
            recv_sem=rsem.at[index],
            device_id=(tile, mode),
            device_id_type=MESH,
        )
        copy.start()
        sent.append(copy)
        return copy

    def arrived(copies):
        for copy in copies:
            copy.wait_recv()

    def y_tile(k):
        other = lax.rem(y + k, 4)
        return other, t - y + other

    def x_tile(k):
        other = lax.rem(x + k, 4)
        return other, t - 8 * x + 8 * other

    barrier = pltpu.get_barrier_semaphore()
    rw, lw, observed = com.rtable, com.ltable, com.observed
    loads = [
        pltpu.make_async_copy(rtable, rw, lsem.at[0]),
        pltpu.make_async_copy(ltable, lw, lsem.at[1]),
        pltpu.make_async_copy(measured.at[0, c], observed.at[0], lsem.at[2]),
        pltpu.make_async_copy(measured.at[1, c], observed.at[1], lsem.at[3]),
    ]
    partners = [(t, lax.rem(m + k, 8)) for k in range(1, 8)]
    partners += [(y_tile(k)[1], m) for k in range(1, 4)]
    partners += [(x_tile(k)[1], m) for k in range(1, 4)]
    partners += [(t_pair, m), (t_plus, facing(t_plus)), (t_minus, facing(t_minus))]
    for partner in partners:
        pl.semaphore_signal(barrier, inc=1, device_id=partner, device_id_type=MESH)
    for load in loads:
        load.start()

    for b in range(BATCHES):
        for j in range(2):
            core = c if j == 0 else 1 - c
            row = pos[b, core, 0] - N * t
            column = pos[b, core, 1]
            com.where_own[4 * b + 2 * j : 4 * b + 2 * j + 1, :] = jnp.full((1, N), row, jnp.int32)
            com.where_own[4 * b + 2 * j + 1 : 4 * b + 2 * j + 2, :] = jnp.full(
                (1, N), column, jnp.int32
            )
    for part in range(2):
        mem[0].probes[0, part] = probe[0, part]
    pl.semaphore_wait(barrier, len(partners))

    def place(ref, b, j):
        return ref[4 * b + 2 * j : 4 * b + 2 * j + 1, :], ref[4 * b + 2 * j + 1 : 4 * b + 2 * j + 2, :]

    def whole(part, other):
        return pl.ds(pl.multiple_of(HALF * part + 32 * other, 32), 32)

    def piece(other):
        return pl.ds(pl.multiple_of(8 * other, 8), 8)

    lines = ((y_tile, x_tile), (x_tile, y_tile))
    spots = ((y, x), (x, y))
    held = [
        pl.ds(pl.multiple_of(HALF * part + 32 * spots[part][0] + 8 * spots[part][1], 8), 8)
        for part in range(2)
    ]

    class Reduce:
        def __init__(self, box):
            self.full, self.one, self.onesum = box.full, box.one, box.onesum
            self.two, self.twosum, self.pair = box.two, box.twosum, box.pair

        def start_one(self):
            self.copies = [[], []]
            for k in range(1, 4):
                for part in range(2):
                    other, tile = lines[part][0](k)
                    self.copies[part].append(
                        send(self.full.at[:, whole(part, other)], self.one.at[part, k - 1], tile, m)
                    )

        def start_two(self):
            after = [[], []]
            for part in range(2):
                arrived(self.copies[part])
                self.onesum[part] = (
                    self.full[:, whole(part, spots[part][0])]
                    + self.one[part, 0]
                    + self.one[part, 1]
                    + self.one[part, 2]
                )
                for k in range(1, 4):
                    other, tile = lines[part][1](k)
                    after[part].append(
                        send(
                            self.onesum.at[part, :, piece(other)], self.two.at[part, k - 1], tile, m
                        )
                    )
            self.copies = after

        def start_pair(self):
            for part in range(2):
                arrived(self.copies[part])
                self.twosum[part] = (
                    self.onesum[part, :, piece(spots[part][1])]
                    + self.two[part, 0]
                    + self.two[part, 1]
                    + self.two[part, 2]
                )
            self.copies = [send(self.twosum, self.pair, t_pair, m)]

        def finish(self):
            arrived(self.copies)
            return [self.twosum[part] + self.pair[part] for part in range(2)]

    class Gather:
        def __init__(self, view):
            self.view = view

        def start_one(self):
            self.copies = [[], []]
            for k in range(1, 4):
                for part in range(2):
                    rows = self.view(held[part])
                    self.copies[part].append(send(rows, rows, lines[part][1](k)[1], m))

        def start_two(self):
            after = [[], []]
            for part in range(2):
                arrived(self.copies[part])
                rows = self.view(whole(part, spots[part][0]))
                for k in range(1, 4):
                    after[part].append(send(rows, rows, lines[part][0](k)[1], m))
            self.copies = after

        def finish(self):
            for part in range(2):
                arrived(self.copies[part])

    def send_power(b, values):
        power = mem[b].power
        for part, (real, imag) in enumerate(values):
            power[0, part] = real * real + imag * imag
        return [send(power.at[0], power.at[k], t, lax.rem(m + k, 8)) for k in range(1, 8)]

    def sum_power(b, copies):
        arrived(copies)
        power = mem[b].power
        total = power[0]
        for k in range(1, 8):
            total = total + power[k]
        for part in range(2):
            mem[b].probes[0, 2, held[part], :] = total[part]

    def send_edges():
        plus, minus, out, rows = com.edge_plus, com.edge_minus, com.edge_out, com.edge_rows
        columns = iota((16, N), 1)
        spot = pl.ds(pl.multiple_of(16 * block, 16), 16)
        for j in range(2):
            row, column = place(com.where_own, 0, j)
            ahead = jnp.broadcast_to(row, (16, N)) >= 0
            first = columns >= column
            for part in range(2):
                low = jnp.where(ahead, plus[part, :, :N], minus[part, :, :N])
                high = jnp.where(ahead, plus[part, :, N:], minus[part, :, N:])
                out[j, part] = jnp.where(first, low, high)
        copies = [
            send(out.at[k % 2], rows.at[:, spot], t, lax.rem(m + k, 8)) for k in range(1, 8)
        ]
        rows[:, spot] = out[0]
        return copies

    def join_edges():
        rows, patch = com.edge_rows, mem[0].patch
        row, column = place(com.where_own, 0, 0)
        columns = iota((HALF, N), 1)
        first = columns >= column
        for half in range(2):
            span = slice(HALF * half, HALF * (half + 1))
            ahead = HALF * half + iota((HALF, N), 0) - row
            inside = (ahead >= 0) & (ahead < N)
            for part in range(2):
                own = jnp.where(first, obj[part, span, :N], obj[part, span, N:])
                patch[part, span, :] = jnp.where(inside, own, rows[part])

    def send_patches(b, field, halo, part):
        out, patch = mem[b].pout, mem[b].patch
        rows = own_row + iota((OWN, N), 0)
        columns = iota((OWN, N), 1)
        for j in range(2):
            row, column = place(com.where_own, b, j)
            ahead = rows - row
            inside = (ahead >= 0) & (ahead < N)
            first = columns >= column
            low = jnp.where(inside, field[part, :, :N], halo[part, :, :N])
            high = jnp.where(inside, field[part, :, N:], halo[part, :, N:])
            out[j, part] = jnp.where(first, low, high)
        copies = []
        spot = patch.at[part, pl.ds(own_row, OWN)]
        for k in range(1, 8):
            copies.append(send(out.at[k % 2, part], spot, t, lax.rem(m + k, 8)))
        patch[part, pl.ds(own_row, OWN)] = out[0, part]
        return copies

    def shifted(real, imag, row, column):
        i0, i1 = iota((N, N), 0), iota((N, N), 1)
        pick = (((i0 + row) & (N - 1)) == i1).astype(F32).astype(BF16)
        both = real if imag is None else jnp.concatenate([real, imag], axis=1)
        high, low = halves(both)
        moved = dot(jnp.concatenate([pick, pick], axis=1), jnp.concatenate([high, low], axis=0))
        pick = (((i1 + column) & (N - 1)) == i0).astype(F32).astype(BF16)
        if imag is not None:
            moved = jnp.concatenate([moved[:, :N], moved[:, N:]], axis=0)
        high, low = halves(moved)
        moved = dot(jnp.concatenate([high, low], axis=1), jnp.concatenate([pick, pick], axis=0))
        return moved[:N], moved[N:]

    def roll_probes(b):
        row, column = place(com.where_own, b, 0)
        probes = mem[b].probes
        for mode in range(2):
            rolled[mode, 0], rolled[mode, 1] = shifted(
                probes[mode, 0], probes[mode, 1], -row, -column
            )

    def unroll_step(b, mode):
        row, column = place(com.where_own, b, 0)
        dstep = mem[b].dstep
        dstep[mode, 0], dstep[mode, 1] = shifted(dstep[mode, 0], dstep[mode, 1], row, column)

    def unrolled_one(field, b):
        row, column = place(com.where_own, b, 0)
        return shifted(field, None, row, column)[0]

    def chunk_rows(q):
        return pl.ds(pl.multiple_of(q * 64, 64), 64)

    stage = com.stage

    def right_stage(mode, q, real, imag, sign):
        high, low = halves(jnp.concatenate([real, imag], axis=0))
        product = dot(jnp.concatenate([high, high, low], axis=1), rw[...])
        out_real = product[:64, :N] + sign * product[64:, N:]
        out_imag = product[64:, :N] - sign * product[:64, N:]
        high, low = halves(jnp.concatenate([out_real, out_imag], axis=1))
        stage[mode, pl.ds(pl.multiple_of(q * 64, 64), 64), :] = high
        stage[mode, pl.ds(pl.multiple_of(N + q * 64, 64), 64), :] = low
        stage[mode, pl.ds(pl.multiple_of(2 * N + q * 64, 64), 64), :] = high

    def left_stage(mode, q, sign):
        product = dot(lw[q], stage[mode])
        return (
            product[:64, :N] + sign * product[64:, N:],
            product[:64, N:] - sign * product[64:, :N],
        )

    far, rolled = com.far, com.rolled

    def forward(b):
        ofield, inten = mem[b].patch, mem[b].inten

        def first(q, carry):
            rows = chunk_rows(q)
            o_real, o_imag = ofield[0, rows, :], ofield[1, rows, :]
            for mode in range(2):
                p_real, p_imag = rolled[mode, 0, rows, :], rolled[mode, 1, rows, :]
                right_stage(
                    mode,
                    q,
                    p_real * o_real - p_imag * o_imag,
                    p_real * o_imag + p_imag * o_real,
                    1.0,
                )
            return carry

        lax.fori_loop(0, 4, first, 0)

        irecv, copies = mem[b].irecv, []
        for k in (1, 2, 3, 0):
            q = lax.rem(z + k, 4)
            rows = chunk_rows(q)
            total = None
            for mode in range(2):
                f_real, f_imag = left_stage(mode, q, 1.0)
                far[mode, 0, rows, :] = f_real
                far[mode, 1, rows, :] = f_imag
                power = f_real * f_real + f_imag * f_imag
                total = power if total is None else total + power
            inten[rows, :] = total
            if k:
                copies.append(send(inten.at[rows], irecv.at[k - 1], t, 2 * q + c))
        return copies

    def inverse(b, copies, between):
        ofield, factor = mem[b].patch, mem[b].factor
        grad, dstep, grecv = mem[b].grad, mem[b].dstep, mem[b].grecv

        for k in range(4):
            if k:
                arrived(copies[k - 1 : k])
            q = lax.rem(z - k + 4, 4)
            rows = chunk_rows(q)
            scale = factor[rows, :]
            for mode in range(2):
                right_stage(mode, q, scale * far[mode, 0, rows, :], scale * far[mode, 1, rows, :], -1.0)
        between()

        sends, later = [], []
        for k in (2, 1, 3, 0):
            q = lax.rem(z + k, 4)
            chunk = mirrored(q)
            rows = chunk_rows(chunk)
            o_real, o_imag = ofield[0, rows, :], ofield[1, rows, :]
            g_real = jnp.zeros((64, N), F32)
            g_imag = jnp.zeros((64, N), F32)
            for mode in range(2):
                c_real, c_imag = left_stage(mode, chunk, -1.0)
                p_real, p_imag = rolled[mode, 0, rows, :], rolled[mode, 1, rows, :]
                g_real = g_real + p_real * c_real + p_imag * c_imag
                g_imag = g_imag + p_real * c_imag - p_imag * c_real
                dstep[mode, 0, rows, :] = o_real * c_real + o_imag * c_imag
                dstep[mode, 1, rows, :] = o_real * c_imag - o_imag * c_real
            grad[0, rows, :] = g_real
            grad[1, rows, :] = g_imag
            for twin in range(2):
                if k == 0 and twin == 0:
                    continue
                core = c if twin == 0 else 1 - c
                part = pl.ds(pl.multiple_of(OWN * (2 * chunk + core), OWN), OWN)
                slot = 2 * k + twin - 1
                sends.append(send(grad.at[0, part], grecv.at[slot, 0], t, 2 * q + core))
                later.append((grad.at[1, part], grecv.at[slot, 1], t, 2 * q + core))
        return [sends, [send(*args) for args in later]]

    def masks(ref, b, j):
        rows = own_row + iota((OWN, N), 0)
        row, column = place(ref, b, j)
        ahead = rows - row
        inside = (ahead >= 0) & (ahead < N)
        first = iota((OWN, N), 1) >= column
        return inside, first

    def sides(ref, b, j, here):
        inside, first = masks(ref, b, j)
        if not here:
            inside = jnp.logical_not(inside)
        return inside & first, inside & jnp.logical_not(first)

    def illumination(b, with_halo):
        high, low = halves(mem[b].probes[0, 2])
        power = jnp.concatenate([high, low], axis=0)
        rows = own_row + iota((OWN, N), 0)
        lanes = iota((OWN, N), 1)
        refs = [com.where_own, com.where_minus] + ([com.where_plus] if with_halo else [])
        spots_of = [(ref, j) for ref in refs for j in range(2)]
        picks = []
        for ref, j in spots_of:
            row, _ = place(ref, b, j)
            pick = (((rows - row) & (N - 1)) == lanes).astype(F32).astype(BF16)
            picks.append(jnp.concatenate([pick, pick], axis=1))
        taken = dot(jnp.concatenate(picks, axis=0), power)
        i0, i1 = iota((N, N), 0), iota((N, N), 1)
        blocks = [[jnp.zeros((OWN, N), F32) for _ in range(2)] for _ in range(2)]
        for index, (ref, j) in enumerate(spots_of):
            _, column = place(ref, b, j)
            pick = (((i1 - column) & (N - 1)) == i0).astype(F32).astype(BF16)
            high, low = halves(taken[OWN * index : OWN * (index + 1)])
            moved = dot(
                jnp.concatenate([high, low], axis=1), jnp.concatenate([pick, pick], axis=0)
            )
            kind = index // 2
            for block, here in ((0, kind == 0), (1, kind == 2)):
                if (block, kind) in ((0, 2), (1, 1)):
                    continue
                for side_index, mask in enumerate(sides(ref, b, j, here)):
                    blocks[block][side_index] = blocks[block][side_index] + jnp.where(
                        mask, moved, 0.0
                    )
        for block in range(2 if with_halo else 1):
            com.illum[block, :, :N] = blocks[block][0]
            com.illum[block, :, N:] = blocks[block][1]

    def update_block(b, part, field, field_rows, new, block, steps):
        for side_index, columns in ((0, slice(0, N)), (1, slice(N, WIDTH))):
            total = jnp.zeros((OWN, N), F32)
            for step, j, ref, here in steps:
                total = total + jnp.where(sides(ref, b, j, here)[side_index], step[j, part], 0.0)
            new[part, :, columns] = field[part, field_rows, columns] + total / (
                com.illum[block, :, columns] + 1.0
            )

    def refine():
        spot = pl.ds(pl.multiple_of(16 * block, 16), 16)
        far_spot = pl.ds(pl.multiple_of(HALF + 16 * block, 16), 16)
        below, above = lax.rem(t + 31, 32), lax.rem(t + 1, 32)
        edge_copies = [
            send(obj.at[:, spot], com.edge_plus, below, facing(below)),
            send(obj.at[:, far_spot], com.edge_minus, above, facing(above)),
        ]
        probe_copy = send(
            mem[0].probes.at[0, pl.ds(0, 2)], mem[0].probes.at[1, pl.ds(0, 2)], t, sibling
        )
        where_copies = [
            send(com.where_own, com.where_minus, t_plus, facing(t_plus)),
            send(com.where_own, com.where_plus, t_minus, facing(t_minus)),
        ]
        halo_copy = send(obj.at[:, pl.ds(own_row, OWN)], mem[0].halo, t_minus, facing(t_minus))
        arrived(edge_copies)
        patch_copies = send_edges()
        arrived([probe_copy])
        roll_probes(0)
        power_copies = send_power(
            0, [(probe[0, 0, held[part]], probe[0, 1, held[part]]) for part in range(2)]
        )
        arrived(where_copies)
        for load in loads:
            load.wait()
        for b in range(BATCHES):
            last = b == BATCHES - 1
            if b == 0:
                field, field_rows = obj, pl.ds(own_row, OWN)
            else:
                field, field_rows = mem[b - 1].objnew, slice(0, OWN)
            arrived(patch_copies)
            if b == 0:
                join_edges()
            if b:
                arrived([probe_copy])
                roll_probes(b)
            copies = forward(b)
            sum_power(b, power_copies)
            power_gather = Gather(lambda rows: mem[b].probes.at[0, 2, rows])
            power_gather.start_one()
            patch, cover = mem[b].patch, mem[b].cov
            cover[0] = unrolled_one(patch[0] * patch[0] + patch[1] * patch[1], b)
            cover_copy = send(cover, mem[b].csib, t, sibling)
            arrived([cover_copy])
            mem[b].cover_sum.full[...] = cover[...] + mem[b].csib[...]
            cover_sum = Reduce(mem[b].cover_sum)
            cover_sum.start_one()
            inten, irecv, factor = mem[b].inten, mem[b].irecv, mem[b].factor
            arrived(copies)
            own_rows = pl.ds(i_row, 64)
            total = inten[own_rows, :] + irecv[0] + irecv[1] + irecv[2]
            factor[own_rows, :] = (
                jnp.sqrt((observed[b, own_rows, :] + 1.0) / (total + 1.0)) - 1.0
            )
            copies = []
            for k in range(1, 4):
                other = lax.rem(z + k, 4)
                copies.append(send(factor.at[own_rows], factor.at[own_rows], t, 2 * other + c))
            power_gather.start_two()
            cover_sum.start_two()
            copies = inverse(b, copies, cover_sum.start_pair)
            grad, grecv, dstep = mem[b].grad, mem[b].grecv, mem[b].dstep
            unroll_step(b, 1)
            step_copy = send(dstep.at[1], mem[b].dsib, t, sibling)
            unroll_step(b, 0)
            power_gather.finish()
            arrived([step_copy])
            mem[b].probe_sum.full[...] = dstep[0] + mem[b].dsib[...]
            probe_sum = Reduce(mem[b].probe_sum)
            probe_sum.start_one()
            illumination(b, not last)
            own, minus, plus = mem[b].gown, mem[b].gminus, mem[b].gplus
            near = []
            for part in range(2):
                arrived(copies[part])
                here = grad[part, pl.ds(own_row, OWN)]
                own[0, part] = here + grecv[1, part] + grecv[3, part] + grecv[5, part]
                own[1, part] = (
                    grecv[0, part] + grecv[2, part] + grecv[4, part] + grecv[6, part]
                )
                near.append([send(own.at[:, part], minus.at[:, part], t_plus, facing(t_plus))])
                if not last:
                    near[part].append(send(own.at[:, part], plus.at[:, part], t_minus, facing(t_minus)))
                if part == 0:
                    probe_sum.start_two()
            probe_sum.start_pair()
            if b == 0:
                arrived([halo_copy])
            own_steps = [(own, j, com.where_own, True) for j in range(2)]
            own_steps += [(minus, j, com.where_minus, False) for j in range(2)]
            halo_steps = [(plus, j, com.where_plus, True) for j in range(2)]
            halo_steps += [(own, j, com.where_own, False) for j in range(2)]
            new = mem[b].objnew
            final_copies, sibling_copies, patch_copies = [], [], []
            for part in range(2):
                arrived(near[part])
                update_block(b, part, field, field_rows, new, 0, own_steps)
                if last:
                    rows = pl.ds(own_row, OWN)
                    spot = out_obj.at[part, rows]
                    final_copies.append(
                        [
                            send(new.at[part], spot, t, 2 * lax.rem(z + k, 4) + c)
                            for k in range(1, 4)
                        ]
                    )
                    sibling_copies.append(send(new.at[part], spot, t, sibling))
                    out_obj[part, rows] = new[part]
                else:
                    halo = mem[b + 1].halo
                    update_block(b, part, mem[b].halo, slice(0, OWN), halo, 1, halo_steps)
                    patch_copies += send_patches(b + 1, new, halo, part)
            coverage = cover_sum.finish()
            step = probe_sum.finish()
            probes = mem[b].probes
            following = out_probe if last else mem[b + 1].probes
            values = []
            for half in range(2):
                values.append(
                    [
                        probes[0, part, held[half], :]
                        + step[half][part] / (coverage[half][0] + 1.0)
                        for part in range(2)
                    ]
                )
                for part in range(2):
                    following[0, part, held[half], :] = values[half][part]
            gather = Gather(lambda rows: following.at[0, pl.ds(0, 2), rows])
            gather.start_one()
            gather.start_two()
            if last:
                for part in range(2):
                    for k in range(1, 4):
                        arrived(final_copies[part][k - 1 : k])
                        other = 2 * mirrored(lax.rem(z - k + 4, 4)) + c
                        rows = pl.ds(pl.multiple_of(OWN * other, OWN), OWN)
                        spot = out_obj.at[part, rows]
                        sibling_copies.append(send(spot, spot, t, sibling))
                gather.finish()
                arrived(sibling_copies)
            else:
                power_copies = send_power(b + 1, values)
                gather.finish()
                probe_copy = send(
                    following.at[0, pl.ds(0, 2)], following.at[1, pl.ds(0, 2)], t, sibling
                )

    refine()
    for copy in sent:
        copy.wait_send()


def shards(object_field, probe, positions, measured):
    right, left = split_tables()
    plan = scratch_plan()
    leaves, tree = jax.tree.flatten(plan)

    def body(*refs):
        kernel(tree, *refs)

    vmem = pl.BlockSpec(memory_space=pltpu.VMEM)
    anywhere = pl.BlockSpec(memory_space=pl.ANY)
    return pl.pallas_call(
        body,
        name="refine",
        out_shape=(
            jax.ShapeDtypeStruct(object_field.shape, F32),
            jax.ShapeDtypeStruct(probe.shape, F32),
        ),
        in_specs=[pl.BlockSpec(memory_space=pltpu.SMEM)] + [vmem] * 2 + [anywhere] * 3,
        out_specs=(vmem, vmem),
        scratch_shapes=leaves
        + [pltpu.SemaphoreType.DMA((count,)) for count in (COPIES, COPIES, 4)],
        compiler_params=pltpu.CompilerParams(
            collective_id=0, has_side_effects=True, vmem_limit_bytes=30 * 1024 * 1024
        ),
    )(positions, object_field, probe, measured, jnp.asarray(right), jnp.asarray(left))


def solution(mesh):
    in_specs = (
        P(None, "tile", None),
        P("mode", None, None, None),
        P(None, "tile", None),
        P(None, "tile", None, None),
    )
    out_specs = (P(None, "tile", None), P("mode", None, None, None))
    return jax.shard_map(shards, mesh=mesh, in_specs=in_specs, out_specs=out_specs, check_vma=False)
```

```python
import math

import jax
import jax.numpy as jnp
import ml_dtypes
import numpy as np
from jax import lax
from jax.experimental import pallas as pl
from jax.experimental.pallas import tpu as pltpu
from jax.sharding import PartitionSpec as P

N = 256
HALF = 128
WIDTH = 512
OWN = 32
BATCHES = 2
F32 = jnp.float32
BF16 = jnp.bfloat16
MESH = pl.DeviceIdType.MESH


def split_tables():
    index = np.arange(N)
    angle = (np.outer(index, index) % N) * (2.0 * math.pi / N)
    cosine = np.cos(angle) / math.sqrt(N)
    sine = np.sin(angle) / math.sqrt(N)
    bf16 = ml_dtypes.bfloat16

    def parts(table):
        high = table.astype(np.float32).astype(bf16)
        low = (table - high.astype(np.float64)).astype(np.float32).astype(bf16)
        return high, low

    ch, cl = parts(cosine)
    sh, sl = parts(sine)
    high = np.concatenate([ch, sh], axis=1)
    low = np.concatenate([cl, sl], axis=1)
    right = np.concatenate([high, low, high], axis=0)
    left = np.concatenate(
        [np.concatenate([ch, ch, cl], axis=1), np.concatenate([sh, sh, sl], axis=1)], axis=0
    )
    left = left.reshape(2, 4, 64, 3 * N).transpose(1, 0, 2, 3).reshape(4, 128, 3 * N)
    return right, left


def halves(value):
    high = value.astype(BF16)
    low = (value - high.astype(F32)).astype(BF16)
    return high, low


def dot(a, b):
    return jnp.dot(a, b, preferred_element_type=F32)


def iota(shape, dim):
    return lax.broadcasted_iota(jnp.int32, shape, dim)


def reduce_plan(parts):
    return dict(
        full=pltpu.VMEM((parts, N, N), F32),
        one=pltpu.VMEM((2, 3, parts, 32, N), F32),
        onesum=pltpu.VMEM((2, parts, 32, N), F32),
        two=pltpu.VMEM((2, 3, parts, 8, N), F32),
        twosum=pltpu.VMEM((2, parts, 8, N), F32),
        pair=pltpu.VMEM((2, parts, 8, N), F32),
    )


def batch_plan():
    return dict(
        halo=pltpu.VMEM((2, OWN, WIDTH), F32),
        patch=pltpu.VMEM((2, N, N), F32),
        pout=pltpu.VMEM((2, 2, OWN, N), F32),
        probes=pltpu.VMEM((2, 3, N, N), F32),
        power=pltpu.VMEM((8, 2, 8, N), F32),
        inten=pltpu.VMEM((N, N), F32),
        irecv=pltpu.VMEM((3, 64, N), F32),
        factor=pltpu.VMEM((N, N), F32),
        grad=pltpu.VMEM((2, N, N), F32),
        grecv=pltpu.VMEM((7, 2, OWN, N), F32),
        gown=pltpu.VMEM((2, 2, OWN, N), F32),
        gminus=pltpu.VMEM((2, 2, OWN, N), F32),
        gplus=pltpu.VMEM((2, 2, OWN, N), F32),
        objnew=pltpu.VMEM((2, OWN, WIDTH), F32),
        dstep=pltpu.VMEM((2, 2, N, N), F32),
        dsib=pltpu.VMEM((2, N, N), F32),
        cov=pltpu.VMEM((1, N, N), F32),
        csib=pltpu.VMEM((1, N, N), F32),
        probe_sum=reduce_plan(2),
        cover_sum=reduce_plan(1),
    )


def scratch_plan():
    common = dict(
        edge_plus=pltpu.VMEM((2, 16, WIDTH), F32),
        edge_minus=pltpu.VMEM((2, 16, WIDTH), F32),
        edge_out=pltpu.VMEM((2, 2, 16, N), F32),
        edge_rows=pltpu.VMEM((2, HALF, N), F32),
        observed=pltpu.VMEM((2, N, N), F32),
        rtable=pltpu.VMEM((3 * N, 2 * N), BF16),
        ltable=pltpu.VMEM((4, 128, 3 * N), BF16),
        where_own=pltpu.VMEM((8, N), jnp.int32),
        where_minus=pltpu.VMEM((8, N), jnp.int32),
        where_plus=pltpu.VMEM((8, N), jnp.int32),
        strip=pltpu.VMEM((2, N, WIDTH), F32),
        rolled=pltpu.VMEM((2, 2, N, N), F32),
        far=pltpu.VMEM((2, 2, N, N), F32),
        stage=pltpu.VMEM((2, 3 * N, 2 * N), BF16),
        illum=pltpu.VMEM((2, OWN, WIDTH), F32),
    )
    return [common] + [batch_plan() for _ in range(BATCHES)]


class Box:
    def __init__(self, entries):
        for name, entry in entries.items():
            setattr(self, name, Box(entry) if isinstance(entry, dict) else entry)


COPIES = 248


def kernel(tree, pos, object_field, probe, measured, rtable, ltable, out_obj, out_probe, *scratch):
    ssem, rsem, lsem = scratch[-3:]
    com, *mem = [Box(entries) for entries in jax.tree.unflatten(tree, scratch[:-3])]
    t = lax.axis_index("tile")
    m = lax.axis_index("mode")
    x, zh, y = t // 8, (t // 4) % 2, t % 4
    z, c = m // 2, m % 2
    sibling = m + 1 - 2 * c

    def mirrored(chip):
        return chip + zh * (3 - 2 * chip)

    def facing(tile):
        flip = jnp.abs((tile // 4) % 2 - zh)
        return 2 * (z + flip * (3 - 2 * z)) + c

    block = 2 * mirrored(z) + c
    side = 1 - 2 * (block // 4)
    t_plus = lax.rem(t + side + 32, 32)
    t_minus = lax.rem(t - side + 32, 32)
    t_pair = t + 4 - 8 * zh
    own_row = pl.multiple_of(OWN * block, OWN)
    i_row = pl.multiple_of(64 * z, 64)
    sent = []
    obj = com.strip
    first_loads = [
        pltpu.make_async_copy(object_field, obj, lsem.at[4]),
        pltpu.make_async_copy(probe.at[0], mem[0].probes.at[0, pl.ds(0, 2)], lsem.at[5]),
    ]
    for load in first_loads:
        load.start()

    def send(src, dst, tile, mode):
        index = len(sent)
        copy = pltpu.make_async_remote_copy(
            src_ref=src,
            dst_ref=dst,
            send_sem=ssem.at[index],
            recv_sem=rsem.at[index],
            device_id=(tile, mode),
            device_id_type=MESH,
        )
        copy.start()
        sent.append(copy)
        return copy

    def arrived(copies):
        for copy in copies:
            copy.wait_recv()

    def y_tile(k):
        other = lax.rem(y + k, 4)
        return other, t - y + other

    def x_tile(k):
        other = lax.rem(x + k, 4)
        return other, t - 8 * x + 8 * other

    barrier = pltpu.get_barrier_semaphore()
    rw, lw, observed = com.rtable, com.ltable, com.observed
    loads = [
        pltpu.make_async_copy(rtable, rw, lsem.at[0]),
        pltpu.make_async_copy(ltable, lw, lsem.at[1]),
        pltpu.make_async_copy(measured.at[0, c], observed.at[0], lsem.at[2]),
        pltpu.make_async_copy(measured.at[1, c], observed.at[1], lsem.at[3]),
    ]
    partners = [(t, lax.rem(m + k, 8)) for k in range(1, 8)]
    partners += [(y_tile(k)[1], m) for k in range(1, 4)]
    partners += [(x_tile(k)[1], m) for k in range(1, 4)]
    partners += [(t_pair, m), (t_plus, facing(t_plus)), (t_minus, facing(t_minus))]
    for partner in partners:
        pl.semaphore_signal(barrier, inc=1, device_id=partner, device_id_type=MESH)
    for load in loads:
        load.start()

    for b in range(BATCHES):
        for j in range(2):
            core = c if j == 0 else 1 - c
            row = pos[b, core, 0] - N * t
            column = pos[b, core, 1]
            com.where_own[4 * b + 2 * j : 4 * b + 2 * j + 1, :] = jnp.full((1, N), row, jnp.int32)
            com.where_own[4 * b + 2 * j + 1 : 4 * b + 2 * j + 2, :] = jnp.full(
                (1, N), column, jnp.int32
            )
    for load in first_loads:
        load.wait()
    pl.semaphore_wait(barrier, len(partners))

    def place(ref, b, j):
        return ref[4 * b + 2 * j : 4 * b + 2 * j + 1, :], ref[4 * b + 2 * j + 1 : 4 * b + 2 * j + 2, :]

    def whole(part, other):
        return pl.ds(pl.multiple_of(HALF * part + 32 * other, 32), 32)

    def piece(other):
        return pl.ds(pl.multiple_of(8 * other, 8), 8)

    lines = ((y_tile, x_tile), (x_tile, y_tile))
    spots = ((y, x), (x, y))
    held = [
        pl.ds(pl.multiple_of(HALF * part + 32 * spots[part][0] + 8 * spots[part][1], 8), 8)
        for part in range(2)
    ]

    class Reduce:
        def __init__(self, box):
            self.full, self.one, self.onesum = box.full, box.one, box.onesum
            self.two, self.twosum, self.pair = box.two, box.twosum, box.pair

        def start_one(self):
            self.copies = [[], []]
            for k in range(1, 4):
                for part in range(2):
                    other, tile = lines[part][0](k)
                    self.copies[part].append(
                        send(self.full.at[:, whole(part, other)], self.one.at[part, k - 1], tile, m)
                    )

        def start_two(self):
            after = [[], []]
            for part in range(2):
                arrived(self.copies[part])
                self.onesum[part] = (
                    self.full[:, whole(part, spots[part][0])]
                    + self.one[part, 0]
                    + self.one[part, 1]
                    + self.one[part, 2]
                )
                for k in range(1, 4):
                    other, tile = lines[part][1](k)
                    after[part].append(
                        send(
                            self.onesum.at[part, :, piece(other)], self.two.at[part, k - 1], tile, m
                        )
                    )
            self.copies = after

        def start_pair(self):
            for part in range(2):
                arrived(self.copies[part])
                self.twosum[part] = (
                    self.onesum[part, :, piece(spots[part][1])]
                    + self.two[part, 0]
                    + self.two[part, 1]
                    + self.two[part, 2]
                )
            self.copies = [send(self.twosum, self.pair, t_pair, m)]

        def finish(self):
            arrived(self.copies)
            return [self.twosum[part] + self.pair[part] for part in range(2)]

    class Gather:
        def __init__(self, view):
            self.view = view

        def start_one(self):
            self.copies = [[], []]
            for k in range(1, 4):
                for part in range(2):
                    rows = self.view(held[part])
                    self.copies[part].append(send(rows, rows, lines[part][1](k)[1], m))

        def start_two(self):
            after = [[], []]
            for part in range(2):
                arrived(self.copies[part])
                rows = self.view(whole(part, spots[part][0]))
                for k in range(1, 4):
                    after[part].append(send(rows, rows, lines[part][0](k)[1], m))
            self.copies = after

        def finish(self):
            for part in range(2):
                arrived(self.copies[part])

    def send_power(b, values):
        power = mem[b].power
        for part, (real, imag) in enumerate(values):
            power[0, part] = real * real + imag * imag
        return [send(power.at[0], power.at[k], t, lax.rem(m + k, 8)) for k in range(1, 8)]

    def sum_power(b, copies):
        arrived(copies)
        power = mem[b].power
        total = power[0]
        for k in range(1, 8):
            total = total + power[k]
        for part in range(2):
            mem[b].probes[0, 2, held[part], :] = total[part]

    def send_edges():
        plus, minus, out, rows = com.edge_plus, com.edge_minus, com.edge_out, com.edge_rows
        columns = iota((16, N), 1)
        spot = pl.ds(pl.multiple_of(16 * block, 16), 16)
        for j in range(2):
            row, column = place(com.where_own, 0, j)
            ahead = jnp.broadcast_to(row, (16, N)) >= 0
            first = columns >= column
            for part in range(2):
                low = jnp.where(ahead, plus[part, :, :N], minus[part, :, :N])
                high = jnp.where(ahead, plus[part, :, N:], minus[part, :, N:])
                out[j, part] = jnp.where(first, low, high)
        copies = [
            send(out.at[k % 2], rows.at[:, spot], t, lax.rem(m + k, 8)) for k in range(1, 8)
        ]
        rows[:, spot] = out[0]
        return copies

    def join_edges():
        rows, patch = com.edge_rows, mem[0].patch
        row, column = place(com.where_own, 0, 0)
        columns = iota((HALF, N), 1)
        first = columns >= column
        for half in range(2):
            span = slice(HALF * half, HALF * (half + 1))
            ahead = HALF * half + iota((HALF, N), 0) - row
            inside = (ahead >= 0) & (ahead < N)
            for part in range(2):
                own = jnp.where(first, obj[part, span, :N], obj[part, span, N:])
                patch[part, span, :] = jnp.where(inside, own, rows[part])

    def send_patches(b, field, halo, part):
        out, patch = mem[b].pout, mem[b].patch
        rows = own_row + iota((OWN, N), 0)
        columns = iota((OWN, N), 1)
        for j in range(2):
            row, column = place(com.where_own, b, j)
            ahead = rows - row
            inside = (ahead >= 0) & (ahead < N)
            first = columns >= column
            low = jnp.where(inside, field[part, :, :N], halo[part, :, :N])
            high = jnp.where(inside, field[part, :, N:], halo[part, :, N:])
            out[j, part] = jnp.where(first, low, high)
        copies = []
        spot = patch.at[part, pl.ds(own_row, OWN)]
        for k in range(1, 8):
            copies.append(send(out.at[k % 2, part], spot, t, lax.rem(m + k, 8)))
        patch[part, pl.ds(own_row, OWN)] = out[0, part]
        return copies

    def shifted(real, imag, row, column):
        i0, i1 = iota((N, N), 0), iota((N, N), 1)
        pick = (((i0 + row) & (N - 1)) == i1).astype(F32).astype(BF16)
        both = real if imag is None else jnp.concatenate([real, imag], axis=1)
        high, low = halves(both)
        moved = dot(jnp.concatenate([pick, pick], axis=1), jnp.concatenate([high, low], axis=0))
        pick = (((i1 + column) & (N - 1)) == i0).astype(F32).astype(BF16)
        if imag is not None:
            moved = jnp.concatenate([moved[:, :N], moved[:, N:]], axis=0)
        high, low = halves(moved)
        moved = dot(jnp.concatenate([high, low], axis=1), jnp.concatenate([pick, pick], axis=0))
        return moved[:N], moved[N:]

    def roll_probe(b, mode):
        row, column = place(com.where_own, b, 0)
        probes = mem[b].probes
        rolled[mode, 0], rolled[mode, 1] = shifted(
            probes[mode, 0], probes[mode, 1], -row, -column
        )

    def unroll_step(b, mode):
        row, column = place(com.where_own, b, 0)
        dstep = mem[b].dstep
        dstep[mode, 0], dstep[mode, 1] = shifted(dstep[mode, 0], dstep[mode, 1], row, column)

    def unrolled_one(field, b):
        row, column = place(com.where_own, b, 0)
        return shifted(field, None, row, column)[0]

    def chunk_rows(q):
        return pl.ds(pl.multiple_of(q * 64, 64), 64)

    stage = com.stage

    def right_stage(mode, q, real, imag, sign):
        high, low = halves(jnp.concatenate([real, imag], axis=0))
        product = dot(jnp.concatenate([high, high, low], axis=1), rw[...])
        out_real = product[:64, :N] + sign * product[64:, N:]
        out_imag = product[64:, :N] - sign * product[:64, N:]
        high, low = halves(jnp.concatenate([out_real, out_imag], axis=1))
        stage[mode, pl.ds(pl.multiple_of(q * 64, 64), 64), :] = high
        stage[mode, pl.ds(pl.multiple_of(N + q * 64, 64), 64), :] = low
        stage[mode, pl.ds(pl.multiple_of(2 * N + q * 64, 64), 64), :] = high

    def left_stage(mode, q, sign):
        product = dot(lw[q], stage[mode])
        return (
            product[:64, :N] + sign * product[64:, N:],
            product[:64, N:] - sign * product[64:, :N],
        )

    far, rolled = com.far, com.rolled

    def forward(b):
        ofield, inten = mem[b].patch, mem[b].inten

        def first(q, carry):
            rows = chunk_rows(q)
            o_real, o_imag = ofield[0, rows, :], ofield[1, rows, :]
            for mode in range(2):
                p_real, p_imag = rolled[mode, 0, rows, :], rolled[mode, 1, rows, :]
                right_stage(
                    mode,
                    q,
                    p_real * o_real - p_imag * o_imag,
                    p_real * o_imag + p_imag * o_real,
                    1.0,
                )
            return carry

        lax.fori_loop(0, 4, first, 0)

        irecv, copies = mem[b].irecv, []
        for k in (1, 2, 3, 0):
            q = lax.rem(z + k, 4)
            rows = chunk_rows(q)
            total = None
            for mode in range(2):
                f_real, f_imag = left_stage(mode, q, 1.0)
                far[mode, 0, rows, :] = f_real
                far[mode, 1, rows, :] = f_imag
                power = f_real * f_real + f_imag * f_imag
                total = power if total is None else total + power
            inten[rows, :] = total
            if k:
                copies.append(send(inten.at[rows], irecv.at[k - 1], t, 2 * q + c))
        return copies

    def inverse(b, copies, between):
        ofield, factor = mem[b].patch, mem[b].factor
        grad, dstep, grecv = mem[b].grad, mem[b].dstep, mem[b].grecv

        for k in range(4):
            if k:
                arrived(copies[k - 1 : k])
            q = lax.rem(z - k + 4, 4)
            rows = chunk_rows(q)
            scale = factor[rows, :]
            for mode in range(2):
                right_stage(mode, q, scale * far[mode, 0, rows, :], scale * far[mode, 1, rows, :], -1.0)
        between()

        sends, later = [], []
        for k in (2, 1, 3, 0):
            q = lax.rem(z + k, 4)
            chunk = mirrored(q)
            rows = chunk_rows(chunk)
            o_real, o_imag = ofield[0, rows, :], ofield[1, rows, :]
            g_real = jnp.zeros((64, N), F32)
            g_imag = jnp.zeros((64, N), F32)
            for mode in range(2):
                c_real, c_imag = left_stage(mode, chunk, -1.0)
                p_real, p_imag = rolled[mode, 0, rows, :], rolled[mode, 1, rows, :]
                g_real = g_real + p_real * c_real + p_imag * c_imag
                g_imag = g_imag + p_real * c_imag - p_imag * c_real
                dstep[mode, 0, rows, :] = o_real * c_real + o_imag * c_imag
                dstep[mode, 1, rows, :] = o_real * c_imag - o_imag * c_real
            grad[0, rows, :] = g_real
            grad[1, rows, :] = g_imag
            for twin in range(2):
                if k == 0 and twin == 0:
                    continue
                core = c if twin == 0 else 1 - c
                part = pl.ds(pl.multiple_of(OWN * (2 * chunk + core), OWN), OWN)
                slot = 2 * k + twin - 1
                sends.append(send(grad.at[0, part], grecv.at[slot, 0], t, 2 * q + core))
                later.append((grad.at[1, part], grecv.at[slot, 1], t, 2 * q + core))
        return [sends, [send(*args) for args in later]]

    def masks(ref, b, j):
        rows = own_row + iota((OWN, N), 0)
        row, column = place(ref, b, j)
        ahead = rows - row
        inside = (ahead >= 0) & (ahead < N)
        first = iota((OWN, N), 1) >= column
        return inside, first

    def sides(ref, b, j, here):
        inside, first = masks(ref, b, j)
        if not here:
            inside = jnp.logical_not(inside)
        return inside & first, inside & jnp.logical_not(first)

    def illumination(b, with_halo):
        high, low = halves(mem[b].probes[0, 2])
        power = jnp.concatenate([high, low], axis=0)
        rows = own_row + iota((OWN, N), 0)
        lanes = iota((OWN, N), 1)
        refs = [com.where_own, com.where_minus] + ([com.where_plus] if with_halo else [])
        spots_of = [(ref, j) for ref in refs for j in range(2)]
        picks = []
        for ref, j in spots_of:
            row, _ = place(ref, b, j)
            pick = (((rows - row) & (N - 1)) == lanes).astype(F32).astype(BF16)
            picks.append(jnp.concatenate([pick, pick], axis=1))
        taken = dot(jnp.concatenate(picks, axis=0), power)
        i0, i1 = iota((N, N), 0), iota((N, N), 1)
        blocks = [[jnp.zeros((OWN, N), F32) for _ in range(2)] for _ in range(2)]
        for index, (ref, j) in enumerate(spots_of):
            _, column = place(ref, b, j)
            pick = (((i1 - column) & (N - 1)) == i0).astype(F32).astype(BF16)
            high, low = halves(taken[OWN * index : OWN * (index + 1)])
            moved = dot(
                jnp.concatenate([high, low], axis=1), jnp.concatenate([pick, pick], axis=0)
            )
            kind = index // 2
            for block, here in ((0, kind == 0), (1, kind == 2)):
                if (block, kind) in ((0, 2), (1, 1)):
                    continue
                for side_index, mask in enumerate(sides(ref, b, j, here)):
                    blocks[block][side_index] = blocks[block][side_index] + jnp.where(
                        mask, moved, 0.0
                    )
        for block in range(2 if with_halo else 1):
            com.illum[block, :, :N] = blocks[block][0]
            com.illum[block, :, N:] = blocks[block][1]

    def update_block(b, part, field, field_rows, new, block, steps):
        for side_index, columns in ((0, slice(0, N)), (1, slice(N, WIDTH))):
            total = jnp.zeros((OWN, N), F32)
            for step, j, ref, here in steps:
                total = total + jnp.where(sides(ref, b, j, here)[side_index], step[j, part], 0.0)
            new[part, :, columns] = field[part, field_rows, columns] + total / (
                com.illum[block, :, columns] + 1.0
            )

    def refine():
        spot = pl.ds(pl.multiple_of(16 * block, 16), 16)
        far_spot = pl.ds(pl.multiple_of(HALF + 16 * block, 16), 16)
        below, above = lax.rem(t + 31, 32), lax.rem(t + 1, 32)
        edge_copies = [
            send(obj.at[:, spot], com.edge_plus, below, facing(below)),
            send(obj.at[:, far_spot], com.edge_minus, above, facing(above)),
        ]
        probe_copy = send(
            mem[0].probes.at[0, pl.ds(0, 2)], mem[0].probes.at[1, pl.ds(0, 2)], t, sibling
        )
        where_copies = [
            send(com.where_own, com.where_minus, t_plus, facing(t_plus)),
            send(com.where_own, com.where_plus, t_minus, facing(t_minus)),
        ]
        halo_copy = send(obj.at[:, pl.ds(own_row, OWN)], mem[0].halo, t_minus, facing(t_minus))
        arrived(edge_copies)
        patch_copies = send_edges()
        roll_probe(0, 0)
        mine = mem[0].probes.at[0]
        power_copies = send_power(
            0, [(mine[0, held[part]], mine[1, held[part]]) for part in range(2)]
        )
        arrived(where_copies)
        for load in loads:
            load.wait()
        for b in range(BATCHES):
            last = b == BATCHES - 1
            if b == 0:
                field, field_rows = obj, pl.ds(own_row, OWN)
            else:
                field, field_rows = mem[b - 1].objnew, slice(0, OWN)
            if b:
                roll_probe(b, 0)
            arrived([probe_copy])
            roll_probe(b, 1)
            arrived(patch_copies)
            if b == 0:
                join_edges()
            copies = forward(b)
            sum_power(b, power_copies)
            power_gather = Gather(lambda rows: mem[b].probes.at[0, 2, rows])
            power_gather.start_one()
            patch, cover = mem[b].patch, mem[b].cov
            cover[0] = unrolled_one(patch[0] * patch[0] + patch[1] * patch[1], b)
            cover_copy = send(cover, mem[b].csib, t, sibling)
            arrived([cover_copy])
            mem[b].cover_sum.full[...] = cover[...] + mem[b].csib[...]
            cover_sum = Reduce(mem[b].cover_sum)
            cover_sum.start_one()
            inten, irecv, factor = mem[b].inten, mem[b].irecv, mem[b].factor
            arrived(copies)
            own_rows = pl.ds(i_row, 64)
            total = inten[own_rows, :] + irecv[0] + irecv[1] + irecv[2]
            factor[own_rows, :] = (
                jnp.sqrt((observed[b, own_rows, :] + 1.0) / (total + 1.0)) - 1.0
            )
            copies = []
            for k in range(1, 4):
                other = lax.rem(z + k, 4)
                copies.append(send(factor.at[own_rows], factor.at[own_rows], t, 2 * other + c))
            power_gather.start_two()
            cover_sum.start_two()
            copies = inverse(b, copies, cover_sum.start_pair)
            grad, grecv, dstep = mem[b].grad, mem[b].grecv, mem[b].dstep
            unroll_step(b, 1)
            step_copy = send(dstep.at[1], mem[b].dsib, t, sibling)
            unroll_step(b, 0)
            power_gather.finish()
            arrived([step_copy])
            mem[b].probe_sum.full[...] = dstep[0] + mem[b].dsib[...]
            probe_sum = Reduce(mem[b].probe_sum)
            probe_sum.start_one()
            illumination(b, not last)
            own, minus, plus = mem[b].gown, mem[b].gminus, mem[b].gplus
            near = []
            for part in range(2):
                arrived(copies[part])
                here = grad[part, pl.ds(own_row, OWN)]
                own[0, part] = here + grecv[1, part] + grecv[3, part] + grecv[5, part]
                own[1, part] = (
                    grecv[0, part] + grecv[2, part] + grecv[4, part] + grecv[6, part]
                )
                near.append([send(own.at[:, part], minus.at[:, part], t_plus, facing(t_plus))])
                if not last:
                    near[part].append(send(own.at[:, part], plus.at[:, part], t_minus, facing(t_minus)))
                if part == 0:
                    probe_sum.start_two()
            probe_sum.start_pair()
            if b == 0:
                arrived([halo_copy])
            own_steps = [(own, j, com.where_own, True) for j in range(2)]
            own_steps += [(minus, j, com.where_minus, False) for j in range(2)]
            halo_steps = [(plus, j, com.where_plus, True) for j in range(2)]
            halo_steps += [(own, j, com.where_own, False) for j in range(2)]
            new = mem[b].objnew
            final_copies, sibling_copies, patch_copies = [], [], []
            for part in range(2):
                arrived(near[part])
                update_block(b, part, field, field_rows, new, 0, own_steps)
                if last:
                    rows = pl.ds(own_row, OWN)
                    spot = out_obj.at[part, rows]
                    final_copies.append(
                        [
                            send(new.at[part], spot, t, 2 * lax.rem(z + k, 4) + c)
                            for k in range(1, 4)
                        ]
                    )
                    sibling_copies.append(send(new.at[part], spot, t, sibling))
                    out_obj[part, rows] = new[part]
                else:
                    halo = mem[b + 1].halo
                    update_block(b, part, mem[b].halo, slice(0, OWN), halo, 1, halo_steps)
                    patch_copies += send_patches(b + 1, new, halo, part)
            coverage = cover_sum.finish()
            step = probe_sum.finish()
            probes = mem[b].probes
            following = out_probe if last else mem[b + 1].probes
            values = []
            for half in range(2):
                values.append(
                    [
                        probes[0, part, held[half], :]
                        + step[half][part] / (coverage[half][0] + 1.0)
                        for part in range(2)
                    ]
                )
                for part in range(2):
                    following[0, part, held[half], :] = values[half][part]
            gather = Gather(lambda rows: following.at[0, pl.ds(0, 2), rows])
            gather.start_one()
            gather.start_two()
            if last:
                for part in range(2):
                    for k in range(1, 4):
                        arrived(final_copies[part][k - 1 : k])
                        other = 2 * mirrored(lax.rem(z - k + 4, 4)) + c
                        rows = pl.ds(pl.multiple_of(OWN * other, OWN), OWN)
                        spot = out_obj.at[part, rows]
                        sibling_copies.append(send(spot, spot, t, sibling))
                gather.finish()
                arrived(sibling_copies)
            else:
                power_copies = send_power(b + 1, values)
                gather.finish()
                probe_copy = send(
                    following.at[0, pl.ds(0, 2)], following.at[1, pl.ds(0, 2)], t, sibling
                )

    refine()
    for copy in sent:
        copy.wait_send()


def shards(object_field, probe, positions, measured):
    right, left = split_tables()
    plan = scratch_plan()
    leaves, tree = jax.tree.flatten(plan)

    def body(*refs):
        kernel(tree, *refs)

    vmem = pl.BlockSpec(memory_space=pltpu.VMEM)
    main = pl.BlockSpec(memory_space=pltpu.HBM)
    return pl.pallas_call(
        body,
        name="refine",
        out_shape=(
            jax.ShapeDtypeStruct(object_field.shape, F32),
            jax.ShapeDtypeStruct(probe.shape, F32),
        ),
        in_specs=[pl.BlockSpec(memory_space=pltpu.SMEM)] + [main] * 5,
        out_specs=(vmem, vmem),
        scratch_shapes=leaves
        + [pltpu.SemaphoreType.DMA((count,)) for count in (COPIES, COPIES, 6)],
        compiler_params=pltpu.CompilerParams(
            collective_id=0, has_side_effects=True, vmem_limit_bytes=30 * 1024 * 1024
        ),
    )(positions, object_field, probe, measured, jnp.asarray(right), jnp.asarray(left))


def solution(mesh):
    in_specs = (
        P(None, "tile", None),
        P("mode", None, None, None),
        P(None, "tile", None),
        P(None, "tile", None, None),
    )
    out_specs = (P(None, "tile", None), P("mode", None, None, None))
    return jax.shard_map(shards, mesh=mesh, in_specs=in_specs, out_specs=out_specs, check_vma=False)
```

```python
import math

import jax
import jax.numpy as jnp
import ml_dtypes
import numpy as np
from jax import lax
from jax.experimental import pallas as pl
from jax.experimental.pallas import tpu as pltpu
from jax.sharding import PartitionSpec as P

N = 256
HALF = 128
WIDTH = 512
OWN = 32
BATCHES = 2
F32 = jnp.float32
BF16 = jnp.bfloat16
MESH = pl.DeviceIdType.MESH


def split_tables():
    index = np.arange(N)
    angle = (np.outer(index, index) % N) * (2.0 * math.pi / N)
    cosine = np.cos(angle) / math.sqrt(N)
    sine = np.sin(angle) / math.sqrt(N)
    bf16 = ml_dtypes.bfloat16

    def parts(table):
        high = table.astype(np.float32).astype(bf16)
        low = (table - high.astype(np.float64)).astype(np.float32).astype(bf16)
        return high, low

    ch, cl = parts(cosine)
    sh, sl = parts(sine)
    high = np.concatenate([ch, sh], axis=1)
    low = np.concatenate([cl, sl], axis=1)
    right = np.concatenate([high, low, high], axis=0)
    left = np.concatenate(
        [np.concatenate([ch, ch, cl], axis=1), np.concatenate([sh, sh, sl], axis=1)], axis=0
    )
    left = left.reshape(2, 4, 64, 3 * N).transpose(1, 0, 2, 3).reshape(4, 128, 3 * N)
    return right, left


def halves(value):
    high = value.astype(BF16)
    low = (value - high.astype(F32)).astype(BF16)
    return high, low


def dot(a, b):
    return jnp.dot(a, b, preferred_element_type=F32)


def iota(shape, dim):
    return lax.broadcasted_iota(jnp.int32, shape, dim)


def reduce_plan(parts):
    return dict(
        full=pltpu.VMEM((parts, N, N), F32),
        one=pltpu.VMEM((2, 3, parts, 32, N), F32),
        onesum=pltpu.VMEM((2, parts, 32, N), F32),
        two=pltpu.VMEM((2, 3, parts, 8, N), F32),
        twosum=pltpu.VMEM((2, parts, 8, N), F32),
        pair=pltpu.VMEM((2, parts, 8, N), F32),
    )


def batch_plan():
    return dict(
        halo=pltpu.VMEM((2, OWN, WIDTH), F32),
        patch=pltpu.VMEM((2, N, N), F32),
        pout=pltpu.VMEM((2, 2, OWN, N), F32),
        probes=pltpu.VMEM((2, 3, N, N), F32),
        power=pltpu.VMEM((8, 2, 8, N), F32),
        inten=pltpu.VMEM((N, N), F32),
        irecv=pltpu.VMEM((3, 64, N), F32),
        factor=pltpu.VMEM((N, N), F32),
        grad=pltpu.VMEM((2, N, N), F32),
        grecv=pltpu.VMEM((7, 2, OWN, N), F32),
        gown=pltpu.VMEM((2, 2, OWN, N), F32),
        gminus=pltpu.VMEM((2, 2, OWN, N), F32),
        gplus=pltpu.VMEM((2, 2, OWN, N), F32),
        objnew=pltpu.VMEM((2, OWN, WIDTH), F32),
        dstep=pltpu.VMEM((2, 2, N, N), F32),
        dsib=pltpu.VMEM((2, N, N), F32),
        cov=pltpu.VMEM((1, N, N), F32),
        csib=pltpu.VMEM((1, N, N), F32),
        probe_sum=reduce_plan(2),
        cover_sum=reduce_plan(1),
    )


def scratch_plan():
    common = dict(
        edge_plus=pltpu.VMEM((2, 16, WIDTH), F32),
        edge_minus=pltpu.VMEM((2, 16, WIDTH), F32),
        edge_out=pltpu.VMEM((2, 2, 16, N), F32),
        edge_rows=pltpu.VMEM((2, HALF, N), F32),
        observed=pltpu.VMEM((2, N, N), F32),
        rtable=pltpu.VMEM((3 * N, 2 * N), BF16),
        ltable=pltpu.VMEM((4, 128, 3 * N), BF16),
        where_own=pltpu.VMEM((8, N), jnp.int32),
        where_minus=pltpu.VMEM((8, N), jnp.int32),
        where_plus=pltpu.VMEM((8, N), jnp.int32),
        strip=pltpu.VMEM((2, N, WIDTH), F32),
        rolled=pltpu.VMEM((2, 2, N, N), F32),
        far=pltpu.VMEM((2, 2, N, N), F32),
        stage=pltpu.VMEM((2, 3 * N, 2 * N), BF16),
        illum=pltpu.VMEM((2, OWN, WIDTH), F32),
    )
    return [common] + [batch_plan() for _ in range(BATCHES)]


class Box:
    def __init__(self, entries):
        for name, entry in entries.items():
            setattr(self, name, Box(entry) if isinstance(entry, dict) else entry)


COPIES = 248


def kernel(tree, pos, object_field, probe, measured, rtable, ltable, out_obj, out_probe, *scratch):
    ssem, rsem, lsem = scratch[-3:]
    com, *mem = [Box(entries) for entries in jax.tree.unflatten(tree, scratch[:-3])]
    t = lax.axis_index("tile")
    m = lax.axis_index("mode")
    x, zh, y = t // 8, (t // 4) % 2, t % 4
    z, c = m // 2, m % 2
    sibling = m + 1 - 2 * c

    def mirrored(chip):
        return chip + zh * (3 - 2 * chip)

    def facing(tile):
        flip = jnp.abs((tile // 4) % 2 - zh)
        return 2 * (z + flip * (3 - 2 * z)) + c

    block = 2 * mirrored(z) + c
    side = 1 - 2 * (block // 4)
    t_plus = lax.rem(t + side + 32, 32)
    t_minus = lax.rem(t - side + 32, 32)
    t_pair = t + 4 - 8 * zh
    own_row = pl.multiple_of(OWN * block, OWN)
    i_row = pl.multiple_of(64 * z, 64)
    sent = []
    obj = com.strip
    first_loads = [
        pltpu.make_async_copy(object_field, obj, lsem.at[4]),
        pltpu.make_async_copy(probe.at[0], mem[0].probes.at[0, pl.ds(0, 2)], lsem.at[5]),
    ]
    for load in first_loads:
        load.start()

    def send(src, dst, tile, mode):
        index = len(sent)
        copy = pltpu.make_async_remote_copy(
            src_ref=src,
            dst_ref=dst,
            send_sem=ssem.at[index],
            recv_sem=rsem.at[index],
            device_id=(tile, mode),
            device_id_type=MESH,
        )
        copy.start()
        sent.append(copy)
        return copy

    def arrived(copies):
        for copy in copies:
            copy.wait_recv()

    def y_tile(k):
        other = lax.rem(y + k, 4)
        return other, t - y + other

    def x_tile(k):
        other = lax.rem(x + k, 4)
        return other, t - 8 * x + 8 * other

    barrier = pltpu.get_barrier_semaphore()
    rw, lw, observed = com.rtable, com.ltable, com.observed
    loads = [
        pltpu.make_async_copy(rtable, rw, lsem.at[0]),
        pltpu.make_async_copy(ltable, lw, lsem.at[1]),
        pltpu.make_async_copy(measured.at[0, c], observed.at[0], lsem.at[2]),
        pltpu.make_async_copy(measured.at[1, c], observed.at[1], lsem.at[3]),
    ]
    partners = [(t, lax.rem(m + k, 8)) for k in range(1, 8)]
    partners += [(y_tile(k)[1], m) for k in range(1, 4)]
    partners += [(x_tile(k)[1], m) for k in range(1, 4)]
    partners += [(t_pair, m), (t_plus, facing(t_plus)), (t_minus, facing(t_minus))]
    for partner in partners:
        pl.semaphore_signal(barrier, inc=1, device_id=partner, device_id_type=MESH)
    for load in loads:
        load.start()

    for b in range(BATCHES):
        for j in range(2):
            core = c if j == 0 else 1 - c
            row = pos[b, core, 0] - N * t
            column = pos[b, core, 1]
            com.where_own[4 * b + 2 * j : 4 * b + 2 * j + 1, :] = jnp.full((1, N), row, jnp.int32)
            com.where_own[4 * b + 2 * j + 1 : 4 * b + 2 * j + 2, :] = jnp.full(
                (1, N), column, jnp.int32
            )
    for load in first_loads:
        load.wait()
    pl.semaphore_wait(barrier, len(partners))

    def place(ref, b, j):
        return ref[4 * b + 2 * j : 4 * b + 2 * j + 1, :], ref[4 * b + 2 * j + 1 : 4 * b + 2 * j + 2, :]

    def whole(part, other):
        return pl.ds(pl.multiple_of(HALF * part + 32 * other, 32), 32)

    def piece(other):
        return pl.ds(pl.multiple_of(8 * other, 8), 8)

    lines = ((y_tile, x_tile), (x_tile, y_tile))
    spots = ((y, x), (x, y))
    held = [
        pl.ds(pl.multiple_of(HALF * part + 32 * spots[part][0] + 8 * spots[part][1], 8), 8)
        for part in range(2)
    ]

    class Reduce:
        def __init__(self, box):
            self.full, self.one, self.onesum = box.full, box.one, box.onesum
            self.two, self.twosum, self.pair = box.two, box.twosum, box.pair

        def start_one(self):
            self.copies = [[], []]
            for k in range(1, 4):
                for part in range(2):
                    other, tile = lines[part][0](k)
                    self.copies[part].append(
                        send(self.full.at[:, whole(part, other)], self.one.at[part, k - 1], tile, m)
                    )

        def start_two(self):
            after = [[], []]
            for part in range(2):
                arrived(self.copies[part])
                self.onesum[part] = (
                    self.full[:, whole(part, spots[part][0])]
                    + self.one[part, 0]
                    + self.one[part, 1]
                    + self.one[part, 2]
                )
                for k in range(1, 4):
                    other, tile = lines[part][1](k)
                    after[part].append(
                        send(
                            self.onesum.at[part, :, piece(other)], self.two.at[part, k - 1], tile, m
                        )
                    )
            self.copies = after

        def start_pair(self):
            for part in range(2):
                arrived(self.copies[part])
                self.twosum[part] = (
                    self.onesum[part, :, piece(spots[part][1])]
                    + self.two[part, 0]
                    + self.two[part, 1]
                    + self.two[part, 2]
                )
            self.copies = [send(self.twosum, self.pair, t_pair, m)]

        def finish(self):
            arrived(self.copies)
            return [self.twosum[part] + self.pair[part] for part in range(2)]

    class Gather:
        def __init__(self, view):
            self.view = view

        def start_one(self):
            self.copies = [[], []]
            for k in range(1, 4):
                for part in range(2):
                    rows = self.view(held[part])
                    self.copies[part].append(send(rows, rows, lines[part][1](k)[1], m))

        def start_two(self):
            after = [[], []]
            for part in range(2):
                arrived(self.copies[part])
                rows = self.view(whole(part, spots[part][0]))
                for k in range(1, 4):
                    after[part].append(send(rows, rows, lines[part][0](k)[1], m))
            self.copies = after

        def finish(self):
            for part in range(2):
                arrived(self.copies[part])

    def send_power(b, values):
        power = mem[b].power
        for part, (real, imag) in enumerate(values):
            power[0, part] = real * real + imag * imag
        return [send(power.at[0], power.at[k], t, lax.rem(m + k, 8)) for k in range(1, 8)]

    def sum_power(b, copies):
        arrived(copies)
        power = mem[b].power
        total = power[0]
        for k in range(1, 8):
            total = total + power[k]
        for part in range(2):
            mem[b].probes[0, 2, held[part], :] = total[part]

    def send_edges():
        plus, minus, out, rows = com.edge_plus, com.edge_minus, com.edge_out, com.edge_rows
        columns = iota((16, N), 1)
        spot = pl.ds(pl.multiple_of(16 * block, 16), 16)
        for j in range(2):
            row, column = place(com.where_own, 0, j)
            ahead = jnp.broadcast_to(row, (16, N)) >= 0
            first = columns >= column
            for part in range(2):
                low = jnp.where(ahead, plus[part, :, :N], minus[part, :, :N])
                high = jnp.where(ahead, plus[part, :, N:], minus[part, :, N:])
                out[j, part] = jnp.where(first, low, high)
        copies = [
            send(out.at[k % 2], rows.at[:, spot], t, lax.rem(m + k, 8)) for k in range(1, 8)
        ]
        rows[:, spot] = out[0]
        return copies

    def join_edges():
        rows, patch = com.edge_rows, mem[0].patch
        row, column = place(com.where_own, 0, 0)
        columns = iota((HALF, N), 1)
        first = columns >= column
        for half in range(2):
            span = slice(HALF * half, HALF * (half + 1))
            ahead = HALF * half + iota((HALF, N), 0) - row
            inside = (ahead >= 0) & (ahead < N)
            for part in range(2):
                own = jnp.where(first, obj[part, span, :N], obj[part, span, N:])
                patch[part, span, :] = jnp.where(inside, own, rows[part])

    def send_patches(b, field, halo, part):
        out, patch = mem[b].pout, mem[b].patch
        rows = own_row + iota((OWN, N), 0)
        columns = iota((OWN, N), 1)
        for j in range(2):
            row, column = place(com.where_own, b, j)
            ahead = rows - row
            inside = (ahead >= 0) & (ahead < N)
            first = columns >= column
            low = jnp.where(inside, field[part, :, :N], halo[part, :, :N])
            high = jnp.where(inside, field[part, :, N:], halo[part, :, N:])
            out[j, part] = jnp.where(first, low, high)
        copies = []
        spot = patch.at[part, pl.ds(own_row, OWN)]
        for k in range(1, 8):
            copies.append(send(out.at[k % 2, part], spot, t, lax.rem(m + k, 8)))
        patch[part, pl.ds(own_row, OWN)] = out[0, part]
        return copies

    def shifted(real, imag, row, column):
        i0, i1 = iota((N, N), 0), iota((N, N), 1)
        pick = (((i0 + row) & (N - 1)) == i1).astype(F32).astype(BF16)
        both = real if imag is None else jnp.concatenate([real, imag], axis=1)
        high, low = halves(both)
        moved = dot(jnp.concatenate([pick, pick], axis=1), jnp.concatenate([high, low], axis=0))
        pick = (((i1 + column) & (N - 1)) == i0).astype(F32).astype(BF16)
        if imag is not None:
            moved = jnp.concatenate([moved[:, :N], moved[:, N:]], axis=0)
        high, low = halves(moved)
        moved = dot(jnp.concatenate([high, low], axis=1), jnp.concatenate([pick, pick], axis=0))
        return moved[:N], moved[N:]

    def roll_probe(b, mode):
        row, column = place(com.where_own, b, 0)
        probes = mem[b].probes
        rolled[mode, 0], rolled[mode, 1] = shifted(
            probes[mode, 0], probes[mode, 1], -row, -column
        )

    def unroll_step(b, mode):
        row, column = place(com.where_own, b, 0)
        dstep = mem[b].dstep
        dstep[mode, 0], dstep[mode, 1] = shifted(dstep[mode, 0], dstep[mode, 1], row, column)

    def unrolled_one(field, b):
        row, column = place(com.where_own, b, 0)
        return shifted(field, None, row, column)[0]

    def chunk_rows(q):
        return pl.ds(pl.multiple_of(q * 64, 64), 64)

    stage = com.stage

    def right_stage(mode, q, real, imag, sign):
        high, low = halves(jnp.concatenate([real, imag], axis=0))
        product = dot(jnp.concatenate([high, high, low], axis=1), rw[...])
        out_real = product[:64, :N] + sign * product[64:, N:]
        out_imag = product[64:, :N] - sign * product[:64, N:]
        high, low = halves(jnp.concatenate([out_real, out_imag], axis=1))
        stage[mode, pl.ds(pl.multiple_of(q * 64, 64), 64), :] = high
        stage[mode, pl.ds(pl.multiple_of(N + q * 64, 64), 64), :] = low
        stage[mode, pl.ds(pl.multiple_of(2 * N + q * 64, 64), 64), :] = high

    def left_stage(mode, q, sign):
        product = dot(lw[q], stage[mode])
        return (
            product[:64, :N] + sign * product[64:, N:],
            product[:64, N:] - sign * product[64:, :N],
        )

    far, rolled = com.far, com.rolled

    def forward(b):
        ofield, inten = mem[b].patch, mem[b].inten

        def first(q, carry):
            rows = chunk_rows(q)
            o_real, o_imag = ofield[0, rows, :], ofield[1, rows, :]
            for mode in range(2):
                p_real, p_imag = rolled[mode, 0, rows, :], rolled[mode, 1, rows, :]
                right_stage(
                    mode,
                    q,
                    p_real * o_real - p_imag * o_imag,
                    p_real * o_imag + p_imag * o_real,
                    1.0,
                )
            return carry

        lax.fori_loop(0, 4, first, 0)

        irecv, copies = mem[b].irecv, []
        for k in (1, 2, 3, 0):
            q = lax.rem(z + k, 4)
            rows = chunk_rows(q)
            total = None
            for mode in range(2):
                f_real, f_imag = left_stage(mode, q, 1.0)
                far[mode, 0, rows, :] = f_real
                far[mode, 1, rows, :] = f_imag
                power = f_real * f_real + f_imag * f_imag
                total = power if total is None else total + power
            inten[rows, :] = total
            if k:
                copies.append(send(inten.at[rows], irecv.at[k - 1], t, 2 * q + c))
        return copies

    def inverse(b, copies, between):
        ofield, factor = mem[b].patch, mem[b].factor
        grad, dstep, grecv = mem[b].grad, mem[b].dstep, mem[b].grecv

        for k in range(4):
            if k:
                arrived(copies[k - 1 : k])
            q = lax.rem(z - k + 4, 4)
            rows = chunk_rows(q)
            scale = factor[rows, :]
            for mode in range(2):
                right_stage(mode, q, scale * far[mode, 0, rows, :], scale * far[mode, 1, rows, :], -1.0)
        between()

        sends, later = [], []
        for k in (2, 1, 3, 0):
            q = lax.rem(z + k, 4)
            chunk = mirrored(q)
            rows = chunk_rows(chunk)
            o_real, o_imag = ofield[0, rows, :], ofield[1, rows, :]
            g_real = jnp.zeros((64, N), F32)
            g_imag = jnp.zeros((64, N), F32)
            for mode in range(2):
                c_real, c_imag = left_stage(mode, chunk, -1.0)
                p_real, p_imag = rolled[mode, 0, rows, :], rolled[mode, 1, rows, :]
                g_real = g_real + p_real * c_real + p_imag * c_imag
                g_imag = g_imag + p_real * c_imag - p_imag * c_real
                dstep[mode, 0, rows, :] = o_real * c_real + o_imag * c_imag
                dstep[mode, 1, rows, :] = o_real * c_imag - o_imag * c_real
            grad[0, rows, :] = g_real
            grad[1, rows, :] = g_imag
            for twin in range(2):
                if k == 0 and twin == 0:
                    continue
                core = c if twin == 0 else 1 - c
                part = pl.ds(pl.multiple_of(OWN * (2 * chunk + core), OWN), OWN)
                slot = 2 * k + twin - 1
                sends.append(send(grad.at[0, part], grecv.at[slot, 0], t, 2 * q + core))
                later.append((grad.at[1, part], grecv.at[slot, 1], t, 2 * q + core))
        return [sends, [send(*args) for args in later]]

    def masks(ref, b, j):
        rows = own_row + iota((OWN, N), 0)
        row, column = place(ref, b, j)
        ahead = rows - row
        inside = (ahead >= 0) & (ahead < N)
        first = iota((OWN, N), 1) >= column
        return inside, first

    def sides(ref, b, j, here):
        inside, first = masks(ref, b, j)
        if not here:
            inside = jnp.logical_not(inside)
        return inside & first, inside & jnp.logical_not(first)

    def illumination(b, with_halo):
        high, low = halves(mem[b].probes[0, 2])
        power = jnp.concatenate([high, low], axis=0)
        rows = own_row + iota((OWN, N), 0)
        lanes = iota((OWN, N), 1)
        refs = [com.where_own, com.where_minus] + ([com.where_plus] if with_halo else [])
        spots_of = [(ref, j) for ref in refs for j in range(2)]
        picks = []
        for ref, j in spots_of:
            row, _ = place(ref, b, j)
            pick = (((rows - row) & (N - 1)) == lanes).astype(F32).astype(BF16)
            picks.append(jnp.concatenate([pick, pick], axis=1))
        taken = dot(jnp.concatenate(picks, axis=0), power)
        i0, i1 = iota((N, N), 0), iota((N, N), 1)
        blocks = [[jnp.zeros((OWN, N), F32) for _ in range(2)] for _ in range(2)]
        for index, (ref, j) in enumerate(spots_of):
            _, column = place(ref, b, j)
            pick = (((i1 - column) & (N - 1)) == i0).astype(F32).astype(BF16)
            high, low = halves(taken[OWN * index : OWN * (index + 1)])
            moved = dot(
                jnp.concatenate([high, low], axis=1), jnp.concatenate([pick, pick], axis=0)
            )
            kind = index // 2
            for block, here in ((0, kind == 0), (1, kind == 2)):
                if (block, kind) in ((0, 2), (1, 1)):
                    continue
                for side_index, mask in enumerate(sides(ref, b, j, here)):
                    blocks[block][side_index] = blocks[block][side_index] + jnp.where(
                        mask, moved, 0.0
                    )
        for block in range(2 if with_halo else 1):
            com.illum[block, :, :N] = blocks[block][0]
            com.illum[block, :, N:] = blocks[block][1]

    def update_block(b, part, field, field_rows, new, block, steps):
        for side_index, columns in ((0, slice(0, N)), (1, slice(N, WIDTH))):
            total = jnp.zeros((OWN, N), F32)
            for step, j, ref, here in steps:
                total = total + jnp.where(sides(ref, b, j, here)[side_index], step[j, part], 0.0)
            new[part, :, columns] = field[part, field_rows, columns] + total / (
                com.illum[block, :, columns] + 1.0
            )

    def refine():
        spot = pl.ds(pl.multiple_of(16 * block, 16), 16)
        far_spot = pl.ds(pl.multiple_of(HALF + 16 * block, 16), 16)
        below, above = lax.rem(t + 31, 32), lax.rem(t + 1, 32)
        edge_copies = [
            send(obj.at[:, spot], com.edge_plus, below, facing(below)),
            send(obj.at[:, far_spot], com.edge_minus, above, facing(above)),
        ]
        probe_copy = send(
            mem[0].probes.at[0, pl.ds(0, 2)], mem[0].probes.at[1, pl.ds(0, 2)], t, sibling
        )
        where_copies = [
            send(com.where_own, com.where_minus, t_plus, facing(t_plus)),
            send(com.where_own, com.where_plus, t_minus, facing(t_minus)),
        ]
        arrived(edge_copies)
        patch_copies = send_edges()
        roll_probe(0, 0)
        mine = mem[0].probes.at[0]
        power_values = [(mine[0, held[part]], mine[1, held[part]]) for part in range(2)]
        arrived(where_copies)
        for load in loads:
            load.wait()
        for b in range(BATCHES):
            last = b == BATCHES - 1
            if b == 0:
                field, field_rows = obj, pl.ds(own_row, OWN)
            else:
                field, field_rows = mem[b - 1].objnew, slice(0, OWN)
            if b:
                roll_probe(b, 0)
            arrived([probe_copy])
            roll_probe(b, 1)
            arrived(patch_copies)
            power_copies = send_power(b, power_values)
            if b == 0:
                rows = pl.ds(own_row, OWN)
                halo_copy = send(obj.at[:, rows], mem[0].halo, t_minus, facing(t_minus))
            if b == 0:
                join_edges()
            copies = forward(b)
            sum_power(b, power_copies)
            power_gather = Gather(lambda rows: mem[b].probes.at[0, 2, rows])
            power_gather.start_one()
            patch, cover = mem[b].patch, mem[b].cov
            cover[0] = unrolled_one(patch[0] * patch[0] + patch[1] * patch[1], b)
            cover_copy = send(cover, mem[b].csib, t, sibling)
            arrived([cover_copy])
            mem[b].cover_sum.full[...] = cover[...] + mem[b].csib[...]
            cover_sum = Reduce(mem[b].cover_sum)
            cover_sum.start_one()
            inten, irecv, factor = mem[b].inten, mem[b].irecv, mem[b].factor
            arrived(copies)
            own_rows = pl.ds(i_row, 64)
            total = inten[own_rows, :] + irecv[0] + irecv[1] + irecv[2]
            factor[own_rows, :] = (
                jnp.sqrt((observed[b, own_rows, :] + 1.0) / (total + 1.0)) - 1.0
            )
            copies = []
            for k in range(1, 4):
                other = lax.rem(z + k, 4)
                copies.append(send(factor.at[own_rows], factor.at[own_rows], t, 2 * other + c))
            power_gather.start_two()
            cover_sum.start_two()
            copies = inverse(b, copies, cover_sum.start_pair)
            grad, grecv, dstep = mem[b].grad, mem[b].grecv, mem[b].dstep
            unroll_step(b, 1)
            step_copy = send(dstep.at[1], mem[b].dsib, t, sibling)
            unroll_step(b, 0)
            power_gather.finish()
            arrived([step_copy])
            mem[b].probe_sum.full[...] = dstep[0] + mem[b].dsib[...]
            probe_sum = Reduce(mem[b].probe_sum)
            probe_sum.start_one()
            illumination(b, not last)
            own, minus, plus = mem[b].gown, mem[b].gminus, mem[b].gplus
            near = []
            for part in range(2):
                arrived(copies[part])
                here = grad[part, pl.ds(own_row, OWN)]
                own[0, part] = here + grecv[1, part] + grecv[3, part] + grecv[5, part]
                own[1, part] = (
                    grecv[0, part] + grecv[2, part] + grecv[4, part] + grecv[6, part]
                )
                near.append([send(own.at[:, part], minus.at[:, part], t_plus, facing(t_plus))])
                if not last:
                    near[part].append(send(own.at[:, part], plus.at[:, part], t_minus, facing(t_minus)))
                if part == 0:
                    probe_sum.start_two()
            probe_sum.start_pair()
            if b == 0:
                arrived([halo_copy])
            own_steps = [(own, j, com.where_own, True) for j in range(2)]
            own_steps += [(minus, j, com.where_minus, False) for j in range(2)]
            halo_steps = [(plus, j, com.where_plus, True) for j in range(2)]
            halo_steps += [(own, j, com.where_own, False) for j in range(2)]
            new = mem[b].objnew
            final_copies, sibling_copies, patch_copies = [], [], []
            for part in range(2):
                arrived(near[part])
                update_block(b, part, field, field_rows, new, 0, own_steps)
                if last:
                    rows = pl.ds(own_row, OWN)
                    spot = out_obj.at[part, rows]
                    final_copies.append(
                        [
                            send(new.at[part], spot, t, 2 * lax.rem(z + k, 4) + c)
                            for k in range(1, 4)
                        ]
                    )
                    sibling_copies.append(send(new.at[part], spot, t, sibling))
                    out_obj[part, rows] = new[part]
                else:
                    halo = mem[b + 1].halo
                    update_block(b, part, mem[b].halo, slice(0, OWN), halo, 1, halo_steps)
                    patch_copies += send_patches(b + 1, new, halo, part)
            coverage = cover_sum.finish()
            step = probe_sum.finish()
            probes = mem[b].probes
            following = out_probe if last else mem[b + 1].probes
            values = []
            for half in range(2):
                values.append(
                    [
                        probes[0, part, held[half], :]
                        + step[half][part] / (coverage[half][0] + 1.0)
                        for part in range(2)
                    ]
                )
                for part in range(2):
                    following[0, part, held[half], :] = values[half][part]
            gather = Gather(lambda rows: following.at[0, pl.ds(0, 2), rows])
            gather.start_one()
            gather.start_two()
            if last:
                for part in range(2):
                    for k in range(1, 4):
                        arrived(final_copies[part][k - 1 : k])
                        other = 2 * mirrored(lax.rem(z - k + 4, 4)) + c
                        rows = pl.ds(pl.multiple_of(OWN * other, OWN), OWN)
                        spot = out_obj.at[part, rows]
                        sibling_copies.append(send(spot, spot, t, sibling))
                gather.finish()
                arrived(sibling_copies)
            else:
                power_values = values
                gather.finish()
                probe_copy = send(
                    following.at[0, pl.ds(0, 2)], following.at[1, pl.ds(0, 2)], t, sibling
                )

    refine()
    for copy in sent:
        copy.wait_send()


def shards(object_field, probe, positions, measured):
    right, left = split_tables()
    plan = scratch_plan()
    leaves, tree = jax.tree.flatten(plan)

    def body(*refs):
        kernel(tree, *refs)

    vmem = pl.BlockSpec(memory_space=pltpu.VMEM)
    main = pl.BlockSpec(memory_space=pltpu.HBM)
    return pl.pallas_call(
        body,
        name="refine",
        out_shape=(
            jax.ShapeDtypeStruct(object_field.shape, F32),
            jax.ShapeDtypeStruct(probe.shape, F32),
        ),
        in_specs=[pl.BlockSpec(memory_space=pltpu.SMEM)] + [main] * 5,
        out_specs=(vmem, vmem),
        scratch_shapes=leaves
        + [pltpu.SemaphoreType.DMA((count,)) for count in (COPIES, COPIES, 6)],
        compiler_params=pltpu.CompilerParams(
            collective_id=0, has_side_effects=True, vmem_limit_bytes=30 * 1024 * 1024
        ),
    )(positions, object_field, probe, measured, jnp.asarray(right), jnp.asarray(left))


def solution(mesh):
    in_specs = (
        P(None, "tile", None),
        P("mode", None, None, None),
        P(None, "tile", None),
        P(None, "tile", None, None),
    )
    out_specs = (P(None, "tile", None), P("mode", None, None, None))
    return jax.shard_map(shards, mesh=mesh, in_specs=in_specs, out_specs=out_specs, check_vma=False)
```
